32 devices in a mesh: fsdp: 32 (over z, y, x, core).
Axes of the slice: x: 2, y: 2, z: 4, core: 2. Of those that a mesh axis runs over, the one named last changes fastest.
Arguments:
- inputs: bfloat16 [32768, 768], P('fsdp'), may hold values from -6 to 6
- cotangent: bfloat16 [32768, 768], P('fsdp'), may hold values from -6 to 6
- lengths: int32 [32], P('fsdp'), may hold values from 250 to 800, as said below
- skip_bit: int32 [32], P('fsdp'), may hold values from 0 to 1, as said below
- w_query: bfloat16 [768, 768], P('fsdp'), may hold values from -0.21875 to 0.21875
- w_key: bfloat16 [768, 768], P('fsdp'), may hold values from -0.21875 to 0.21875
- w_value: bfloat16 [768, 768], P('fsdp'), may hold values from -0.21875 to 0.21875
- w_out: bfloat16 [768, 768], P('fsdp'), may hold values from -3.5 to 3.5
- b_query: bfloat16 [768], P('fsdp'), may hold values from -3 to 3
- b_value: bfloat16 [768], P('fsdp'), may hold values from -0.29882812 to 0.29882812
- b_out: bfloat16 [768], P('fsdp'), may hold values from -2 to 2
- ln1_gain: bfloat16 [768], P('fsdp'), may hold values from 0.5 to 1.5
- ln1_bias: bfloat16 [768], P('fsdp'), may hold values from -2 to 2
- w_hidden: bfloat16 [768, 3072], P('fsdp'), may hold values from -0.21875 to 0.21875
- b_hidden: bfloat16 [3072], P('fsdp'), may hold values from -2 to 2
- w_proj: bfloat16 [3072, 768], P('fsdp'), may hold values from -0.15625 to 0.15625
- b_proj: bfloat16 [768], P('fsdp'), may hold values from -2 to 2
- ln2_gain: bfloat16 [768], P('fsdp'), may hold values from 0.5 to 1.5
- ln2_bias: bfloat16 [768], P('fsdp'), may hold values from -2 to 2
Outputs:
- outputs: bfloat16 [32768, 768], P('fsdp')
- grad_inputs: float32 [32768, 768], P('fsdp')
- grad_w_query: float32 [768, 768], P('fsdp')
- grad_w_key: float32 [768, 768], P('fsdp')
- grad_w_value: float32 [768, 768], P('fsdp')
- grad_w_out: float32 [768, 768], P('fsdp')
- grad_b_query: float32 [768], P('fsdp')
- grad_b_value: float32 [768], P('fsdp')
- grad_b_out: float32 [768], P('fsdp')
- grad_ln1_gain: float32 [768], P('fsdp')
- grad_ln1_bias: float32 [768], P('fsdp')
- grad_w_hidden: float32 [768, 3072], P('fsdp')
- grad_b_hidden: float32 [3072], P('fsdp')
- grad_w_proj: float32 [3072, 768], P('fsdp')
- grad_b_proj: float32 [768], P('fsdp')
- grad_ln2_gain: float32 [768], P('fsdp')
- grad_ln2_bias: float32 [768], P('fsdp')
The draws below stay inside these ranges and needn't reach their ends.
Inputs may be any that keep to these rules, and one draw needn't show every extreme that they name: Utterance lengths in frames; one utterance has exactly 800 frames and one exactly 250. `skip_bit`: 1 drops the layer for that utterance slot, 0 keeps it; at least one slot is dropped and at least one is kept.
All inputs are finite; a program needn't handle non-finite values.
Results may differ from the reference program's by a relative error of at most 0.015.
Values may be sent and summed in bfloat16 or wider, within the bound.
A program may use at most 256 MiB of HBM per device.

```python
import jax
import jax.numpy as jnp
from jax import lax

D = 768
HEADS = 12
FF = 3072
SLOT = 1024
MAXLEN = 800
MINLEN = 250
UTTS = 32
TOKENS = 32768


def draw_lengths(key, part):
    len_key, pos_key = jax.random.split(key)
    drawn = jax.random.randint(len_key, (UTTS,), MINLEN, MAXLEN + 1)
    picked = jax.random.permutation(pos_key, UTTS)
    drawn = drawn.at[picked[0]].set(MAXLEN)
    drawn = drawn.at[picked[1]].set(MINLEN)
    return drawn.astype(jnp.int32)


def draw_skip_bit(key, part):
    roll_key, pos_key = jax.random.split(jax.random.fold_in(key, 7))
    rolls = jax.random.randint(roll_key, (UTTS,), 0, 20)
    bits = jnp.where(rolls == 0, 1, 0).astype(jnp.int32)
    picked = jax.random.permutation(pos_key, UTTS)
    bits = bits.at[picked[0]].set(1)
    bits = bits.at[picked[1]].set(0)
    return bits.astype(jnp.int32)


def levels(own_key, extent, pieces, smallest, high):
    level, own = 1.0, jax.random.fold_in(own_key, 6)
    for position, blocks in pieces:
        heights = jnp.exp(jax.random.uniform(jax.random.fold_in(own, position), (blocks,), jnp.float32, smallest / len(pieces), high / len(pieces)))
        level = level * jnp.repeat(heights, extent[position] // blocks).reshape([-1 if axis == position else 1 for axis in range(len(extent))])
    return level


def bell_draw(rng, shape, scale, bound, cuts=(), kind=jnp.bfloat16):
    values = scale * jax.random.normal(rng, shape, jnp.float32)
    if cuts:
        values = values * levels(rng, shape, cuts, -0.22, 0.18)
    return jnp.clip(values, -bound, bound).astype(kind)


def setup_inputs(seed: int = 0) -> dict:
    streams_of = jax.random.split(jax.random.key(seed), 20)
    inputs = bell_draw(streams_of[0], (TOKENS, D), 1.0, 6.0, ((0, 32),))
    cotangent = bell_draw(streams_of[1], (TOKENS, D), 1.0, 6.0, ((0, 32),))
    lengths = draw_lengths(jax.random.fold_in(streams_of[19], 71), 0)
    skip_bit = draw_skip_bit(jax.random.fold_in(streams_of[19], 71), 0)
    w_query = bell_draw(streams_of[4], (D, D), D ** -0.5, 0.21875, ((0, 32),))
    w_key = bell_draw(streams_of[5], (D, D), D ** -0.5, 0.21875, ((0, 32),))
    w_value = bell_draw(streams_of[6], (D, D), D ** -0.5, 0.21875, ((0, 32),))
    w_out = bell_draw(streams_of[7], (D, D), (D // 256) ** -0.5, 3.5, ((0, 32),))
    b_query = bell_draw(streams_of[8], (D,), 0.5, 3.0, ((0, 32),))
    b_value = bell_draw(streams_of[9], (D,), 0.05, 0.29882812, ((0, 32),))
    b_out = bell_draw(streams_of[10], (D,), 0.3, 2.0, ((0, 32),))
    ln1_gain = jnp.clip(1.0 + 0.1 * jax.random.normal(streams_of[11], (D,), jnp.float32), 0.5, 1.5).astype(jnp.bfloat16)
    ln1_bias = bell_draw(streams_of[12], (D,), 0.3, 2.0, ((0, 32),))
    w_hidden = bell_draw(streams_of[13], (D, FF), D ** -0.5, 0.21875, ((0, 32),))
    b_hidden = bell_draw(streams_of[14], (FF,), 0.3, 2.0, ((0, 32),))
    w_proj = bell_draw(streams_of[15], (FF, D), (FF // 2) ** -0.5, 0.15625, ((0, 32),))
    b_proj = bell_draw(streams_of[16], (D,), 0.3, 2.0, ((0, 32),))
    ln2_gain = jnp.clip(1.0 + 0.1 * jax.random.normal(streams_of[17], (D,), jnp.float32), 0.5, 1.5).astype(jnp.bfloat16)
    ln2_bias = bell_draw(streams_of[18], (D,), 0.3, 2.0, ((0, 32),))
    return {"inputs": inputs, "cotangent": cotangent, "lengths": lengths, "skip_bit": skip_bit, "w_query": w_query, "w_key": w_key, "w_value": w_value, "w_out": w_out, "b_query": b_query, "b_value": b_value, "b_out": b_out, "ln1_gain": ln1_gain, "ln1_bias": ln1_bias, "w_hidden": w_hidden, "b_hidden": b_hidden, "w_proj": w_proj, "b_proj": b_proj, "ln2_gain": ln2_gain, "ln2_bias": ln2_bias}


@jax.custom_vjp
def low(v):
    return lax.optimization_barrier(v.astype(jnp.bfloat16)).astype(jnp.float32)

@jax.custom_vjp
def low_back(v):
    return v

def low_keep(v):
    return (low(v), None)

def low_pass(kept, grad):
    return (grad,)

def back_keep(v):
    return (v, None)

def back_low(kept, grad):
    return (low(grad),)
low.defvjp(low_keep, low_pass)
low_back.defvjp(back_keep, back_low)
EPSILON = 1e-05

def layer_norm(hidden, gain, shift):
    row_mean = lax.optimization_barrier(jnp.mean(hidden, -1, keepdims=True))
    centred = hidden - row_mean
    inv_std = lax.rsqrt(lax.optimization_barrier(jnp.mean(jnp.square(centred), -1, keepdims=True)) + EPSILON)
    return centred * inv_std * gain + shift

def slot_layer(params, frames, live_mask):
    w_query, w_key, w_value, w_out, b_query, b_value, b_out, ln1_gain, ln1_bias, w_hidden, b_hidden, w_proj, b_proj, ln2_gain, ln2_bias = params
    highest = lax.Precision.HIGHEST
    slot_rows = frames.shape[0]
    head_dim = D // HEADS
    factor = 1.0 / jnp.sqrt(jnp.float32(head_dim))
    queries = low(low_back(jnp.dot(frames, w_query, precision=highest, preferred_element_type=jnp.float32) + b_query))
    keys_all = low(low_back(jnp.dot(frames, w_key, precision=highest, preferred_element_type=jnp.float32)))
    values_all = low(low_back(jnp.dot(frames, w_value, precision=highest, preferred_element_type=jnp.float32) + b_value))
    queries = queries.reshape(slot_rows, HEADS, head_dim)
    keys_all = keys_all.reshape(slot_rows, HEADS, head_dim)
    values_all = values_all.reshape(slot_rows, HEADS, head_dim)
    scores = jnp.einsum('qhd,khd->hqk', queries, keys_all, precision=highest) * factor
    scores = jnp.where(live_mask[None, None, :], scores, jnp.float32(-1e+30))
    scores = low_back(scores)
    probs = low(jax.nn.softmax(scores, axis=-1))
    attended = jnp.einsum('hqk,khd->qhd', probs, values_all, precision=highest).reshape(slot_rows, D)
    attended = low(low_back(attended))
    branch = low_back(jnp.dot(attended, w_out, precision=highest, preferred_element_type=jnp.float32) + b_out)
    first_norm = low(layer_norm(frames + branch, ln1_gain, ln1_bias))
    pre_act = low_back(jnp.dot(first_norm, w_hidden, precision=highest, preferred_element_type=jnp.float32) + b_hidden)
    gelu_out = low(jax.nn.gelu(pre_act, approximate=False))
    ffn_out = low_back(jnp.dot(gelu_out, w_proj, precision=highest, preferred_element_type=jnp.float32) + b_proj)
    return layer_norm(first_norm + ffn_out, ln2_gain, ln2_bias)

def reference(inputs, cotangent, lengths, skip_bit, w_query, w_key, w_value, w_out, b_query, b_value, b_out, ln1_gain, ln1_bias, w_hidden, b_hidden, w_proj, b_proj, ln2_gain, ln2_bias):
    params = tuple((item.astype(jnp.float32) for item in (w_query, w_key, w_value, w_out, b_query, b_value, b_out, ln1_gain, ln1_bias, w_hidden, b_hidden, w_proj, b_proj, ln2_gain, ln2_bias)))
    frames_all = inputs.astype(jnp.float32)
    live_rows = jnp.arange(SLOT, dtype=jnp.int32)[None, :] < lengths[:, None]
    skip_rows = jnp.repeat(skip_bit, SLOT, total_repeat_length=UTTS * SLOT)

    def forward(weights, frames_in):
        shaped = frames_in.reshape(UTTS, SLOT, D)

        def one_slot(items):
            return slot_layer(weights, items[0], items[1])
        layer_rows = lax.map(jax.checkpoint(one_slot), (shaped, live_rows)).reshape(UTTS * SLOT, D)
        return jnp.where(skip_rows[:, None] == 1, frames_in, layer_rows)
    result, pull = jax.vjp(forward, params, frames_all)
    row_mask = live_rows.reshape(UTTS * SLOT).astype(jnp.float32)[:, None]
    grads, grad_inputs = pull(cotangent.astype(jnp.float32) * row_mask)
    return (result.astype(jnp.bfloat16), grad_inputs, grads[0], grads[1], grads[2], grads[3], grads[4], grads[5], grads[6], grads[7], grads[8], grads[9], grads[10], grads[11], grads[12], grads[13], grads[14])
```

```python
import functools
import math

import jax
import jax.numpy as jnp
from jax import lax
from jax.experimental import pallas as pl
from jax.experimental.pallas import tpu as pltpu
from jax.sharding import PartitionSpec as P

HEADS = 12


EPSILON = 1e-05
NEG_FILL = -1e30


def as_float(value):
    return value.astype(jnp.float32)


def layer_norm(hidden, gain, shift):
    row_mean = jnp.mean(hidden, -1, keepdims=True)
    centred = hidden - row_mean
    inv_std = lax.rsqrt(jnp.mean(centred * centred, -1, keepdims=True) + EPSILON)
    normed = centred * inv_std
    return (normed * gain + shift, normed, inv_std)


def norm_back(grad, normed, inv_std, gain):
    scaled = grad * gain
    return inv_std * (
        scaled
        - jnp.mean(scaled, -1, keepdims=True)
        - normed * jnp.mean(scaled * normed, -1, keepdims=True)
    )


def gelu_slope(pre_act):
    return (
        0.5 * (1.0 + lax.erf(pre_act * 0.7071067811865476))
        + pre_act * jnp.exp(-0.5 * pre_act * pre_act) * 0.3989422804014327
    )


def scores_of(q_block, keys_all, live_mask):
    factor = 1.0 / math.sqrt(q_block.shape[2])
    raw = jnp.einsum("qhd,khd->hqk", q_block, keys_all, preferred_element_type=jnp.float32) * factor
    return jnp.where(live_mask[None, None, :], raw, NEG_FILL)


def attend_forward(queries, keys_all, values_all, live_mask):
    row_count, head_count, head_dim = queries.shape
    block_rows = min(512, row_count)
    q_blocks = queries.reshape(row_count // block_rows, block_rows, head_count, head_dim)

    def one_block(q_block):
        scores = scores_of(q_block, keys_all, live_mask)
        row_peak = jnp.max(scores, -1, keepdims=True)
        exp_scores = jnp.exp(scores - row_peak)
        exp_total = jnp.sum(exp_scores, -1, keepdims=True)
        probs = (exp_scores / exp_total).astype(jnp.bfloat16)
        mixed_out = jnp.einsum(
            "hqk,khd->qhd", probs, values_all, preferred_element_type=jnp.float32
        )
        return (mixed_out.astype(jnp.bfloat16), (row_peak + jnp.log(exp_total))[..., 0])

    mixed_out, log_sum = lax.map(one_block, q_blocks)
    return (mixed_out.reshape(row_count, head_count * head_dim), log_sum)


def attend_backward(queries, keys_all, values_all, live_mask, grad_out, log_sum):
    row_count, head_count, head_dim = queries.shape
    block_rows = min(512, row_count)
    block_count = row_count // block_rows
    factor = 1.0 / math.sqrt(head_dim)
    q_blocks = queries.reshape(block_count, block_rows, head_count, head_dim)
    g_blocks = grad_out.reshape(block_count, block_rows, head_count, head_dim)

    def one_block(carry, items):
        q_block, g_block, lse_block = items
        scores = scores_of(q_block, keys_all, live_mask)
        probs = jnp.exp(scores - lse_block[..., None])
        d_probs = jnp.einsum(
            "qhd,khd->hqk", g_block, values_all, preferred_element_type=jnp.float32
        )
        d_scores = (probs * (d_probs - jnp.sum(probs * d_probs, -1, keepdims=True))).astype(
            jnp.bfloat16
        )
        d_query = (
            jnp.einsum("hqk,khd->qhd", d_scores, keys_all, preferred_element_type=jnp.float32)
            * factor
        )
        d_key = (
            carry[0]
            + jnp.einsum("hqk,qhd->khd", d_scores, q_block, preferred_element_type=jnp.float32)
            * factor
        )
        d_value = carry[1] + jnp.einsum(
            "hqk,qhd->khd", probs.astype(jnp.bfloat16), g_block, preferred_element_type=jnp.float32
        )
        return ((d_key, d_value), d_query)

    zero_grad = jnp.zeros(keys_all.shape, jnp.float32)
    (d_key, d_value), d_query = lax.scan(
        one_block, (zero_grad, zero_grad), (q_blocks, g_blocks, log_sum)
    )
    width_all = head_count * head_dim
    return (
        d_query.reshape(row_count, width_all),
        d_key.reshape(row_count, width_all),
        d_value.reshape(row_count, width_all),
    )


MESH = pl.DeviceIdType.MESH


def place(me, planes):
    core = lax.rem(me, 2)
    chip = me // 2
    col = lax.rem(chip, 2)
    row = lax.rem(chip // 2, 2)
    plane = chip // 4
    near = jnp.where(core == 0, row, col)
    far = jnp.where(core == 0, col, row)

    def index(plane_, near_, far_, core_):
        row_ = jnp.where(core_ == 0, near_, far_)
        col_ = jnp.where(core_ == 0, far_, near_)
        return ((plane_ * 2 + row_) * 2 + col_) * 2 + core_

    return core, near, far, plane, index


def greet(peers):
    barrier = pltpu.get_barrier_semaphore()
    for peer in peers:
        pl.semaphore_signal(barrier, inc=1, device_id=(peer,), device_id_type=MESH)
    pl.semaphore_wait(barrier, len(peers))


def gather_kernel(count, planes, *refs):
    own = refs[:count]
    full = refs[count : 2 * count]
    send_sem, recv_sem, local_sem = refs[2 * count :]
    me = lax.axis_index("fsdp")
    core, near, far, plane, index = place(me, planes)
    other = index(plane, far, near, 1 - core)
    near_peer = index(plane, 1 - near, far, core)
    far_peer = index(plane, near, 1 - far, core)
    others = [lax.rem(plane + step, planes) for step in range(1, planes)]
    plane_peers = [index(p, near, far, core) for p in others]
    greet([other, near_peer, far_peer, *plane_peers])

    sent = [0] * count

    def push(which, chunk, peer, first=False):
        src = own[which] if first else full[which].at[chunk]
        copy = pltpu.make_async_remote_copy(
            src_ref=src,
            dst_ref=full[which].at[chunk],
            send_sem=send_sem.at[which, sent[which]],
            recv_sem=recv_sem.at[which, chunk],
            device_id=(peer,),
            device_id_type=MESH,
        )
        copy.start()
        sent[which] += 1
        pending.append(copy)

    pending = []

    def arrive(which, chunk):
        pltpu.make_async_copy(
            full[which].at[chunk], full[which].at[chunk], recv_sem.at[which, chunk]
        ).wait()

    for which in range(count):
        for peer in [*plane_peers, near_peer, far_peer, other]:
            push(which, me, peer, True)
    keep = [
        pltpu.make_async_copy(own[w], full[w].at[me], local_sem.at[w]) for w in range(count)
    ]
    for copy in keep:
        copy.start()
    for which in range(count):
        for p in others:
            chunk = index(p, near, far, core)
            arrive(which, chunk)
            for peer in (near_peer, far_peer, other):
                push(which, chunk, peer)
    for which in range(count):
        for p in [plane, *others]:
            chunk = index(p, 1 - near, far, core)
            arrive(which, chunk)
            for peer in (far_peer, other):
                push(which, chunk, peer)
    for which in range(count):
        for near_ in (near, 1 - near):
            for p in [plane, *others]:
                chunk = index(p, near_, 1 - far, core)
                arrive(which, chunk)
                push(which, chunk, other)
    for which in range(count):
        for p in range(planes):
            for spot in range(4):
                arrive(which, ((p * 2 + spot // 2) * 2 + spot % 2) * 2 + 1 - core)
    for copy in keep:
        copy.wait()
    for copy in pending:
        copy.wait_send()


def gather(arrays, size):
    planes = size // 8
    count = len(arrays)
    sends = (planes + 2) + (planes - 1) * 3 + planes * 2 + planes * 2
    return pl.pallas_call(
        functools.partial(gather_kernel, count, planes),
        out_shape=[jax.ShapeDtypeStruct((size, *a.shape), a.dtype) for a in arrays],
        in_specs=[pl.BlockSpec(memory_space=pl.ANY)] * count,
        out_specs=[pl.BlockSpec(memory_space=pl.ANY)] * count,
        scratch_shapes=[
            pltpu.SemaphoreType.DMA((count, sends)),
            pltpu.SemaphoreType.DMA((count, size)),
            pltpu.SemaphoreType.DMA((count,)),
        ],
        compiler_params=pltpu.CompilerParams(collective_id=0, has_side_effects=True),
        name="gather",
    )(*arrays)


def scatter_kernel(shapes, planes, *refs):
    count = len(shapes)
    half = planes * 4
    refs = list(refs)

    def take(n):
        out = refs[:n]
        del refs[:n]
        return out

    part = take(count)
    result = take(count)
    mine, got0, got1, got2, got3, final = (take(count) for _ in range(6))
    send_sem, recv_sem, load_sem = refs
    me = lax.axis_index("fsdp")
    core, near, far, plane, index = place(me, planes)
    other = index(plane, far, near, 1 - core)
    near_peer = index(plane, 1 - near, far, core)
    far_peer = index(plane, near, 1 - far, core)
    others = [lax.rem(plane + step, planes) for step in range(1, planes)]
    plane_peers = [index(p, near, far, core) for p in others]
    greet([other, near_peer, far_peer, *plane_peers])
    pending = []

    def push(src, dst, send, recv, peer):
        copy = pltpu.make_async_remote_copy(
            src_ref=src, dst_ref=dst, send_sem=send, recv_sem=recv,
            device_id=(peer,), device_id_type=MESH,
        )
        copy.start()
        pending.append(copy)

    def slot_of(far_step, near_step, p):
        return (1 - far_step) * 2 * planes + (1 - near_step) * planes + p

    loads = []
    for which in range(count):
        for far_step in (1, 0):
            for near_step in (1, 0):
                for p in range(planes):
                    slot = slot_of(far_step, near_step, p)
                    chunk = index(
                        p,
                        jnp.where(near_step == 1, 1 - far, far),
                        jnp.where(far_step == 1, 1 - near, near),
                        1 - core,
                    )
                    push(
                        part[which].at[chunk],
                        got0[which].at[slot],
                        send_sem.at[which, slot],
                        recv_sem.at[which, slot],
                        other,
                    )
                    own = index(
                        p,
                        jnp.where(near_step == 1, 1 - near, near),
                        jnp.where(far_step == 1, 1 - far, far),
                        core,
                    )
                    load = pltpu.make_async_copy(
                        part[which].at[own], mine[which].at[slot], load_sem.at[which, slot]
                    )
                    load.start()
                    loads.append(load)

    def landed(ref, sem):
        pltpu.make_async_copy(ref, ref, sem).wait()

    def add(which, first, number, extra):
        @pl.loop(0, number)
        def _(step):
            total = mine[which][first + step].astype(jnp.float32)
            for ref, start in extra:
                total = total + ref[start + step].astype(jnp.float32)
            mine[which][first + step] = total.astype(mine[which].dtype)

    for which in range(count):
        for slot in range(half // 2):
            loads[which * half + slot].wait()
            landed(got0[which].at[slot], recv_sem.at[which, slot])
        add(which, 0, half // 2, [(got0[which], 0)])
        push(
            mine[which].at[pl.ds(0, half // 2)], got1[which],
            send_sem.at[which, half], recv_sem.at[which, half], far_peer,
        )
    for which in range(count):
        for slot in range(half // 2, half):
            loads[which * half + slot].wait()
            landed(got0[which].at[slot], recv_sem.at[which, slot])
        landed(got1[which], recv_sem.at[which, half])
        add(which, half // 2, planes, [(got0[which], half // 2), (got1[which], 0)])
        push(
            mine[which].at[pl.ds(half // 2, planes)], got2[which],
            send_sem.at[which, half + 1], recv_sem.at[which, half + 1], near_peer,
        )
    last = half - planes
    for which in range(count):
        landed(got2[which], recv_sem.at[which, half + 1])
        spread = jnp.float32
        here = (
            mine[which][last + plane].astype(spread)
            + got0[which][last + plane].astype(spread)
            + got1[which][planes + plane].astype(spread)
            + got2[which][plane].astype(spread)
        )
        final[which][...] = here
        for step, p in enumerate(others):
            total = (
                mine[which][last + p].astype(spread)
                + got0[which][last + p].astype(spread)
                + got1[which][planes + p].astype(spread)
                + got2[which][p].astype(spread)
            )
            mine[which][last + p] = total.astype(mine[which].dtype)
            push(
                mine[which].at[last + p], got3[which].at[step],
                send_sem.at[which, half + 2 + step], recv_sem.at[which, half + 2 + step],
                plane_peers[step],
            )
    outs = []
    for which in range(count):
        total = final[which][...]
        for step in range(planes - 1):
            landed(got3[which].at[step], recv_sem.at[which, half + 2 + step])
            total = total + got3[which][step].astype(jnp.float32)
        final[which][...] = total
        copy = pltpu.make_async_copy(final[which], result[which], load_sem.at[which, half])
        copy.start()
        outs.append(copy)
    for copy in outs:
        copy.wait()
    for copy in pending:
        copy.wait_send()


def scatter(arrays, size):
    planes = size // 8
    half = size // 2
    count = len(arrays)
    shapes = [a.shape[1:] for a in arrays]
    vmem = lambda lead: [pltpu.VMEM((*lead, *a.shape[1:]), a.dtype) for a in arrays]
    return pl.pallas_call(
        functools.partial(scatter_kernel, shapes, planes),
        out_shape=[jax.ShapeDtypeStruct(s, jnp.float32) for s in shapes],
        in_specs=[pl.BlockSpec(memory_space=pl.ANY)] * count,
        out_specs=[pl.BlockSpec(memory_space=pl.ANY)] * count,
        scratch_shapes=[
            *vmem((half,)), *vmem((half,)), *vmem((half // 2,)), *vmem((planes,)), *vmem((planes - 1,)),
            *[pltpu.VMEM(s, jnp.float32) for s in shapes],
            pltpu.SemaphoreType.DMA((count, half + 1 + planes)),
            pltpu.SemaphoreType.DMA((count, half + 1 + planes)),
            pltpu.SemaphoreType.DMA((count, half + 1)),
        ],
        compiler_params=pltpu.CompilerParams(
            collective_id=1, has_side_effects=True, vmem_limit_bytes=60 << 20
        ),
        name="scatter",
    )(*arrays)


def ring_fits(size, rows):
    return size % 8 == 0 and size >= 16 and rows % 8 == 0


def collect(params, size):
    matrices, vectors = params[:6], params[6:]
    rows = matrices[0].shape[0]
    if not ring_fits(size, rows) or size != 32:
        return [lax.all_gather(p, "fsdp", axis=0, tiled=True) for p in params]
    packed = jnp.stack([jnp.pad(v, (0, 128 - v.shape[0])) for v in vectors])
    packed = jnp.pad(packed, ((0, 16 - packed.shape[0]), (0, 0)))
    *full, small = gather([*matrices, packed], size)
    full = [f.reshape(size * f.shape[1], f.shape[2]) for f in full]
    return full + [small[:, k, : v.shape[0]].reshape(-1) for k, v in enumerate(vectors)]


def share(grads, size):
    matrices, vectors = grads[:6], grads[6:]
    rows = matrices[0].shape[0] // size
    if not ring_fits(size, rows) or size != 32:
        return [lax.psum_scatter(g, "fsdp", scatter_dimension=0, tiled=True) for g in grads]
    low = [g.astype(jnp.bfloat16).reshape(size, g.shape[0] // size, g.shape[1]) for g in matrices]
    cut = [v.reshape(size, -1) for v in vectors]
    packed = jnp.stack([jnp.pad(v, ((0, 0), (0, 128 - v.shape[1]))) for v in cut], 1)
    packed = jnp.pad(packed, ((0, 0), (0, 16 - packed.shape[1]), (0, 0)))
    *out, small = scatter([*low, packed], size)
    return list(out) + [small[k, : v.shape[1]] for k, v in enumerate(cut)]


def local(
    size,
    inputs,
    cotangent,
    lengths,
    skip_bit,
    w_query,
    w_key,
    w_value,
    w_out,
    b_query,
    b_value,
    b_out,
    ln1_gain,
    ln1_bias,
    w_hidden,
    b_hidden,
    w_proj,
    b_proj,
    ln2_gain,
    ln2_bias,
):
    row_total, model_dim = inputs.shape
    slot_count = lengths.shape[0]
    slot_rows = row_total // slot_count
    head_dim = model_dim // HEADS
    live_rows = jnp.arange(slot_rows, dtype=jnp.int32)[None, :] < lengths[:, None]
    skip_rows = jnp.repeat(skip_bit, slot_rows, total_repeat_length=row_total)
    dropped = (skip_rows == 1)[:, None]
    (
        query_full, key_full, value_full, out_full, hidden_full, proj_full,
        bq_full, bv_full, bo_full, gain_one, shift_one, bh_full, bp_full, gain_two, shift_two,
    ) = collect(
        [
            w_query, w_key, w_value, w_out, w_hidden, w_proj,
            b_query, b_value, b_out, ln1_gain, ln1_bias, b_hidden, b_proj, ln2_gain, ln2_bias,
        ],
        size,
    )
    queries = (
        jnp.dot(inputs, query_full, preferred_element_type=jnp.float32) + as_float(bq_full)
    ).astype(jnp.bfloat16)
    keys_all = jnp.dot(inputs, key_full, preferred_element_type=jnp.float32).astype(jnp.bfloat16)
    values_all = (
        jnp.dot(inputs, value_full, preferred_element_type=jnp.float32) + as_float(bv_full)
    ).astype(jnp.bfloat16)
    q_slots = queries.reshape(slot_count, slot_rows, HEADS, head_dim)
    k_slots = keys_all.reshape(slot_count, slot_rows, HEADS, head_dim)
    v_slots = values_all.reshape(slot_count, slot_rows, HEADS, head_dim)
    slot_idx = 0
    mixed_out, log_sum = attend_forward(
        q_slots[slot_idx], k_slots[slot_idx], v_slots[slot_idx], live_rows[slot_idx]
    )
    lse_list = [log_sum]
    branch = jnp.dot(mixed_out, out_full, preferred_element_type=jnp.float32) + as_float(bo_full)
    first_norm, normed_one, inv_one = layer_norm(
        as_float(inputs) + branch, as_float(gain_one), as_float(shift_one)
    )
    first_low = first_norm.astype(jnp.bfloat16)
    pre_act = jnp.dot(first_low, hidden_full, preferred_element_type=jnp.float32) + as_float(
        bh_full
    )
    gelu_low = jax.nn.gelu(pre_act, approximate=False).astype(jnp.bfloat16)
    ffn_out = jnp.dot(gelu_low, proj_full, preferred_element_type=jnp.float32) + as_float(bp_full)
    layer_out, normed_two, inv_two = layer_norm(
        as_float(first_low) + ffn_out, as_float(gain_two), as_float(shift_two)
    )
    outputs = jnp.where(dropped, inputs, layer_out.astype(jnp.bfloat16))
    row_mask = live_rows.reshape(row_total).astype(jnp.float32)[:, None]
    cot_rows = as_float(cotangent) * row_mask
    grad_top = cot_rows * (1 - skip_rows).astype(jnp.float32)[:, None]
    d_gain_two = jnp.sum(grad_top * normed_two, 0)
    d_shift_two = jnp.sum(grad_top, 0)
    d_resid_two = norm_back(grad_top, normed_two, inv_two, as_float(gain_two))
    d_ffn = d_resid_two.astype(jnp.bfloat16)
    d_bias_proj = jnp.sum(as_float(d_ffn), 0)
    d_gelu = jnp.einsum("rd,fd->rf", d_ffn, proj_full, preferred_element_type=jnp.float32)
    d_pre = (d_gelu * gelu_slope(pre_act)).astype(jnp.bfloat16)
    d_bias_hidden = jnp.sum(as_float(d_pre), 0)
    d_first = d_resid_two + jnp.einsum(
        "rf,df->rd", d_pre, hidden_full, preferred_element_type=jnp.float32
    )
    d_weight_proj = jnp.einsum("rf,rd->fd", gelu_low, d_ffn, preferred_element_type=jnp.float32)
    d_weight_hidden = jnp.einsum("rd,rf->df", first_low, d_pre, preferred_element_type=jnp.float32)
    d_gain_one = jnp.sum(d_first * normed_one, 0)
    d_shift_one = jnp.sum(d_first, 0)
    d_resid_one = norm_back(d_first, normed_one, inv_one, as_float(gain_one))
    d_branch = d_resid_one.astype(jnp.bfloat16)
    d_bias_out = jnp.sum(as_float(d_branch), 0)
    d_attended = jnp.einsum(
        "re,de->rd", d_branch, out_full, preferred_element_type=jnp.float32
    ).astype(jnp.bfloat16)
    d_att_slots = d_attended.reshape(slot_count, slot_rows, HEADS, head_dim)
    slot_idx = 0
    d_query, d_key, d_value = attend_backward(
        q_slots[slot_idx],
        k_slots[slot_idx],
        v_slots[slot_idx],
        live_rows[slot_idx],
        d_att_slots[slot_idx],
        lse_list[slot_idx],
    )
    dq_low = d_query.astype(jnp.bfloat16)
    dk_low = d_key.astype(jnp.bfloat16)
    dv_low = d_value.astype(jnp.bfloat16)
    d_bias_query = jnp.sum(as_float(dq_low), 0)
    d_bias_value = jnp.sum(as_float(dv_low), 0)
    d_inputs = d_resid_one + jnp.einsum(
        "re,de->rd", dq_low, query_full, preferred_element_type=jnp.float32
    )
    d_inputs = d_inputs + jnp.einsum(
        "re,de->rd", dk_low, key_full, preferred_element_type=jnp.float32
    )
    d_inputs = d_inputs + jnp.einsum(
        "re,de->rd", dv_low, value_full, preferred_element_type=jnp.float32
    )
    d_weight_out = jnp.einsum("rd,re->de", mixed_out, d_branch, preferred_element_type=jnp.float32)
    d_weight_query = jnp.einsum("rd,re->de", inputs, dq_low, preferred_element_type=jnp.float32)
    d_weight_key = jnp.einsum("rd,re->de", inputs, dk_low, preferred_element_type=jnp.float32)
    d_weight_value = jnp.einsum("rd,re->de", inputs, dv_low, preferred_element_type=jnp.float32)
    (
        g_w_query, g_w_key, g_w_value, g_w_out, g_w_hidden, g_w_proj,
        g_b_query, g_b_value, g_b_out, g_ln1_gain, g_ln1_bias,
        g_b_hidden, g_b_proj, g_ln2_gain, g_ln2_bias,
    ) = share(
        [
            d_weight_query, d_weight_key, d_weight_value, d_weight_out, d_weight_hidden, d_weight_proj,
            d_bias_query, d_bias_value, d_bias_out, d_gain_one, d_shift_one,
            d_bias_hidden, d_bias_proj, d_gain_two, d_shift_two,
        ],
        size,
    )
    grad_inputs = jnp.where(dropped, cot_rows, d_inputs)
    return (
        outputs,
        grad_inputs,
        g_w_query,
        g_w_key,
        g_w_value,
        g_w_out,
        g_b_query,
        g_b_value,
        g_b_out,
        g_ln1_gain,
        g_ln1_bias,
        g_w_hidden,
        g_b_hidden,
        g_w_proj,
        g_b_proj,
        g_ln2_gain,
        g_ln2_bias,
    )


def solution(mesh):
    placed = (
        P("fsdp", None),
        P("fsdp", None),
        P("fsdp"),
        P("fsdp"),
        P("fsdp", None),
        P("fsdp", None),
        P("fsdp", None),
        P("fsdp", None),
        P("fsdp"),
        P("fsdp"),
        P("fsdp"),
        P("fsdp"),
        P("fsdp"),
        P("fsdp", None),
        P("fsdp"),
        P("fsdp", None),
        P("fsdp"),
        P("fsdp"),
        P("fsdp"),
    )
    return jax.shard_map(
        functools.partial(local, mesh.shape["fsdp"]),
        mesh=mesh,
        in_specs=placed,
        out_specs=(
            P("fsdp", None),
            P("fsdp", None),
            P("fsdp", None),
            P("fsdp", None),
            P("fsdp", None),
            P("fsdp", None),
            P("fsdp"),
            P("fsdp"),
            P("fsdp"),
            P("fsdp"),
            P("fsdp"),
            P("fsdp", None),
            P("fsdp"),
            P("fsdp", None),
            P("fsdp"),
            P("fsdp"),
            P("fsdp"),
        ),
        check_vma=False,
    )
```

```python
import functools
import math

import jax
import jax.numpy as jnp
from jax import lax
from jax.experimental import pallas as pl
from jax.experimental.pallas import tpu as pltpu
from jax.sharding import PartitionSpec as P

HEADS = 12
LIVE = 800
EPSILON = 1e-05
NEG_FILL = -1e30
NT = (((1,), (1,)), ((), ()))
TN = (((0,), (0,)), ((), ()))
VMEM = pltpu.VMEM
F32, BF16 = jnp.float32, jnp.bfloat16


def dot(a, b, dims=(((1,), (0,)), ((), ()))):
    return lax.dot_general(a, b, dims, preferred_element_type=F32)


def lanes_of(shape, head, dim):
    lane = lax.broadcasted_iota(jnp.int32, shape, 1)
    return (lane < dim) if head == 0 else (lane >= dim)


def attend_kernel(lengths, x, wq, wk, wv, bq, bv, q, k, v, att, keys, values):
    rows, width = x.shape
    dim = width // HEADS
    pair = 2 * dim
    group = 2 * pair
    step = 256
    key_lane = lax.broadcasted_iota(jnp.int32, (1, LIVE), 1)
    bias = jnp.where(key_lane < lengths[0], 0.0, NEG_FILL).astype(F32)
    for head in range(2):
        values[head, :, pair:] = jnp.ones((LIVE, pair), BF16)
    for first in range(0, width, group):
        cols = pl.ds(first, group)

        @pl.loop(0, rows // step)
        def _(part):
            at = pl.ds(pl.multiple_of(part * step, step), step)
            here = x[at, :]
            q[at, cols] = ((dot(here, wq[:, cols]) + bq[:, cols]).astype(BF16).astype(F32) * (1.0 / math.sqrt(dim))).astype(BF16)
            k[at, cols] = dot(here, wk[:, cols]).astype(BF16)
            v[at, cols] = (dot(here, wv[:, cols]) + bv[:, cols]).astype(BF16)

        for start in range(first, first + group, pair):
            wide = pl.ds(start, pair)
            whole = k[:LIVE, wide]
            for head in range(2):
                keys[head] = jnp.where(lanes_of(whole.shape, head, dim), whole, jnp.zeros_like(whole))
                values[head, :, :pair] = v[:LIVE, wide]

            @pl.loop(0, rows // step)
            def _(part):
                at = pl.ds(pl.multiple_of(part * step, step), step)
                here = q[at, wide]
                outs = []
                for head in range(2):
                    s = dot(here, keys[head], NT) + bias
                    e = jnp.exp(s - jnp.max(s, -1, keepdims=True))
                    o = dot(e.astype(BF16), values[head])
                    outs.append(o[:, :pair] / o[:, pair:])
                att[at, wide] = jnp.where(lanes_of(outs[0].shape, 0, dim), outs[0], outs[1]).astype(BF16)


def attend(lengths, x, wq, wk, wv, bq, bv):
    rows, width = x.shape
    pair = 2 * width // HEADS
    return pl.pallas_call(
        attend_kernel,
        out_shape=[jax.ShapeDtypeStruct(x.shape, BF16)] * 4,
        in_specs=[pl.BlockSpec(memory_space=pltpu.SMEM)] + [pl.BlockSpec(memory_space=VMEM)] * 6,
        out_specs=[pl.BlockSpec(memory_space=VMEM)] * 4,
        scratch_shapes=[VMEM((2, LIVE, pair), BF16), VMEM((2, LIVE, 2 * pair), BF16)],
        compiler_params=pltpu.CompilerParams(vmem_limit_bytes=60 << 20),
        name="attend",
    )(lengths, x, wq, wk, wv, bq, bv)


def attend_back_kernel(lengths, x, dh1, q, k, v, da, wq, wk, wv, cot, skip, gin, gwq, gwk, gwv, gbq, gbv,
                       dq, dk, dv, keys, values, bias, dk_acc, dv_acc):
    rows, width = x.shape
    dim = width // HEADS
    pair = 2 * dim
    chunk = 256
    tops = [(c, min(chunk, -(-LIVE // 128) * 128 - c)) for c in range(0, LIVE, chunk)]
    key_row = lax.broadcasted_iota(jnp.int32, (LIVE, 128), 0)
    bias[...] = jnp.where(key_row < lengths[0], 0.0, NEG_FILL).astype(F32)
    dk[...] = jnp.zeros_like(dk)
    dv[...] = jnp.zeros_like(dv)

    def block(wide, start, size):
        at = pl.ds(start, size)
        q_c, da_c = q[at, wide], da[at, wide]
        dq_c = jnp.zeros((size, pair), F32)
        for head in range(2):
            mine = lanes_of(q_c.shape, head, dim)
            s = dot(keys[head], q_c, NT) + jnp.tile(bias[...], (1, size // 128))
            e = jnp.exp(s - jnp.max(s, 0, keepdims=True))
            p = e * (1.0 / jnp.sum(e, 0, keepdims=True))
            dp = dot(values[head], da_c, NT)
            t = p * dp
            ds = (t - p * jnp.sum(t, 0, keepdims=True)).astype(BF16)
            dv_acc[...] += dot(p.astype(BF16), jnp.where(mine, da_c, jnp.zeros_like(da_c)))
            dk_acc[...] += dot(ds, jnp.where(mine, q_c, jnp.zeros_like(q_c)))
            dq_c = dq_c + dot(ds, keys[head], TN)
        dq[at, wide] = (dq_c * (1.0 / math.sqrt(dim))).astype(BF16)

    @pl.loop(0, width // pair)
    def _(which):
        wide = pl.ds(pl.multiple_of(which * pair, pair), pair)
        whole, whole_v = k[:LIVE, wide], v[:LIVE, wide]
        for head in range(2):
            mine = lanes_of(whole.shape, head, dim)
            keys[head] = jnp.where(mine, whole, jnp.zeros_like(whole))
            values[head] = jnp.where(mine, whole_v, jnp.zeros_like(whole_v))
        dk_acc[...] = jnp.zeros_like(dk_acc)
        dv_acc[...] = jnp.zeros_like(dv_acc)

        @pl.loop(0, LIVE // chunk)
        def _(part):
            block(wide, pl.multiple_of(part * chunk, chunk), chunk)

        for start, size in tops:
            if size < chunk:
                block(wide, start, size)
        dk[:LIVE, wide] = dk_acc[...].astype(BF16)
        dv[:LIVE, wide] = dv_acc[...].astype(BF16)

    gbq[...] = jnp.sum(dq[:LIVE, :].astype(F32), 0, keepdims=True)
    gbv[...] = jnp.sum(dv[:LIVE, :].astype(F32), 0, keepdims=True)
    here = x[:LIVE, :]
    for grad, out in ((dq, gwq), (dk, gwk), (dv, gwv)):
        for start in range(0, width, 256):
            cols = pl.ds(start, 256)
            out[:, cols] = dot(here, grad[:LIVE, cols], TN).astype(BF16)
    step = 160

    @pl.loop(0, LIVE // step)
    def _(part):
        at = pl.ds(pl.multiple_of(part * step, step), step)
        total = dh1[at, :] + dot(dq[at, :], wq[...], NT)
        total = total + dot(dk[at, :], wk[...], NT)
        total = total + dot(dv[at, :], wv[...], NT)
        row = lax.broadcasted_iota(jnp.int32, (step, 1), 0) + part * step
        dropped = jnp.where(row < lengths[0], cot[at, :].astype(F32), 0.0)
        gin[at, :] = jnp.where(skip[0] == 1, dropped, total)

    gin[LIVE:, :] = jnp.zeros((rows - LIVE, width), F32)


def attend_back(lengths, x, dh1, q, k, v, da, wq, wk, wv, cot, skip):
    rows, width = x.shape
    pair = 2 * width // HEADS
    like = jax.ShapeDtypeStruct
    smem = pl.BlockSpec(memory_space=pltpu.SMEM)
    return pl.pallas_call(
        attend_back_kernel,
        out_shape=[like((rows, width), F32)] + [like((width, width), BF16)] * 3 + [like((1, width), F32)] * 2,
        in_specs=[smem] + [pl.BlockSpec(memory_space=VMEM)] * 10 + [smem],
        out_specs=[pl.BlockSpec(memory_space=VMEM)] * 6,
        scratch_shapes=[VMEM(x.shape, BF16)] * 3
        + [VMEM((2, LIVE, pair), BF16)] * 2
        + [VMEM((LIVE, 128), F32)]
        + [VMEM((LIVE, pair), F32)] * 2,
        compiler_params=pltpu.CompilerParams(vmem_limit_bytes=62 << 20),
        name="attend_back",
    )(lengths, x, dh1, q, k, v, da, wq, wk, wv, cot, skip)


def middle_kernel(lengths, skip, x_in, att_in, cot_in, wo_in, wh_in, wp_in, vec, bh,
                  outputs, dh1, da, gwo, gwh, gwp, gvec, gbh,
                  x, att, cot, wo, wh, wp, z1, n1, inv1, f, g, slope, df, z1t, out_h, out_p, load_sem, out_sem):
    rows, width = x.shape
    inner = wh.shape[1]
    loads = [
        pltpu.make_async_copy(a, b, load_sem.at[i])
        for i, (a, b) in enumerate(
            ((x_in, x), (att_in, att), (wo_in, wo), (wh_in, wh), (wp_in, wp), (cot_in, cot))
        )
    ]
    for load in loads:
        load.start()
    bo, gain1, shift1, bp, gain2, shift2 = (vec[i : i + 1, :] for i in range(6))
    for load in loads[:3]:
        load.wait()
    step = 256

    def norm(h):
        centred = h - jnp.mean(h, -1, keepdims=True)
        inv = lax.rsqrt(jnp.mean(centred * centred, -1, keepdims=True) + EPSILON)
        return centred * inv, inv

    def norm_back(e, n, inv):
        return inv * (e - jnp.mean(e, -1, keepdims=True) - n * jnp.mean(e * n, -1, keepdims=True))

    @pl.loop(0, rows // step)
    def _(part):
        at = pl.ds(pl.multiple_of(part * step, step), step)
        h = x[at, :].astype(F32) + (dot(att[at, :], wo[...]) + bo)
        n, inv = norm(h)
        n1[at, :] = n
        inv1[at, :] = jnp.broadcast_to(inv, (step, 128))
        z1[at, :] = (n * gain1 + shift1).astype(BF16)

    loads[3].wait()
    loads[4].wait()
    f[...] = jnp.zeros_like(f)
    wide = 256

    @pl.loop(0, inner // wide)
    def _(block):
        cols = pl.ds(pl.multiple_of(block * wide, wide), wide)
        b = bh[:, cols]
        for start in range(0, rows, step):
            at = pl.ds(start, step)
            u = dot(z1[at, :], wh[:, cols]) + b
            phi = 0.5 * (1.0 + lax.erf(u * 0.7071067811865476))
            g[at, cols] = (u * phi).astype(BF16)
            slope[at, cols] = (phi + u * (jnp.exp(-0.5 * u * u) * 0.3989422804014327)).astype(BF16)
            f[at, :] += dot(g[at, cols], wp[cols, :])

    loads[5].wait()
    gvec[...] = jnp.zeros_like(gvec)
    keep = 1.0 - skip[0].astype(F32)

    @pl.loop(0, rows // step)
    def _(part):
        at = pl.ds(pl.multiple_of(part * step, step), step)
        n, inv = norm(z1[at, :].astype(F32) + (f[at, :] + bp))
        outputs[at, :] = jnp.where(skip[0] == 1, x[at, :], (n * gain2 + shift2).astype(BF16))
        row = lax.broadcasted_iota(jnp.int32, (step, 1), 0) + part * step
        dy = jnp.where(row < lengths[0], cot[at, :].astype(F32), 0.0) * keep
        d = norm_back(dy * gain2, n, inv)
        low = d.astype(BF16)
        f[at, :] = d
        df[at, :] = low
        gvec[3:4, :] += jnp.sum(low.astype(F32), 0, keepdims=True)
        gvec[4:5, :] += jnp.sum(dy * n, 0, keepdims=True)
        gvec[5:6, :] += jnp.sum(dy, 0, keepdims=True)

    z1t[...] = z1[:LIVE, :].T

    def flush(block, buf, slot):
        cols = pl.ds(pl.multiple_of(block * wide, wide), wide)
        if buf is out_h:
            return pltpu.make_async_copy(buf.at[slot], gwh.at[:, cols], out_sem.at[0, slot])
        return pltpu.make_async_copy(buf.at[slot], gwp.at[cols, :], out_sem.at[1, slot])

    @pl.loop(0, inner // wide)
    def _(block):
        slot = lax.rem(block, 2)
        cols = pl.ds(pl.multiple_of(block * wide, wide), wide)

        @pl.when(block >= 2)
        def _():
            flush(block, out_h, slot).wait()
            flush(block, out_p, slot).wait()

        out_p[slot] = dot(g[:LIVE, cols], df[:LIVE, :], TN).astype(BF16)
        flush(block, out_p, slot).start()
        total = jnp.zeros((1, wide), F32)
        half = LIVE // 2
        for start in range(0, LIVE, half):
            at = pl.ds(start, half)
            du = (dot(df[at, :], wp[cols, :], NT) * slope[at, cols].astype(F32)).astype(BF16)
            total = total + jnp.sum(du.astype(F32), 0, keepdims=True)
            g[at, cols] = du
            f[at, :] += dot(du, wh[:, cols], NT)
        gbh[:, cols] = total
        out_h[slot] = dot(z1t[...], g[:LIVE, cols]).astype(BF16)
        flush(block, out_h, slot).start()

    half = LIVE // 5
    @pl.loop(0, LIVE // half)
    def _(part):
        at = pl.ds(pl.multiple_of(part * half, half), half)
        dz = f[at, :]
        n = n1[at, :]
        gvec[1:2, :] += jnp.sum(dz * n, 0, keepdims=True)
        gvec[2:3, :] += jnp.sum(dz, 0, keepdims=True)
        d = norm_back(dz * gain1, n, inv1[at, :1])
        dh1[at, :] = d
        low = d.astype(BF16)
        df[at, :] = low
        gvec[0:1, :] += jnp.sum(low.astype(F32), 0, keepdims=True)
        da[at, :] = dot(low, wo[...], NT).astype(BF16)

    da[LIVE:, :] = jnp.zeros((rows - LIVE, width), BF16)
    for start in range(0, width, wide):
        cols = pl.ds(start, wide)
        gwo[cols, :] = dot(att[:LIVE, cols], df[:LIVE, :], TN).astype(BF16)
    for block in (inner // wide - 2, inner // wide - 1):
        flush(block, out_h, block % 2).wait()
        flush(block, out_p, block % 2).wait()


def middle(lengths, skip, x, att, cot, wo, wh, wp, vec, bh):
    rows, width = x.shape
    inner = wh.shape[1]
    like = jax.ShapeDtypeStruct
    smem, vmem, any_ = (pl.BlockSpec(memory_space=m) for m in (pltpu.SMEM, VMEM, pl.ANY))
    pad = -(-LIVE // 128) * 128
    return pl.pallas_call(
        middle_kernel,
        out_shape=[
            like((rows, width), BF16), like((LIVE, width), F32), like((rows, width), BF16),
            like((width, width), BF16), like((width, inner), BF16), like((inner, width), BF16),
            like((8, width), F32), like((1, inner), F32),
        ],
        in_specs=[smem] * 2 + [any_] * 6 + [vmem] * 2,
        out_specs=[vmem] * 4 + [any_] * 2 + [vmem] * 2,
        scratch_shapes=[
            VMEM((rows, width), BF16), VMEM((rows, width), BF16), VMEM((rows, width), BF16),
            VMEM((width, width), BF16), VMEM((width, inner), BF16), VMEM((inner, width), BF16),
            VMEM((rows, width), BF16), VMEM((rows, width), F32), VMEM((rows, 128), F32),
            VMEM((rows, width), F32), VMEM((rows, inner), BF16), VMEM((rows, inner), BF16),
            VMEM((rows, width), BF16), VMEM((width, LIVE), BF16),
            VMEM((2, width, 256), BF16), VMEM((2, 256, width), BF16),
            pltpu.SemaphoreType.DMA((6,)), pltpu.SemaphoreType.DMA((2, 2)),
        ],
        compiler_params=pltpu.CompilerParams(vmem_limit_bytes=63 << 20),
        name="middle",
    )(lengths, skip, x, att, cot, wo, wh, wp, vec, bh)


def as_float(value):
    return value.astype(jnp.float32)


MESH = pl.DeviceIdType.MESH


def place(me, planes):
    core = lax.rem(me, 2)
    chip = me // 2
    col = lax.rem(chip, 2)
    row = lax.rem(chip // 2, 2)
    plane = chip // 4
    near = jnp.where(core == 0, row, col)
    far = jnp.where(core == 0, col, row)

    def index(plane_, near_, far_, core_):
        row_ = jnp.where(core_ == 0, near_, far_)
        col_ = jnp.where(core_ == 0, far_, near_)
        return ((plane_ * 2 + row_) * 2 + col_) * 2 + core_

    return core, near, far, plane, index


def greet(peers):
    barrier = pltpu.get_barrier_semaphore()
    for peer in peers:
        pl.semaphore_signal(barrier, inc=1, device_id=(peer,), device_id_type=MESH)
    pl.semaphore_wait(barrier, len(peers))


def gather_kernel(count, planes, *refs):
    own = refs[:count]
    full = refs[count : 2 * count]
    send_sem, recv_sem, local_sem = refs[2 * count :]
    me = lax.axis_index("fsdp")
    core, near, far, plane, index = place(me, planes)
    other = index(plane, far, near, 1 - core)
    near_peer = index(plane, 1 - near, far, core)
    far_peer = index(plane, near, 1 - far, core)
    others = [lax.rem(plane + step, planes) for step in range(1, planes)]
    plane_peers = [index(p, near, far, core) for p in others]
    greet([other, near_peer, far_peer, *plane_peers])

    sent = [0] * count

    def push(which, chunk, peer, first=False):
        src = own[which] if first else full[which].at[chunk]
        copy = pltpu.make_async_remote_copy(
            src_ref=src,
            dst_ref=full[which].at[chunk],
            send_sem=send_sem.at[which, sent[which]],
            recv_sem=recv_sem.at[which, chunk],
            device_id=(peer,),
            device_id_type=MESH,
        )
        copy.start()
        sent[which] += 1
        pending.append(copy)

    pending = []

    def arrive(which, chunk):
        pltpu.make_async_copy(
            full[which].at[chunk], full[which].at[chunk], recv_sem.at[which, chunk]
        ).wait()

    for which in range(count):
        for peer in [*plane_peers, near_peer, far_peer, other]:
            push(which, me, peer, True)
    keep = [
        pltpu.make_async_copy(own[w], full[w].at[me], local_sem.at[w]) for w in range(count)
    ]
    for copy in keep:
        copy.start()
    for which in range(count):
        for p in others:
            chunk = index(p, near, far, core)
            arrive(which, chunk)
            for peer in (near_peer, far_peer, other):
                push(which, chunk, peer)
    for which in range(count):
        for p in [plane, *others]:
            chunk = index(p, 1 - near, far, core)
            arrive(which, chunk)
            for peer in (far_peer, other):
                push(which, chunk, peer)
    for which in range(count):
        for near_ in (near, 1 - near):
            for p in [plane, *others]:
                chunk = index(p, near_, 1 - far, core)
                arrive(which, chunk)
                push(which, chunk, other)
    for which in range(count):
        for p in range(planes):
            for spot in range(4):
                arrive(which, ((p * 2 + spot // 2) * 2 + spot % 2) * 2 + 1 - core)
    for copy in keep:
        copy.wait()
    for copy in pending:
        copy.wait_send()


def gather(arrays, size):
    planes = size // 8
    count = len(arrays)
    sends = (planes + 2) + (planes - 1) * 3 + planes * 2 + planes * 2
    return pl.pallas_call(
        functools.partial(gather_kernel, count, planes),
        out_shape=[jax.ShapeDtypeStruct((size, *a.shape), a.dtype) for a in arrays],
        in_specs=[pl.BlockSpec(memory_space=pl.ANY)] * count,
        out_specs=[pl.BlockSpec(memory_space=pl.ANY)] * count,
        scratch_shapes=[
            pltpu.SemaphoreType.DMA((count, sends)),
            pltpu.SemaphoreType.DMA((count, size)),
            pltpu.SemaphoreType.DMA((count,)),
        ],
        compiler_params=pltpu.CompilerParams(collective_id=0, has_side_effects=True),
        name="gather",
    )(*arrays)


def scatter_kernel(shapes, planes, *refs):
    count = len(shapes)
    half = planes * 4
    refs = list(refs)

    def take(n):
        out = refs[:n]
        del refs[:n]
        return out

    part = take(count)
    result = take(count)
    mine, got0, got1, got2, got3, final = (take(count) for _ in range(6))
    send_sem, recv_sem, load_sem = refs
    me = lax.axis_index("fsdp")
    core, near, far, plane, index = place(me, planes)
    other = index(plane, far, near, 1 - core)
    near_peer = index(plane, 1 - near, far, core)
    far_peer = index(plane, near, 1 - far, core)
    others = [lax.rem(plane + step, planes) for step in range(1, planes)]
    plane_peers = [index(p, near, far, core) for p in others]
    greet([other, near_peer, far_peer, *plane_peers])
    pending = []

    def push(src, dst, send, recv, peer):
        copy = pltpu.make_async_remote_copy(
            src_ref=src, dst_ref=dst, send_sem=send, recv_sem=recv,
            device_id=(peer,), device_id_type=MESH,
        )
        copy.start()
        pending.append(copy)

    def slot_of(far_step, near_step, p):
        return (1 - far_step) * 2 * planes + (1 - near_step) * planes + p

    loads = []
    for which in range(count):
        for far_step in (1, 0):
            for near_step in (1, 0):
                for p in range(planes):
                    slot = slot_of(far_step, near_step, p)
                    chunk = index(
                        p,
                        jnp.where(near_step == 1, 1 - far, far),
                        jnp.where(far_step == 1, 1 - near, near),
                        1 - core,
                    )
                    push(
                        part[which].at[chunk],
                        got0[which].at[slot],
                        send_sem.at[which, slot],
                        recv_sem.at[which, slot],
                        other,
                    )
                    own = index(
                        p,
                        jnp.where(near_step == 1, 1 - near, near),
                        jnp.where(far_step == 1, 1 - far, far),
                        core,
                    )
                    load = pltpu.make_async_copy(
                        part[which].at[own], mine[which].at[slot], load_sem.at[which, slot]
                    )
                    load.start()
                    loads.append(load)

    def landed(ref, sem):
        pltpu.make_async_copy(ref, ref, sem).wait()

    def add(which, first, number, extra):
        @pl.loop(0, number)
        def _(step):
            total = mine[which][first + step].astype(jnp.float32)
            for ref, start in extra:
                total = total + ref[start + step].astype(jnp.float32)
            mine[which][first + step] = total.astype(mine[which].dtype)

    for which in range(count):
        for slot in range(half // 2):
            loads[which * half + slot].wait()
            landed(got0[which].at[slot], recv_sem.at[which, slot])
        add(which, 0, half // 2, [(got0[which], 0)])
        push(
            mine[which].at[pl.ds(0, half // 2)], got1[which],
            send_sem.at[which, half], recv_sem.at[which, half], far_peer,
        )
    for which in range(count):
        for slot in range(half // 2, half):
            loads[which * half + slot].wait()
            landed(got0[which].at[slot], recv_sem.at[which, slot])
        landed(got1[which], recv_sem.at[which, half])
        add(which, half // 2, planes, [(got0[which], half // 2), (got1[which], 0)])
        push(
            mine[which].at[pl.ds(half // 2, planes)], got2[which],
            send_sem.at[which, half + 1], recv_sem.at[which, half + 1], near_peer,
        )
    last = half - planes
    for which in range(count):
        landed(got2[which], recv_sem.at[which, half + 1])
        spread = jnp.float32
        here = (
            mine[which][last + plane].astype(spread)
            + got0[which][last + plane].astype(spread)
            + got1[which][planes + plane].astype(spread)
            + got2[which][plane].astype(spread)
        )
        final[which][...] = here
        for step, p in enumerate(others):
            total = (
                mine[which][last + p].astype(spread)
                + got0[which][last + p].astype(spread)
                + got1[which][planes + p].astype(spread)
                + got2[which][p].astype(spread)
            )
            mine[which][last + p] = total.astype(mine[which].dtype)
            push(
                mine[which].at[last + p], got3[which].at[step],
                send_sem.at[which, half + 2 + step], recv_sem.at[which, half + 2 + step],
                plane_peers[step],
            )
    outs = []
    for which in range(count):
        total = final[which][...]
        for step in range(planes - 1):
            landed(got3[which].at[step], recv_sem.at[which, half + 2 + step])
            total = total + got3[which][step].astype(jnp.float32)
        final[which][...] = total
        copy = pltpu.make_async_copy(final[which], result[which], load_sem.at[which, half])
        copy.start()
        outs.append(copy)
    for copy in outs:
        copy.wait()
    for copy in pending:
        copy.wait_send()


def scatter(arrays, size):
    planes = size // 8
    half = size // 2
    count = len(arrays)
    shapes = [a.shape[1:] for a in arrays]
    vmem = lambda lead: [pltpu.VMEM((*lead, *a.shape[1:]), a.dtype) for a in arrays]
    return pl.pallas_call(
        functools.partial(scatter_kernel, shapes, planes),
        out_shape=[jax.ShapeDtypeStruct(s, jnp.float32) for s in shapes],
        in_specs=[pl.BlockSpec(memory_space=pl.ANY)] * count,
        out_specs=[pl.BlockSpec(memory_space=pl.ANY)] * count,
        scratch_shapes=[
            *vmem((half,)), *vmem((half,)), *vmem((half // 2,)), *vmem((planes,)), *vmem((planes - 1,)),
            *[pltpu.VMEM(s, jnp.float32) for s in shapes],
            pltpu.SemaphoreType.DMA((count, half + 1 + planes)),
            pltpu.SemaphoreType.DMA((count, half + 1 + planes)),
            pltpu.SemaphoreType.DMA((count, half + 1)),
        ],
        compiler_params=pltpu.CompilerParams(
            collective_id=1, has_side_effects=True, vmem_limit_bytes=60 << 20
        ),
        name="scatter",
    )(*arrays)


def ring_fits(size, rows):
    return size % 8 == 0 and size >= 16 and rows % 8 == 0


def collect(params, size):
    matrices, vectors = params[:6], params[6:]
    rows = matrices[0].shape[0]
    if not ring_fits(size, rows) or size != 32:
        return [lax.all_gather(p, "fsdp", axis=0, tiled=True) for p in params]
    packed = jnp.stack([jnp.pad(v, (0, 128 - v.shape[0])) for v in vectors])
    packed = jnp.pad(packed, ((0, 16 - packed.shape[0]), (0, 0)))
    *full, small = gather([*matrices, packed], size)
    full = [f.reshape(size * f.shape[1], f.shape[2]) for f in full]
    return full + [small[:, k, : v.shape[0]].reshape(-1) for k, v in enumerate(vectors)]


def share(grads, size):
    matrices, vectors = grads[:6], grads[6:]
    rows = matrices[0].shape[0] // size
    if not ring_fits(size, rows) or size != 32:
        return [lax.psum_scatter(as_float(g), "fsdp", scatter_dimension=0, tiled=True) for g in grads]
    low = [g.astype(jnp.bfloat16).reshape(size, g.shape[0] // size, g.shape[1]) for g in matrices]
    cut = [v.reshape(size, -1) for v in vectors]
    packed = jnp.stack([jnp.pad(v, ((0, 0), (0, 128 - v.shape[1]))) for v in cut], 1)
    packed = jnp.pad(packed, ((0, 0), (0, 16 - packed.shape[1]), (0, 0)))
    *out, small = scatter([*low, packed], size)
    return list(out) + [small[k, : v.shape[1]] for k, v in enumerate(cut)]


def local(
    size,
    inputs,
    cotangent,
    lengths,
    skip_bit,
    w_query,
    w_key,
    w_value,
    w_out,
    b_query,
    b_value,
    b_out,
    ln1_gain,
    ln1_bias,
    w_hidden,
    b_hidden,
    w_proj,
    b_proj,
    ln2_gain,
    ln2_bias,
):
    (
        query_full, key_full, value_full, out_full, hidden_full, proj_full,
        bq_full, bv_full, bo_full, gain_one, shift_one, bh_full, bp_full, gain_two, shift_two,
    ) = collect(
        [
            w_query, w_key, w_value, w_out, w_hidden, w_proj,
            b_query, b_value, b_out, ln1_gain, ln1_bias, b_hidden, b_proj, ln2_gain, ln2_bias,
        ],
        size,
    )
    row = lambda v: as_float(v)[None, :]
    q, k, v, att = attend(
        lengths, inputs, query_full, key_full, value_full, row(bq_full), row(bv_full)
    )
    vec = jnp.stack([as_float(v_) for v_ in (bo_full, gain_one, shift_one, bp_full, gain_two, shift_two)])
    vec = jnp.pad(vec, ((0, 2), (0, 0)))
    outputs, dh1, da, d_weight_out, d_weight_hidden, d_weight_proj, gvec, gbh = middle(
        lengths, skip_bit, inputs, att, cotangent, out_full, hidden_full, proj_full, vec, row(bh_full)
    )
    grad_inputs, d_weight_query, d_weight_key, d_weight_value, gbq, gbv = attend_back(
        lengths, inputs, dh1, q, k, v, da, query_full, key_full, value_full, cotangent, skip_bit
    )
    (
        g_w_query, g_w_key, g_w_value, g_w_out, g_w_hidden, g_w_proj,
        g_b_query, g_b_value, g_b_out, g_ln1_gain, g_ln1_bias,
        g_b_hidden, g_b_proj, g_ln2_gain, g_ln2_bias,
    ) = share(
        [
            d_weight_query, d_weight_key, d_weight_value, d_weight_out, d_weight_hidden, d_weight_proj,
            gbq[0], gbv[0], gvec[0], gvec[1], gvec[2], gbh[0], gvec[3], gvec[4], gvec[5],
        ],
        size,
    )
    return (
        outputs,
        grad_inputs,
        g_w_query,
        g_w_key,
        g_w_value,
        g_w_out,
        g_b_query,
        g_b_value,
        g_b_out,
        g_ln1_gain,
        g_ln1_bias,
        g_w_hidden,
        g_b_hidden,
        g_w_proj,
        g_b_proj,
        g_ln2_gain,
        g_ln2_bias,
    )


def solution(mesh):
    placed = (
        P("fsdp", None),
        P("fsdp", None),
        P("fsdp"),
        P("fsdp"),
        P("fsdp", None),
        P("fsdp", None),
        P("fsdp", None),
        P("fsdp", None),
        P("fsdp"),
        P("fsdp"),
        P("fsdp"),
        P("fsdp"),
        P("fsdp"),
        P("fsdp", None),
        P("fsdp"),
        P("fsdp", None),
        P("fsdp"),
        P("fsdp"),
        P("fsdp"),
    )
    return jax.shard_map(
        functools.partial(local, mesh.shape["fsdp"]),
        mesh=mesh,
        in_specs=placed,
        out_specs=(
            P("fsdp", None),
            P("fsdp", None),
            P("fsdp", None),
            P("fsdp", None),
            P("fsdp", None),
            P("fsdp", None),
            P("fsdp"),
            P("fsdp"),
            P("fsdp"),
            P("fsdp"),
            P("fsdp"),
            P("fsdp", None),
            P("fsdp"),
            P("fsdp", None),
            P("fsdp"),
            P("fsdp"),
            P("fsdp"),
        ),
        check_vma=False,
    )
```

```python
import functools
import math

import jax
import jax.numpy as jnp
from jax import lax
from jax.experimental import pallas as pl
from jax.experimental.pallas import tpu as pltpu
from jax.sharding import PartitionSpec as P

HEADS = 12
LIVE = 800
EPSILON = 1e-05
NEG_FILL = -1e30
NT = (((1,), (1,)), ((), ()))
TN = (((0,), (0,)), ((), ()))
VMEM = pltpu.VMEM
F32, BF16 = jnp.float32, jnp.bfloat16


def dot(a, b, dims=(((1,), (0,)), ((), ()))):
    return lax.dot_general(a, b, dims, preferred_element_type=F32)


def lanes_of(shape, head, dim):
    lane = lax.broadcasted_iota(jnp.int32, shape, 1)
    return (lane < dim) if head == 0 else (lane >= dim)


def attend_kernel(lengths, x, wq, wk, wv, bq, bv, q, k, v, att, keys, values):
    rows, width = x.shape
    dim = width // HEADS
    pair = 2 * dim
    group = 2 * pair
    step = 256
    key_lane = lax.broadcasted_iota(jnp.int32, (1, LIVE), 1)
    bias = jnp.where(key_lane < lengths[0], 0.0, NEG_FILL).astype(F32)
    for head in range(2):
        values[head, :, pair:] = jnp.ones((LIVE, pair), BF16)
    for first in range(0, width, group):
        cols = pl.ds(first, group)

        @pl.loop(0, rows // step)
        def _(part):
            at = pl.ds(pl.multiple_of(part * step, step), step)
            here = x[at, :]
            q[at, cols] = ((dot(here, wq[:, cols]) + bq[:, cols]).astype(BF16).astype(F32) * (1.0 / math.sqrt(dim))).astype(BF16)
            k[at, cols] = dot(here, wk[:, cols]).astype(BF16)
            v[at, cols] = (dot(here, wv[:, cols]) + bv[:, cols]).astype(BF16)

        for start in range(first, first + group, pair):
            wide = pl.ds(start, pair)
            whole = k[:LIVE, wide]
            for head in range(2):
                keys[head] = jnp.where(lanes_of(whole.shape, head, dim), whole, jnp.zeros_like(whole))
                values[head, :, :pair] = v[:LIVE, wide]

            @pl.loop(0, rows // step)
            def _(part):
                at = pl.ds(pl.multiple_of(part * step, step), step)
                here = q[at, wide]
                outs = []
                for head in range(2):
                    s = dot(here, keys[head], NT) + bias
                    e = jnp.exp(s - jnp.max(s, -1, keepdims=True))
                    o = dot(e.astype(BF16), values[head])
                    outs.append(o[:, :pair] / o[:, pair:])
                att[at, wide] = jnp.where(lanes_of(outs[0].shape, 0, dim), outs[0], outs[1]).astype(BF16)


def attend(lengths, x, wq, wk, wv, bq, bv):
    rows, width = x.shape
    pair = 2 * width // HEADS
    return pl.pallas_call(
        attend_kernel,
        out_shape=[jax.ShapeDtypeStruct(x.shape, BF16)] * 4,
        in_specs=[pl.BlockSpec(memory_space=pltpu.SMEM)] + [pl.BlockSpec(memory_space=VMEM)] * 6,
        out_specs=[pl.BlockSpec(memory_space=VMEM)] * 4,
        scratch_shapes=[VMEM((2, LIVE, pair), BF16), VMEM((2, LIVE, 2 * pair), BF16)],
        compiler_params=pltpu.CompilerParams(vmem_limit_bytes=60 << 20),
        name="attend",
    )(lengths, x, wq, wk, wv, bq, bv)


def attend_back_kernel(lengths, x, dh1, q, k, v, da, wq, wk, wv, cot, skip, gin, gwq, gwk, gwv, gbq, gbv,
                       dq, dk, dv, keys, values, bias, dk_acc, dv_acc):
    rows, width = x.shape
    dim = width // HEADS
    pair = 2 * dim
    chunk = 256
    tops = [(c, min(chunk, -(-LIVE // 128) * 128 - c)) for c in range(0, LIVE, chunk)]
    key_row = lax.broadcasted_iota(jnp.int32, (LIVE, 128), 0)
    bias[...] = jnp.where(key_row < lengths[0], 0.0, NEG_FILL).astype(F32)
    dk[...] = jnp.zeros_like(dk)
    dv[...] = jnp.zeros_like(dv)

    def block(wide, start, size):
        at = pl.ds(start, size)
        q_c, da_c = q[at, wide], da[at, wide]
        dq_c = jnp.zeros((size, pair), F32)
        for head in range(2):
            mine = lanes_of(q_c.shape, head, dim)
            s = dot(keys[head], q_c, NT) + jnp.tile(bias[...], (1, size // 128))
            e = jnp.exp(s - jnp.max(s, 0, keepdims=True))
            p = e * (1.0 / jnp.sum(e, 0, keepdims=True))
            dp = dot(values[head], da_c, NT)
            t = p * dp
            ds = (t - p * jnp.sum(t, 0, keepdims=True)).astype(BF16)
            dv_acc[...] += dot(p.astype(BF16), jnp.where(mine, da_c, jnp.zeros_like(da_c)))
            dk_acc[...] += dot(ds, jnp.where(mine, q_c, jnp.zeros_like(q_c)))
            dq_c = dq_c + dot(ds, keys[head], TN)
        dq[at, wide] = (dq_c * (1.0 / math.sqrt(dim))).astype(BF16)

    @pl.loop(0, width // pair)
    def _(which):
        wide = pl.ds(pl.multiple_of(which * pair, pair), pair)
        whole, whole_v = k[:LIVE, wide], v[:LIVE, wide]
        for head in range(2):
            mine = lanes_of(whole.shape, head, dim)
            keys[head] = jnp.where(mine, whole, jnp.zeros_like(whole))
            values[head] = jnp.where(mine, whole_v, jnp.zeros_like(whole_v))
        dk_acc[...] = jnp.zeros_like(dk_acc)
        dv_acc[...] = jnp.zeros_like(dv_acc)

        @pl.loop(0, LIVE // chunk)
        def _(part):
            block(wide, pl.multiple_of(part * chunk, chunk), chunk)

        for start, size in tops:
            if size < chunk:
                block(wide, start, size)
        dk[:LIVE, wide] = dk_acc[...].astype(BF16)
        dv[:LIVE, wide] = dv_acc[...].astype(BF16)

    gbq[...] = jnp.sum(dq[:LIVE, :].astype(F32), 0, keepdims=True)
    gbv[...] = jnp.sum(dv[:LIVE, :].astype(F32), 0, keepdims=True)
    here = x[:LIVE, :]
    for grad, out in ((dq, gwq), (dk, gwk), (dv, gwv)):
        for start in range(0, width, 256):
            cols = pl.ds(start, 256)
            out[:, cols] = dot(here, grad[:LIVE, cols], TN).astype(BF16)
    step = 160

    @pl.loop(0, LIVE // step)
    def _(part):
        at = pl.ds(pl.multiple_of(part * step, step), step)
        total = dh1[at, :] + dot(dq[at, :], wq[...], NT)
        total = total + dot(dk[at, :], wk[...], NT)
        total = total + dot(dv[at, :], wv[...], NT)
        row = lax.broadcasted_iota(jnp.int32, (step, 1), 0) + part * step
        dropped = jnp.where(row < lengths[0], cot[at, :].astype(F32), 0.0)
        gin[at, :] = jnp.where(skip[0] == 1, dropped, total)

    gin[LIVE:, :] = jnp.zeros((rows - LIVE, width), F32)


def attend_back(lengths, x, dh1, q, k, v, da, wq, wk, wv, cot, skip):
    rows, width = x.shape
    pair = 2 * width // HEADS
    like = jax.ShapeDtypeStruct
    smem = pl.BlockSpec(memory_space=pltpu.SMEM)
    return pl.pallas_call(
        attend_back_kernel,
        out_shape=[like((rows, width), F32)] + [like((width, width), BF16)] * 3 + [like((1, width), F32)] * 2,
        in_specs=[smem] + [pl.BlockSpec(memory_space=VMEM)] * 10 + [smem],
        out_specs=[pl.BlockSpec(memory_space=VMEM)] * 6,
        scratch_shapes=[VMEM(x.shape, BF16)] * 3
        + [VMEM((2, LIVE, pair), BF16)] * 2
        + [VMEM((LIVE, 128), F32)]
        + [VMEM((LIVE, pair), F32)] * 2,
        compiler_params=pltpu.CompilerParams(vmem_limit_bytes=62 << 20),
        name="attend_back",
    )(lengths, x, dh1, q, k, v, da, wq, wk, wv, cot, skip)


def middle_kernel(lengths, skip, x_in, att_in, cot_in, wo_in, wh_in, wp_in, vec, bh,
                  outputs, dh1, da, gwo, gwh, gwp, gvec, gbh,
                  x, att, cot, wo, wh, wp, z1, n1, inv1, f, g, slope, df, z1t, out_h, out_p, load_sem, out_sem):
    rows, width = x.shape
    inner = wh.shape[1]
    loads = [
        pltpu.make_async_copy(a, b, load_sem.at[i])
        for i, (a, b) in enumerate(
            ((x_in, x), (att_in, att), (wo_in, wo), (wh_in, wh), (wp_in, wp), (cot_in, cot))
        )
    ]
    for load in loads:
        load.start()
    bo, gain1, shift1, bp, gain2, shift2 = (vec[i : i + 1, :] for i in range(6))
    for load in loads[:3]:
        load.wait()
    step = 256

    def norm(h):
        centred = h - jnp.mean(h, -1, keepdims=True)
        inv = lax.rsqrt(jnp.mean(centred * centred, -1, keepdims=True) + EPSILON)
        return centred * inv, inv

    def norm_back(e, n, inv):
        return inv * (e - jnp.mean(e, -1, keepdims=True) - n * jnp.mean(e * n, -1, keepdims=True))

    @pl.loop(0, rows // step)
    def _(part):
        at = pl.ds(pl.multiple_of(part * step, step), step)
        h = x[at, :].astype(F32) + (dot(att[at, :], wo[...]) + bo)
        n, inv = norm(h)
        n1[at, :] = n
        inv1[at, :] = jnp.broadcast_to(inv, (step, 128))
        z1[at, :] = (n * gain1 + shift1).astype(BF16)

    loads[3].wait()
    loads[4].wait()
    f[...] = jnp.zeros_like(f)
    wide = 256

    @pl.loop(0, inner // wide)
    def _(block):
        cols = pl.ds(pl.multiple_of(block * wide, wide), wide)
        b = bh[:, cols]
        for start in range(0, rows, step):
            at = pl.ds(start, step)
            u = dot(z1[at, :], wh[:, cols]) + b
            phi = 0.5 * (1.0 + lax.erf(u * 0.7071067811865476))
            g[at, cols] = (u * phi).astype(BF16)
            slope[at, cols] = (phi + u * (jnp.exp(-0.5 * u * u) * 0.3989422804014327)).astype(BF16)
            f[at, :] += dot(g[at, cols], wp[cols, :])

    loads[5].wait()
    gvec[...] = jnp.zeros_like(gvec)
    keep = 1.0 - skip[0].astype(F32)

    @pl.loop(0, rows // step)
    def _(part):
        at = pl.ds(pl.multiple_of(part * step, step), step)
        n, inv = norm(z1[at, :].astype(F32) + (f[at, :] + bp))
        outputs[at, :] = jnp.where(skip[0] == 1, x[at, :], (n * gain2 + shift2).astype(BF16))
        row = lax.broadcasted_iota(jnp.int32, (step, 1), 0) + part * step
        dy = jnp.where(row < lengths[0], cot[at, :].astype(F32), 0.0) * keep
        d = norm_back(dy * gain2, n, inv)
        low = d.astype(BF16)
        f[at, :] = d
        df[at, :] = low
        gvec[3:4, :] += jnp.sum(low.astype(F32), 0, keepdims=True)
        gvec[4:5, :] += jnp.sum(dy * n, 0, keepdims=True)
        gvec[5:6, :] += jnp.sum(dy, 0, keepdims=True)

    z1t[...] = z1[:LIVE, :].T

    def flush(block, buf, slot):
        cols = pl.ds(pl.multiple_of(block * wide, wide), wide)
        if buf is out_h:
            return pltpu.make_async_copy(buf.at[slot], gwh.at[:, cols], out_sem.at[0, slot])
        return pltpu.make_async_copy(buf.at[slot], gwp.at[cols, :], out_sem.at[1, slot])

    @pl.loop(0, inner // wide)
    def _(block):
        slot = lax.rem(block, 2)
        cols = pl.ds(pl.multiple_of(block * wide, wide), wide)

        @pl.when(block >= 2)
        def _():
            flush(block, out_h, slot).wait()
            flush(block, out_p, slot).wait()

        out_p[slot] = dot(g[:LIVE, cols], df[:LIVE, :], TN).astype(BF16)
        flush(block, out_p, slot).start()
        total = jnp.zeros((1, wide), F32)
        half = LIVE // 2
        for start in range(0, LIVE, half):
            at = pl.ds(start, half)
            du = (dot(df[at, :], wp[cols, :], NT) * slope[at, cols].astype(F32)).astype(BF16)
            total = total + jnp.sum(du.astype(F32), 0, keepdims=True)
            g[at, cols] = du
            f[at, :] += dot(du, wh[:, cols], NT)
        gbh[:, cols] = total
        out_h[slot] = dot(z1t[...], g[:LIVE, cols]).astype(BF16)
        flush(block, out_h, slot).start()

    half = LIVE // 5
    @pl.loop(0, LIVE // half)
    def _(part):
        at = pl.ds(pl.multiple_of(part * half, half), half)
        dz = f[at, :]
        n = n1[at, :]
        gvec[1:2, :] += jnp.sum(dz * n, 0, keepdims=True)
        gvec[2:3, :] += jnp.sum(dz, 0, keepdims=True)
        d = norm_back(dz * gain1, n, inv1[at, :1])
        dh1[at, :] = d
        low = d.astype(BF16)
        df[at, :] = low
        gvec[0:1, :] += jnp.sum(low.astype(F32), 0, keepdims=True)
        da[at, :] = dot(low, wo[...], NT).astype(BF16)

    da[LIVE:, :] = jnp.zeros((rows - LIVE, width), BF16)
    for start in range(0, width, wide):
        cols = pl.ds(start, wide)
        gwo[cols, :] = dot(att[:LIVE, cols], df[:LIVE, :], TN).astype(BF16)
    for block in (inner // wide - 2, inner // wide - 1):
        flush(block, out_h, block % 2).wait()
        flush(block, out_p, block % 2).wait()


def middle(lengths, skip, x, att, cot, wo, wh, wp, vec, bh):
    rows, width = x.shape
    inner = wh.shape[1]
    like = jax.ShapeDtypeStruct
    smem, vmem, any_ = (pl.BlockSpec(memory_space=m) for m in (pltpu.SMEM, VMEM, pl.ANY))
    pad = -(-LIVE // 128) * 128
    return pl.pallas_call(
        middle_kernel,
        out_shape=[
            like((rows, width), BF16), like((LIVE, width), F32), like((rows, width), BF16),
            like((width, width), BF16), like((width, inner), BF16), like((inner, width), BF16),
            like((8, width), F32), like((1, inner), F32),
        ],
        in_specs=[smem] * 2 + [any_] * 6 + [vmem] * 2,
        out_specs=[vmem] * 4 + [any_] * 2 + [vmem] * 2,
        scratch_shapes=[
            VMEM((rows, width), BF16), VMEM((rows, width), BF16), VMEM((rows, width), BF16),
            VMEM((width, width), BF16), VMEM((width, inner), BF16), VMEM((inner, width), BF16),
            VMEM((rows, width), BF16), VMEM((rows, width), F32), VMEM((rows, 128), F32),
            VMEM((rows, width), F32), VMEM((rows, inner), BF16), VMEM((rows, inner), BF16),
            VMEM((rows, width), BF16), VMEM((width, LIVE), BF16),
            VMEM((2, width, 256), BF16), VMEM((2, 256, width), BF16),
            pltpu.SemaphoreType.DMA((6,)), pltpu.SemaphoreType.DMA((2, 2)),
        ],
        compiler_params=pltpu.CompilerParams(vmem_limit_bytes=63 << 20),
        name="middle",
    )(lengths, skip, x, att, cot, wo, wh, wp, vec, bh)


def as_float(value):
    return value.astype(jnp.float32)


MESH = pl.DeviceIdType.MESH


def place(me, planes):
    core = lax.rem(me, 2)
    chip = me // 2
    col = lax.rem(chip, 2)
    row = lax.rem(chip // 2, 2)
    plane = chip // 4
    near = jnp.where(core == 0, row, col)
    far = jnp.where(core == 0, col, row)

    def index(plane_, near_, far_, core_):
        row_ = jnp.where(core_ == 0, near_, far_)
        col_ = jnp.where(core_ == 0, far_, near_)
        return ((plane_ * 2 + row_) * 2 + col_) * 2 + core_

    return core, near, far, plane, index


def greet(peers):
    barrier = pltpu.get_barrier_semaphore()
    for peer in peers:
        pl.semaphore_signal(barrier, inc=1, device_id=(peer,), device_id_type=MESH)
    pl.semaphore_wait(barrier, len(peers))


def scatter_kernel(shapes, planes, *refs):
    count = len(shapes)
    half = planes * 4
    refs = list(refs)

    def take(n):
        out = refs[:n]
        del refs[:n]
        return out

    part = take(count)
    result = take(count)
    mine, got0, got1, got2, got3, final = (take(count) for _ in range(6))
    send_sem, recv_sem, load_sem = refs
    me = lax.axis_index("fsdp")
    core, near, far, plane, index = place(me, planes)
    other = index(plane, far, near, 1 - core)
    near_peer = index(plane, 1 - near, far, core)
    far_peer = index(plane, near, 1 - far, core)
    others = [lax.rem(plane + step, planes) for step in range(1, planes)]
    plane_peers = [index(p, near, far, core) for p in others]
    greet([other, near_peer, far_peer, *plane_peers])
    pending = []

    def push(src, dst, send, recv, peer):
        copy = pltpu.make_async_remote_copy(
            src_ref=src, dst_ref=dst, send_sem=send, recv_sem=recv,
            device_id=(peer,), device_id_type=MESH,
        )
        copy.start()
        pending.append(copy)

    def slot_of(far_step, near_step, p):
        return (1 - far_step) * 2 * planes + (1 - near_step) * planes + p

    loads = []
    for which in range(count):
        for far_step in (1, 0):
            for near_step in (1, 0):
                for p in range(planes):
                    slot = slot_of(far_step, near_step, p)
                    chunk = index(
                        p,
                        jnp.where(near_step == 1, 1 - far, far),
                        jnp.where(far_step == 1, 1 - near, near),
                        1 - core,
                    )
                    push(
                        part[which].at[chunk],
                        got0[which].at[slot],
                        send_sem.at[which, slot],
                        recv_sem.at[which, slot],
                        other,
                    )
                    own = index(
                        p,
                        jnp.where(near_step == 1, 1 - near, near),
                        jnp.where(far_step == 1, 1 - far, far),
                        core,
                    )
                    load = pltpu.make_async_copy(
                        part[which].at[own], mine[which].at[slot], load_sem.at[which, slot]
                    )
                    load.start()
                    loads.append(load)

    def landed(ref, sem):
        pltpu.make_async_copy(ref, ref, sem).wait()

    def add(which, first, number, extra):
        @pl.loop(0, number)
        def _(step):
            total = mine[which][first + step].astype(jnp.float32)
            for ref, start in extra:
                total = total + ref[start + step].astype(jnp.float32)
            mine[which][first + step] = total.astype(mine[which].dtype)

    for which in range(count):
        for slot in range(half // 2):
            loads[which * half + slot].wait()
            landed(got0[which].at[slot], recv_sem.at[which, slot])
        add(which, 0, half // 2, [(got0[which], 0)])
        push(
            mine[which].at[pl.ds(0, half // 2)], got1[which],
            send_sem.at[which, half], recv_sem.at[which, half], far_peer,
        )
    for which in range(count):
        for slot in range(half // 2, half):
            loads[which * half + slot].wait()
            landed(got0[which].at[slot], recv_sem.at[which, slot])
        landed(got1[which], recv_sem.at[which, half])
        add(which, half // 2, planes, [(got0[which], half // 2), (got1[which], 0)])
        push(
            mine[which].at[pl.ds(half // 2, planes)], got2[which],
            send_sem.at[which, half + 1], recv_sem.at[which, half + 1], near_peer,
        )
    last = half - planes
    for which in range(count):
        landed(got2[which], recv_sem.at[which, half + 1])
        spread = jnp.float32
        here = (
            mine[which][last + plane].astype(spread)
            + got0[which][last + plane].astype(spread)
            + got1[which][planes + plane].astype(spread)
            + got2[which][plane].astype(spread)
        )
        final[which][...] = here
        for step, p in enumerate(others):
            total = (
                mine[which][last + p].astype(spread)
                + got0[which][last + p].astype(spread)
                + got1[which][planes + p].astype(spread)
                + got2[which][p].astype(spread)
            )
            mine[which][last + p] = total.astype(mine[which].dtype)
            push(
                mine[which].at[last + p], got3[which].at[step],
                send_sem.at[which, half + 2 + step], recv_sem.at[which, half + 2 + step],
                plane_peers[step],
            )
    outs = []
    for which in range(count):
        total = final[which][...]
        for step in range(planes - 1):
            landed(got3[which].at[step], recv_sem.at[which, half + 2 + step])
            total = total + got3[which][step].astype(jnp.float32)
        final[which][...] = total
        copy = pltpu.make_async_copy(final[which], result[which], load_sem.at[which, half])
        copy.start()
        outs.append(copy)
    for copy in outs:
        copy.wait()
    for copy in pending:
        copy.wait_send()


def scatter(arrays, size):
    planes = size // 8
    half = size // 2
    count = len(arrays)
    shapes = [a.shape[1:] for a in arrays]
    vmem = lambda lead: [pltpu.VMEM((*lead, *a.shape[1:]), a.dtype) for a in arrays]
    return pl.pallas_call(
        functools.partial(scatter_kernel, shapes, planes),
        out_shape=[jax.ShapeDtypeStruct(s, jnp.float32) for s in shapes],
        in_specs=[pl.BlockSpec(memory_space=pl.ANY)] * count,
        out_specs=[pl.BlockSpec(memory_space=pl.ANY)] * count,
        scratch_shapes=[
            *vmem((half,)), *vmem((half,)), *vmem((half // 2,)), *vmem((planes,)), *vmem((planes - 1,)),
            *[pltpu.VMEM(s, jnp.float32) for s in shapes],
            pltpu.SemaphoreType.DMA((count, half + 1 + planes)),
            pltpu.SemaphoreType.DMA((count, half + 1 + planes)),
            pltpu.SemaphoreType.DMA((count, half + 1)),
        ],
        compiler_params=pltpu.CompilerParams(
            collective_id=1, has_side_effects=True, vmem_limit_bytes=60 << 20
        ),
        name="scatter",
    )(*arrays)


class Gather:
    def __init__(self, groups, planes, send_sem, recv_sem, local_sem):
        self.groups = groups
        self.planes = planes
        self.sems = send_sem, recv_sem, local_sem
        self.me = lax.axis_index("fsdp")
        self.core, self.near, self.far, self.plane, self.index = place(self.me, planes)
        self.other = self.index(self.plane, self.far, self.near, 1 - self.core)
        self.near_peer = self.index(self.plane, 1 - self.near, self.far, self.core)
        self.far_peer = self.index(self.plane, self.near, 1 - self.far, self.core)
        self.others = [lax.rem(self.plane + step, planes) for step in range(1, planes)]
        self.plane_peers = [self.index(p, self.near, self.far, self.core) for p in self.others]
        self.number = {}
        for group in groups:
            for item in group:
                self.number[id(item)] = len(self.number)
        self.sent = {key: 0 for key in self.number}
        greet([self.other, self.near_peer, self.far_peer, *self.plane_peers])

    def spot(self, item, chunk):
        own, full, cols = item
        if cols is None:
            return full.at[chunk]
        rows = own.shape[0]
        return full.at[pl.ds(pl.multiple_of(chunk * rows, 8), rows), cols]

    def push(self, item, chunk, peer, src=None):
        n = self.number[id(item)]
        where = self.spot(item, chunk)
        copy = pltpu.make_async_remote_copy(
            src_ref=where if src is None else src,
            dst_ref=where,
            send_sem=self.sems[0].at[n, self.sent[id(item)]],
            recv_sem=self.sems[1].at[n, chunk],
            device_id=(peer,),
            device_id_type=MESH,
        )
        copy.start()
        self.sent[id(item)] += 1

    def arrive(self, item, chunk):
        n = self.number[id(item)]
        where = self.spot(item, chunk)
        pltpu.make_async_copy(where, where, self.sems[1].at[n, chunk]).wait()

    def stage(self, which, g):
        for item in self.groups[g]:
            if which == 1:
                own, full, cols = item
                src = own if cols is None else own.at[:, cols]
                for peer in [*self.plane_peers, self.near_peer, self.far_peer, self.other]:
                    self.push(item, self.me, peer, src)
                copy = pltpu.make_async_copy(
                    src, self.spot(item, self.me), self.sems[2].at[self.number[id(item)]]
                )
                copy.start()
            elif which == 2:
                for p in self.others:
                    chunk = self.index(p, self.near, self.far, self.core)
                    self.arrive(item, chunk)
                    for peer in (self.near_peer, self.far_peer, self.other):
                        self.push(item, chunk, peer)
            elif which == 3:
                for p in [self.plane, *self.others]:
                    chunk = self.index(p, 1 - self.near, self.far, self.core)
                    self.arrive(item, chunk)
                    for peer in (self.far_peer, self.other):
                        self.push(item, chunk, peer)
            elif which == 4:
                for near in (self.near, 1 - self.near):
                    for p in [self.plane, *self.others]:
                        chunk = self.index(p, near, 1 - self.far, self.core)
                        self.arrive(item, chunk)
                        self.push(item, chunk, self.other)
            else:
                for chip in range(4 * self.planes):
                    self.arrive(item, chip * 2 + 1 - self.core)
                where = self.spot(item, self.me)
                pltpu.make_async_copy(where, where, self.sems[2].at[self.number[id(item)]]).wait()

    def finish(self):
        for group in self.groups:
            for item in group:
                n = self.number[id(item)]
                where = self.spot(item, self.me)
                for k in range(self.sent[id(item)]):
                    pltpu.make_async_copy(where, where, self.sems[0].at[n, k]).wait()


def unpack(packed, vec, bh, size):
    width, inner = vec.shape[1], bh.shape[1]
    piece, long = width // size, inner // size
    flat = jnp.concatenate([packed[:, j, :] for j in range(packed.shape[1])], 1).astype(BF16)

    def pick(first, part, total):
        lane = lax.rem(lax.broadcasted_iota(jnp.int32, (flat.shape[1], total), 1), part)
        entry = lax.broadcasted_iota(jnp.int32, (flat.shape[1], total), 0)
        spread = dot(flat, jnp.where(entry == lane + first, 1.0, 0.0).astype(BF16))
        lane = lax.broadcasted_iota(jnp.int32, (size, total), 1)
        owner = lax.broadcasted_iota(jnp.int32, (size, total), 0)
        return jnp.sum(jnp.where(lane - lax.rem(lane, part) == part * owner, spread, 0.0), 0, keepdims=True)

    for k in range(8):
        vec[k : k + 1, :] = pick(k * piece, piece, width)
    for start in range(0, inner, width):
        lane = lax.rem(lax.broadcasted_iota(jnp.int32, (flat.shape[1], width), 1), long)
        entry = lax.broadcasted_iota(jnp.int32, (flat.shape[1], width), 0)
        spread = dot(flat, jnp.where(entry == lane + 8 * piece, 1.0, 0.0).astype(BF16))
        lane = lax.broadcasted_iota(jnp.int32, (size, width), 1) + start
        owner = lax.broadcasted_iota(jnp.int32, (size, width), 0)
        bh[:, start : start + width] = jnp.sum(
            jnp.where(lane - lax.rem(lane, long) == long * owner, spread, 0.0), 0, keepdims=True
        )


def norm(h):
    centred = h - jnp.mean(h, -1, keepdims=True)
    inv = lax.rsqrt(jnp.mean(centred * centred, -1, keepdims=True) + EPSILON)
    return centred * inv, inv


def norm_back(e, n, inv):
    return inv * (e - jnp.mean(e, -1, keepdims=True) - n * jnp.mean(e * n, -1, keepdims=True))


def front_kernel(size, lengths, skip, x_in, cot_in, *refs):
    refs = list(refs)

    def take(n):
        out = refs[:n]
        del refs[:n]
        return out

    own = take(7)
    saved = take(18)
    (x, cot, q, k, v, att, z1, n1, inv1, g, slope, f, outputs, df, gvec) = take(15)
    full = take(7)
    vec, bh, keys, values, send_sem, recv_sem, local_sem, load_sem, save_sem = refs
    wq, wk, wv, wo, wh, wp, packed = full
    rows, width = x.shape
    inner = wh.shape[1]
    dim = width // HEADS
    pair = 2 * dim
    group = 2 * pair
    step = 256
    parts = rows // step
    loads = [pltpu.make_async_copy(a, b, load_sem.at[i]) for i, (a, b) in enumerate(((x_in, x), (cot_in, cot)))]
    for load in loads:
        load.start()

    def item(which, start=None, number=None):
        return own[which], full[which], None if start is None else pl.ds(start, number)

    groups = [[item(w, c, group) for w in range(3)] for c in range(0, width, group)]
    groups[0].insert(0, item(6))
    groups.append([item(3, 0, width)])
    groups += [[item(4, c, inner // 2)] for c in (0, inner // 2)]
    groups += [[item(5, c, n)] for c, n in ((0, 2 * group), (2 * group, width - 2 * group))]
    move = Gather(groups, size // 8, send_sem, recv_sem, local_sem)

    def moves(text):
        for word in text.split():
            move.stage(int(word[0]), int(word[1]))

    saves = []

    def save(src, index):
        copy = pltpu.make_async_copy(src, saved[index], save_sem.at[index])
        copy.start()
        saves.append(copy)

    moves("10 11 12 20 13 30 21 14 40 31 22 15 16 17 50")
    unpack(packed, vec, bh, size)
    bq, bv, bo, gain1, shift1, bp, gain2, shift2 = (vec[i : i + 1, :] for i in range(8))
    loads[0].wait()
    key_lane = lax.broadcasted_iota(jnp.int32, (1, LIVE), 1)
    bias = jnp.where(key_lane < lengths[0], 0.0, NEG_FILL).astype(F32)
    for head in range(2):
        values[head, :, pair:] = jnp.ones((LIVE, pair), BF16)

    ticks = iter(
        ["41 32", "23", "51", "42 33", "52 24", "43", "34 53", "25", "35", "44", "54 26", "36"]
    )
    for number, first in enumerate(range(0, width, group)):
        cols = pl.ds(first, group)

        @pl.loop(0, parts)
        def _(part):
            at = pl.ds(pl.multiple_of(part * step, step), step)
            here = x[at, :]
            query = (dot(here, wq[:, cols]) + bq[:, first : first + group]).astype(BF16)
            q[at, cols] = (query.astype(F32) * (1.0 / math.sqrt(dim))).astype(BF16)
            k[at, cols] = dot(here, wk[:, cols]).astype(BF16)
            v[at, cols] = (dot(here, wv[:, cols]) + bv[:, first : first + group]).astype(BF16)

        for start in range(first, first + group, pair):
            wide = pl.ds(start, pair)
            whole = k[:LIVE, wide]
            for head in range(2):
                keys[head] = jnp.where(lanes_of(whole.shape, head, dim), whole, jnp.zeros_like(whole))
                values[head, :, :pair] = v[:LIVE, wide]
            now = [next(ticks), next(ticks)]

            @pl.loop(0, parts)
            def _(part):
                at = pl.ds(pl.multiple_of(part * step, step), step)
                here = q[at, wide]
                outs = []
                for head in range(2):
                    s = dot(here, keys[head], NT) + bias
                    e = jnp.exp(s - jnp.max(s, -1, keepdims=True))
                    o = dot(e.astype(BF16), values[head])
                    outs.append(o[:, :pair] / o[:, pair:])
                att[at, wide] = jnp.where(lanes_of(outs[0].shape, 0, dim), outs[0], outs[1]).astype(BF16)
                for turn, text in enumerate(now):

                    @pl.when(part == 2 * turn + 1)
                    def _():
                        moves(text)

    save(q, 0)
    save(k, 1)
    save(v, 2)
    save(att, 3)
    for n, w in enumerate((wq, wk, wv, wo)):
        save(w, 12 + n)

    @pl.loop(0, parts)
    def _(part):
        at = pl.ds(pl.multiple_of(part * step, step), step)
        h = x[at, :].astype(F32) + (dot(att[at, :], wo[...]) + bo)
        n, inv = norm(h)
        n1[at, :] = n
        inv1[at, :] = jnp.broadcast_to(inv, (step, 128))
        z1[at, :] = (n * gain1 + shift1).astype(BF16)

    save(z1, 4)
    save(n1.at[pl.ds(0, LIVE)], 5)
    save(inv1.at[pl.ds(0, LIVE)], 6)
    moves("45 27")
    later = {2: "55 37", 6: "46"}

    @pl.loop(0, inner // step)
    def _(block):
        cols = pl.ds(pl.multiple_of(block * step, step), step)
        b = bh[:, cols]
        for start in range(0, rows, step):
            at = pl.ds(start, step)
            u = dot(z1[at, :], wh[:, cols]) + b
            phi = 0.5 * (1.0 + lax.erf(u * 0.7071067811865476))
            g[at, cols] = (u * phi).astype(BF16)
            if start < LIVE:
                slope[at, cols] = (phi + u * (jnp.exp(-0.5 * u * u) * 0.3989422804014327)).astype(BF16)
        for turn, text in later.items():

            @pl.when(block == turn)
            def _():
                moves(text)

    save(g.at[pl.ds(0, LIVE)], 7)
    save(slope.at[pl.ds(0, LIVE)], 8)
    save(wh, 16)
    moves("56 47")
    for turn, (first, many) in enumerate(((0, 2 * group), (2 * group, width - 2 * group))):
        if turn:
            moves("57")
        cols = pl.ds(first, many)

        @pl.loop(0, parts)
        def _(part):
            at = pl.ds(pl.multiple_of(part * step, step), step)
            f[at, cols] = dot(g[at, :], wp[:, cols])

    save(wp, 17)
    loads[1].wait()
    gvec[...] = jnp.zeros_like(gvec)
    keep = 1.0 - skip[0].astype(F32)

    @pl.loop(0, parts)
    def _(part):
        at = pl.ds(pl.multiple_of(part * step, step), step)
        n, inv = norm(z1[at, :].astype(F32) + (f[at, :] + bp))
        outputs[at, :] = jnp.where(skip[0] == 1, x[at, :], (n * gain2 + shift2).astype(BF16))
        row = lax.broadcasted_iota(jnp.int32, (step, 1), 0) + part * step
        dy = jnp.where(row < lengths[0], cot[at, :].astype(F32), 0.0) * keep
        d = norm_back(dy * gain2, n, inv)
        low = d.astype(BF16)
        f[at, :] = d
        df[at, :] = low
        gvec[5:6, :] += jnp.sum(low.astype(F32), 0, keepdims=True)
        gvec[6:7, :] += jnp.sum(dy * n, 0, keepdims=True)
        gvec[7:8, :] += jnp.sum(dy, 0, keepdims=True)

    save(f.at[pl.ds(0, LIVE)], 9)
    save(df.at[pl.ds(0, LIVE)], 10)
    save(outputs, 11)
    for copy in saves:
        copy.wait()
    move.finish()


def front(size, lengths, skip, x, cot, weights, packed):
    rows, width = x.shape
    inner = weights[4].shape[1]
    like = jax.ShapeDtypeStruct
    smem, vmem, any_ = (pl.BlockSpec(memory_space=m) for m in (pltpu.SMEM, VMEM, pl.ANY))
    act = like((rows, width), BF16)
    outs = [
        act, act, act, act, act,
        like((LIVE, width), F32), like((LIVE, 128), F32),
        like((LIVE, inner), BF16), like((LIVE, inner), BF16),
        like((LIVE, width), F32), like((LIVE, width), BF16), act,
        *[like((width, width), BF16)] * 4, like((width, inner), BF16), like((inner, width), BF16),
    ]
    groups_items = 3 * 3 + 1 + 1 + 2 + 2
    pair = 2 * width // HEADS
    scratch = [
        VMEM((rows, width), BF16), VMEM((rows, width), BF16),
        *[VMEM((rows, width), BF16)] * 5,
        VMEM((rows, width), F32), VMEM((rows, 128), F32),
        VMEM((rows, inner), BF16), VMEM((rows, inner), BF16),
        VMEM((rows, width), F32), VMEM((rows, width), BF16), VMEM((rows, width), BF16),
    ]
    weights_full = [*[VMEM((width, width), BF16)] * 4, VMEM((width, inner), BF16), VMEM((inner, width), BF16),
                    VMEM((size, *packed.shape), F32)]
    planes = size // 8
    sends = (planes + 2) + (planes - 1) * 3 + planes * 2 + planes * 2
    return pl.pallas_call(
        functools.partial(front_wrap, size),
        out_shape=[*outs, like((8, width), F32), like((8, width), F32)],
        in_specs=[smem, smem] + [any_] * 9,
        out_specs=[any_] * 18 + [vmem] * 2,
        scratch_shapes=[
            *scratch, *weights_full, VMEM((1, inner), F32),
            VMEM((2, LIVE, pair), BF16), VMEM((2, LIVE, 2 * pair), BF16),
            pltpu.SemaphoreType.DMA((groups_items, sends)),
            pltpu.SemaphoreType.DMA((groups_items, size)),
            pltpu.SemaphoreType.DMA((groups_items,)),
            pltpu.SemaphoreType.DMA((2,)),
            pltpu.SemaphoreType.DMA((18,)),
        ],
        compiler_params=pltpu.CompilerParams(collective_id=0, has_side_effects=True, vmem_limit_bytes=64 << 20),
        name="front",
    )(lengths, skip, x, cot, *weights, packed)


def front_wrap(size, lengths, skip, x_in, cot_in, *refs):
    own, saved, vec, gvec, scratch = refs[:7], refs[7:25], refs[25], refs[26], refs[27:]
    body, full, rest = scratch[:14], scratch[14:21], scratch[21:]
    front_kernel(size, lengths, skip, x_in, cot_in, *own, *saved, *body, gvec, *full, vec, *rest)


def rest_kernel(z1, g_in, slope, f_in, df_in, n1, inv1, att, wo, wh, wp, vec,
                dh1, da, gwo, gwh, gwp, gvec, gbh, g, f, df, z1t, out_h, out_p, out_sem):
    rows, width = att.shape
    inner = wh.shape[1]
    wide = 256
    gain1 = vec[3:4, :]
    g[...] = g_in[...]
    f[...] = f_in[...]
    df[...] = df_in[...]
    gvec[...] = jnp.zeros_like(gvec)
    z1t[...] = z1[:LIVE, :].T

    def flush(block, buf, slot):
        cols = pl.ds(pl.multiple_of(block * wide, wide), wide)
        if buf is out_h:
            return pltpu.make_async_copy(buf.at[slot], gwh.at[:, cols], out_sem.at[0, slot])
        return pltpu.make_async_copy(buf.at[slot], gwp.at[cols, :], out_sem.at[1, slot])

    @pl.loop(0, inner // wide)
    def _(block):
        slot = lax.rem(block, 2)
        cols = pl.ds(pl.multiple_of(block * wide, wide), wide)

        @pl.when(block >= 2)
        def _():
            flush(block, out_h, slot).wait()
            flush(block, out_p, slot).wait()

        out_p[slot] = dot(g[:LIVE, cols], df[:LIVE, :], TN).astype(BF16)
        flush(block, out_p, slot).start()
        total = jnp.zeros((1, wide), F32)
        half = LIVE // 2
        for start in range(0, LIVE, half):
            at = pl.ds(start, half)
            du = (dot(df[at, :], wp[cols, :], NT) * slope[at, cols].astype(F32)).astype(BF16)
            total = total + jnp.sum(du.astype(F32), 0, keepdims=True)
            g[at, cols] = du
            f[at, :] += dot(du, wh[:, cols], NT)
        gbh[:, cols] = total
        out_h[slot] = dot(z1t[...], g[:LIVE, cols]).astype(BF16)
        flush(block, out_h, slot).start()

    half = LIVE // 5
    @pl.loop(0, LIVE // half)
    def _(part):
        at = pl.ds(pl.multiple_of(part * half, half), half)
        dz = f[at, :]
        n = n1[at, :]
        gvec[3:4, :] += jnp.sum(dz * n, 0, keepdims=True)
        gvec[4:5, :] += jnp.sum(dz, 0, keepdims=True)
        d = norm_back(dz * gain1, n, inv1[at, :1])
        dh1[at, :] = d
        low = d.astype(BF16)
        df[at, :] = low
        gvec[2:3, :] += jnp.sum(low.astype(F32), 0, keepdims=True)
        da[at, :] = dot(low, wo[...], NT).astype(BF16)

    da[LIVE:, :] = jnp.zeros((rows - LIVE, width), BF16)
    for start in range(0, width, wide):
        cols = pl.ds(start, wide)
        gwo[cols, :] = dot(att[:LIVE, cols], df[:LIVE, :], TN).astype(BF16)
    for block in (inner // wide - 2, inner // wide - 1):
        flush(block, out_h, block % 2).wait()
        flush(block, out_p, block % 2).wait()


def rest(z1, g, slope, dh2, df, n1, inv1, att, wo, wh, wp, vec):
    rows, width = att.shape
    inner = wh.shape[1]
    like = jax.ShapeDtypeStruct
    vmem, any_ = (pl.BlockSpec(memory_space=m) for m in (VMEM, pl.ANY))
    return pl.pallas_call(
        rest_kernel,
        out_shape=[
            like((LIVE, width), F32), like((rows, width), BF16),
            like((width, width), BF16), like((width, inner), BF16), like((inner, width), BF16),
            like((8, width), F32), like((1, inner), F32),
        ],
        in_specs=[vmem] * 12,
        out_specs=[vmem] * 3 + [any_] * 2 + [vmem] * 2,
        scratch_shapes=[
            VMEM((LIVE, inner), BF16), VMEM((LIVE, width), F32), VMEM((LIVE, width), BF16),
            VMEM((width, LIVE), BF16),
            VMEM((2, width, 256), BF16), VMEM((2, 256, width), BF16), pltpu.SemaphoreType.DMA((2, 2)),
        ],
        compiler_params=pltpu.CompilerParams(vmem_limit_bytes=63 << 20),
        name="rest",
    )(z1, g, slope, dh2, df, n1, inv1, att, wo, wh, wp, vec)


def share(grads, size):
    matrices, vectors = grads[:6], grads[6:]
    low = [g.astype(jnp.bfloat16).reshape(size, g.shape[0] // size, g.shape[1]) for g in matrices]
    cut = [v.reshape(size, -1) for v in vectors]
    packed = jnp.stack([jnp.pad(v, ((0, 0), (0, 128 - v.shape[1]))) for v in cut], 1)
    packed = jnp.pad(packed, ((0, 0), (0, 16 - packed.shape[1]), (0, 0)))
    *out, small = scatter([*low, packed], size)
    return list(out) + [small[k, : v.shape[1]] for k, v in enumerate(cut)]


def local(
    size,
    inputs,
    cotangent,
    lengths,
    skip_bit,
    w_query,
    w_key,
    w_value,
    w_out,
    b_query,
    b_value,
    b_out,
    ln1_gain,
    ln1_bias,
    w_hidden,
    b_hidden,
    w_proj,
    b_proj,
    ln2_gain,
    ln2_bias,
):
    vectors = [b_query, b_value, b_out, ln1_gain, ln1_bias, b_proj, ln2_gain, ln2_bias, b_hidden]
    weights = [w_query, w_key, w_value, w_out, w_hidden, w_proj]
    flat = jnp.concatenate([as_float(v_) for v_ in vectors])
    lines = -(-flat.shape[0] // 128)
    packed = jnp.pad(flat, (0, lines * 128 - flat.shape[0])).reshape(lines, 128)
    (
        q, k, v, att, z1, n1, inv1, g, slope, dh2, df, outputs,
        query_full, key_full, value_full, out_full, hidden_full, proj_full, vec, gtop,
    ) = front(size, lengths, skip_bit, inputs, cotangent, weights, packed)
    dh1, da, d_weight_out, d_weight_hidden, d_weight_proj, gvec, gbh = rest(
        z1, g, slope, dh2, df, n1, inv1, att, out_full, hidden_full, proj_full, vec
    )
    gvec = gvec + gtop
    grad_inputs, d_weight_query, d_weight_key, d_weight_value, gbq, gbv = attend_back(
        lengths, inputs, dh1, q, k, v, da, query_full, key_full, value_full, cotangent, skip_bit
    )
    (
        g_w_query, g_w_key, g_w_value, g_w_out, g_w_hidden, g_w_proj,
        g_b_query, g_b_value, g_b_out, g_ln1_gain, g_ln1_bias,
        g_b_hidden, g_b_proj, g_ln2_gain, g_ln2_bias,
    ) = share(
        [
            d_weight_query, d_weight_key, d_weight_value, d_weight_out, d_weight_hidden, d_weight_proj,
            gbq[0], gbv[0], gvec[2], gvec[3], gvec[4], gbh[0], gvec[5], gvec[6], gvec[7],
        ],
        size,
    )
    return (
        outputs,
        grad_inputs,
        g_w_query,
        g_w_key,
        g_w_value,
        g_w_out,
        g_b_query,
        g_b_value,
        g_b_out,
        g_ln1_gain,
        g_ln1_bias,
        g_w_hidden,
        g_b_hidden,
        g_w_proj,
        g_b_proj,
        g_ln2_gain,
        g_ln2_bias,
    )


def local_plain(
    inputs,
    cotangent,
    lengths,
    skip_bit,
    w_query,
    w_key,
    w_value,
    w_out,
    b_query,
    b_value,
    b_out,
    ln1_gain,
    ln1_bias,
    w_hidden,
    b_hidden,
    w_proj,
    b_proj,
    ln2_gain,
    ln2_bias,
):
    (
        query_full, key_full, value_full, out_full, hidden_full, proj_full,
        bq_full, bv_full, bo_full, gain_one, shift_one, bh_full, bp_full, gain_two, shift_two,
    ) = [
        lax.all_gather(p, "fsdp", axis=0, tiled=True)
        for p in (
            w_query, w_key, w_value, w_out, w_hidden, w_proj,
            b_query, b_value, b_out, ln1_gain, ln1_bias, b_hidden, b_proj, ln2_gain, ln2_bias,
        )
    ]
    row = lambda v: as_float(v)[None, :]
    q, k, v, att = attend(
        lengths, inputs, query_full, key_full, value_full, row(bq_full), row(bv_full)
    )
    vec = jnp.stack([as_float(v_) for v_ in (bo_full, gain_one, shift_one, bp_full, gain_two, shift_two)])
    vec = jnp.pad(vec, ((0, 2), (0, 0)))
    outputs, dh1, da, d_weight_out, d_weight_hidden, d_weight_proj, gvec, gbh = middle(
        lengths, skip_bit, inputs, att, cotangent, out_full, hidden_full, proj_full, vec, row(bh_full)
    )
    grad_inputs, d_weight_query, d_weight_key, d_weight_value, gbq, gbv = attend_back(
        lengths, inputs, dh1, q, k, v, da, query_full, key_full, value_full, cotangent, skip_bit
    )
    (
        g_w_query, g_w_key, g_w_value, g_w_out, g_w_hidden, g_w_proj,
        g_b_query, g_b_value, g_b_out, g_ln1_gain, g_ln1_bias,
        g_b_hidden, g_b_proj, g_ln2_gain, g_ln2_bias,
    ) = [
        lax.psum_scatter(lax.optimization_barrier(as_float(grad)), "fsdp", scatter_dimension=0, tiled=True)
        for grad in (
            d_weight_query, d_weight_key, d_weight_value, d_weight_out, d_weight_hidden, d_weight_proj,
            gbq[0], gbv[0], gvec[0], gvec[1], gvec[2], gbh[0], gvec[3], gvec[4], gvec[5],
        )
    ]
    return (
        outputs,
        grad_inputs,
        g_w_query,
        g_w_key,
        g_w_value,
        g_w_out,
        g_b_query,
        g_b_value,
        g_b_out,
        g_ln1_gain,
        g_ln1_bias,
        g_w_hidden,
        g_b_hidden,
        g_w_proj,
        g_b_proj,
        g_ln2_gain,
        g_ln2_bias,
    )


def solution(mesh):
    size = mesh.shape["fsdp"]
    placed = (
        P("fsdp", None),
        P("fsdp", None),
        P("fsdp"),
        P("fsdp"),
        P("fsdp", None),
        P("fsdp", None),
        P("fsdp", None),
        P("fsdp", None),
        P("fsdp"),
        P("fsdp"),
        P("fsdp"),
        P("fsdp"),
        P("fsdp"),
        P("fsdp", None),
        P("fsdp"),
        P("fsdp", None),
        P("fsdp"),
        P("fsdp"),
        P("fsdp"),
    )
    return jax.shard_map(
        functools.partial(local, size) if size == 32 else local_plain,
        mesh=mesh,
        in_specs=placed,
        out_specs=(
            P("fsdp", None),
            P("fsdp", None),
            P("fsdp", None),
            P("fsdp", None),
            P("fsdp", None),
            P("fsdp", None),
            P("fsdp"),
            P("fsdp"),
            P("fsdp"),
            P("fsdp"),
            P("fsdp"),
            P("fsdp", None),
            P("fsdp"),
            P("fsdp", None),
            P("fsdp"),
            P("fsdp"),
            P("fsdp"),
        ),
        check_vma=False,
    )
```

```python
import functools
import math

import jax
import jax.numpy as jnp
from jax import lax
from jax.experimental import pallas as pl
from jax.experimental.pallas import tpu as pltpu
from jax.sharding import PartitionSpec as P

HEADS = 12
LIVE = 800
EPSILON = 1e-05
NEG_FILL = -1e30
NT = (((1,), (1,)), ((), ()))
TN = (((0,), (0,)), ((), ()))
VMEM = pltpu.VMEM
F32, BF16 = jnp.float32, jnp.bfloat16


def dot(a, b, dims=(((1,), (0,)), ((), ()))):
    return lax.dot_general(a, b, dims, preferred_element_type=F32)


def lanes_of(shape, head, dim):
    lane = lax.broadcasted_iota(jnp.int32, shape, 1)
    return (lane < dim) if head == 0 else (lane >= dim)


def attend_kernel(lengths, x, wq, wk, wv, bq, bv, q, k, v, att, keys, values):
    rows, width = x.shape
    dim = width // HEADS
    pair = 2 * dim
    group = 2 * pair
    step = 256
    key_lane = lax.broadcasted_iota(jnp.int32, (1, LIVE), 1)
    bias = jnp.where(key_lane < lengths[0], 0.0, NEG_FILL).astype(F32)
    for head in range(2):
        values[head, :, pair:] = jnp.ones((LIVE, pair), BF16)
    for first in range(0, width, group):
        cols = pl.ds(first, group)

        @pl.loop(0, rows // step)
        def _(part):
            at = pl.ds(pl.multiple_of(part * step, step), step)
            here = x[at, :]
            q[at, cols] = ((dot(here, wq[:, cols]) + bq[:, cols]).astype(BF16).astype(F32) * (1.0 / math.sqrt(dim))).astype(BF16)
            k[at, cols] = dot(here, wk[:, cols]).astype(BF16)
            v[at, cols] = (dot(here, wv[:, cols]) + bv[:, cols]).astype(BF16)

        for start in range(first, first + group, pair):
            wide = pl.ds(start, pair)
            whole = k[:LIVE, wide]
            for head in range(2):
                keys[head] = jnp.where(lanes_of(whole.shape, head, dim), whole, jnp.zeros_like(whole))
                values[head, :, :pair] = v[:LIVE, wide]

            @pl.loop(0, rows // step)
            def _(part):
                at = pl.ds(pl.multiple_of(part * step, step), step)
                here = q[at, wide]
                outs = []
                for head in range(2):
                    s = dot(here, keys[head], NT) + bias
                    e = jnp.exp(s - jnp.max(s, -1, keepdims=True))
                    o = dot(e.astype(BF16), values[head])
                    outs.append(o[:, :pair] / o[:, pair:])
                att[at, wide] = jnp.where(lanes_of(outs[0].shape, 0, dim), outs[0], outs[1]).astype(BF16)


def attend(lengths, x, wq, wk, wv, bq, bv):
    rows, width = x.shape
    pair = 2 * width // HEADS
    return pl.pallas_call(
        attend_kernel,
        out_shape=[jax.ShapeDtypeStruct(x.shape, BF16)] * 4,
        in_specs=[pl.BlockSpec(memory_space=pltpu.SMEM)] + [pl.BlockSpec(memory_space=VMEM)] * 6,
        out_specs=[pl.BlockSpec(memory_space=VMEM)] * 4,
        scratch_shapes=[VMEM((2, LIVE, pair), BF16), VMEM((2, LIVE, 2 * pair), BF16)],
        compiler_params=pltpu.CompilerParams(vmem_limit_bytes=60 << 20),
        name="attend",
    )(lengths, x, wq, wk, wv, bq, bv)


def attend_back_kernel(lengths, x, dh1, q, k, v, da, wq, wk, wv, cot, skip, gin, gwq, gwk, gwv, gbq, gbv,
                       dq, dk, dv, keys, values, bias, dk_acc, dv_acc):
    rows, width = x.shape
    dim = width // HEADS
    pair = 2 * dim
    chunk = 256
    tops = [(c, min(chunk, -(-LIVE // 128) * 128 - c)) for c in range(0, LIVE, chunk)]
    key_row = lax.broadcasted_iota(jnp.int32, (LIVE, 128), 0)
    bias[...] = jnp.where(key_row < lengths[0], 0.0, NEG_FILL).astype(F32)
    dk[...] = jnp.zeros_like(dk)
    dv[...] = jnp.zeros_like(dv)

    def block(wide, start, size):
        at = pl.ds(start, size)
        q_c, da_c = q[at, wide], da[at, wide]
        dq_c = jnp.zeros((size, pair), F32)
        for head in range(2):
            mine = lanes_of(q_c.shape, head, dim)
            s = dot(keys[head], q_c, NT) + jnp.tile(bias[...], (1, size // 128))
            e = jnp.exp(s - jnp.max(s, 0, keepdims=True))
            p = e * (1.0 / jnp.sum(e, 0, keepdims=True))
            dp = dot(values[head], da_c, NT)
            t = p * dp
            ds = (t - p * jnp.sum(t, 0, keepdims=True)).astype(BF16)
            dv_acc[...] += dot(p.astype(BF16), jnp.where(mine, da_c, jnp.zeros_like(da_c)))
            dk_acc[...] += dot(ds, jnp.where(mine, q_c, jnp.zeros_like(q_c)))
            dq_c = dq_c + dot(ds, keys[head], TN)
        dq[at, wide] = (dq_c * (1.0 / math.sqrt(dim))).astype(BF16)

    @pl.loop(0, width // pair)
    def _(which):
        wide = pl.ds(pl.multiple_of(which * pair, pair), pair)
        whole, whole_v = k[:LIVE, wide], v[:LIVE, wide]
        for head in range(2):
            mine = lanes_of(whole.shape, head, dim)
            keys[head] = jnp.where(mine, whole, jnp.zeros_like(whole))
            values[head] = jnp.where(mine, whole_v, jnp.zeros_like(whole_v))
        dk_acc[...] = jnp.zeros_like(dk_acc)
        dv_acc[...] = jnp.zeros_like(dv_acc)

        @pl.loop(0, LIVE // chunk)
        def _(part):
            block(wide, pl.multiple_of(part * chunk, chunk), chunk)

        for start, size in tops:
            if size < chunk:
                block(wide, start, size)
        dk[:LIVE, wide] = dk_acc[...].astype(BF16)
        dv[:LIVE, wide] = dv_acc[...].astype(BF16)

    gbq[...] = jnp.sum(dq[:LIVE, :].astype(F32), 0, keepdims=True)
    gbv[...] = jnp.sum(dv[:LIVE, :].astype(F32), 0, keepdims=True)
    here = x[:LIVE, :]
    for grad, out in ((dq, gwq), (dk, gwk), (dv, gwv)):
        for start in range(0, width, 256):
            cols = pl.ds(start, 256)
            out[:, cols] = dot(here, grad[:LIVE, cols], TN).astype(BF16)
    step = 160

    @pl.loop(0, LIVE // step)
    def _(part):
        at = pl.ds(pl.multiple_of(part * step, step), step)
        total = dh1[at, :] + dot(dq[at, :], wq[...], NT)
        total = total + dot(dk[at, :], wk[...], NT)
        total = total + dot(dv[at, :], wv[...], NT)
        row = lax.broadcasted_iota(jnp.int32, (step, 1), 0) + part * step
        dropped = jnp.where(row < lengths[0], cot[at, :].astype(F32), 0.0)
        gin[at, :] = jnp.where(skip[0] == 1, dropped, total)

    gin[LIVE:, :] = jnp.zeros((rows - LIVE, width), F32)


def attend_back(lengths, x, dh1, q, k, v, da, wq, wk, wv, cot, skip):
    rows, width = x.shape
    pair = 2 * width // HEADS
    like = jax.ShapeDtypeStruct
    smem = pl.BlockSpec(memory_space=pltpu.SMEM)
    return pl.pallas_call(
        attend_back_kernel,
        out_shape=[like((rows, width), F32)] + [like((width, width), BF16)] * 3 + [like((1, width), F32)] * 2,
        in_specs=[smem] + [pl.BlockSpec(memory_space=VMEM)] * 10 + [smem],
        out_specs=[pl.BlockSpec(memory_space=VMEM)] * 6,
        scratch_shapes=[VMEM(x.shape, BF16)] * 3
        + [VMEM((2, LIVE, pair), BF16)] * 2
        + [VMEM((LIVE, 128), F32)]
        + [VMEM((LIVE, pair), F32)] * 2,
        compiler_params=pltpu.CompilerParams(vmem_limit_bytes=62 << 20),
        name="attend_back",
    )(lengths, x, dh1, q, k, v, da, wq, wk, wv, cot, skip)


def middle_kernel(lengths, skip, x_in, att_in, cot_in, wo_in, wh_in, wp_in, vec, bh,
                  outputs, dh1, da, gwo, gwh, gwp, gvec, gbh,
                  x, att, cot, wo, wh, wp, z1, n1, inv1, f, g, slope, df, z1t, out_h, out_p, load_sem, out_sem):
    rows, width = x.shape
    inner = wh.shape[1]
    loads = [
        pltpu.make_async_copy(a, b, load_sem.at[i])
        for i, (a, b) in enumerate(
            ((x_in, x), (att_in, att), (wo_in, wo), (wh_in, wh), (wp_in, wp), (cot_in, cot))
        )
    ]
    for load in loads:
        load.start()
    bo, gain1, shift1, bp, gain2, shift2 = (vec[i : i + 1, :] for i in range(6))
    for load in loads[:3]:
        load.wait()
    step = 256

    def norm(h):
        centred = h - jnp.mean(h, -1, keepdims=True)
        inv = lax.rsqrt(jnp.mean(centred * centred, -1, keepdims=True) + EPSILON)
        return centred * inv, inv

    def norm_back(e, n, inv):
        return inv * (e - jnp.mean(e, -1, keepdims=True) - n * jnp.mean(e * n, -1, keepdims=True))

    @pl.loop(0, rows // step)
    def _(part):
        at = pl.ds(pl.multiple_of(part * step, step), step)
        h = x[at, :].astype(F32) + (dot(att[at, :], wo[...]) + bo)
        n, inv = norm(h)
        n1[at, :] = n
        inv1[at, :] = jnp.broadcast_to(inv, (step, 128))
        z1[at, :] = (n * gain1 + shift1).astype(BF16)

    loads[3].wait()
    loads[4].wait()
    f[...] = jnp.zeros_like(f)
    wide = 256

    @pl.loop(0, inner // wide)
    def _(block):
        cols = pl.ds(pl.multiple_of(block * wide, wide), wide)
        b = bh[:, cols]
        for start in range(0, rows, step):
            at = pl.ds(start, step)
            u = dot(z1[at, :], wh[:, cols]) + b
            phi = 0.5 * (1.0 + lax.erf(u * 0.7071067811865476))
            g[at, cols] = (u * phi).astype(BF16)
            slope[at, cols] = (phi + u * (jnp.exp(-0.5 * u * u) * 0.3989422804014327)).astype(BF16)
            f[at, :] += dot(g[at, cols], wp[cols, :])

    loads[5].wait()
    gvec[...] = jnp.zeros_like(gvec)
    keep = 1.0 - skip[0].astype(F32)

    @pl.loop(0, rows // step)
    def _(part):
        at = pl.ds(pl.multiple_of(part * step, step), step)
        n, inv = norm(z1[at, :].astype(F32) + (f[at, :] + bp))
        outputs[at, :] = jnp.where(skip[0] == 1, x[at, :], (n * gain2 + shift2).astype(BF16))
        row = lax.broadcasted_iota(jnp.int32, (step, 1), 0) + part * step
        dy = jnp.where(row < lengths[0], cot[at, :].astype(F32), 0.0) * keep
        d = norm_back(dy * gain2, n, inv)
        low = d.astype(BF16)
        f[at, :] = d
        df[at, :] = low
        gvec[3:4, :] += jnp.sum(low.astype(F32), 0, keepdims=True)
        gvec[4:5, :] += jnp.sum(dy * n, 0, keepdims=True)
        gvec[5:6, :] += jnp.sum(dy, 0, keepdims=True)

    z1t[...] = z1[:LIVE, :].T

    def flush(block, buf, slot):
        cols = pl.ds(pl.multiple_of(block * wide, wide), wide)
        if buf is out_h:
            return pltpu.make_async_copy(buf.at[slot], gwh.at[:, cols], out_sem.at[0, slot])
        return pltpu.make_async_copy(buf.at[slot], gwp.at[cols, :], out_sem.at[1, slot])

    @pl.loop(0, inner // wide)
    def _(block):
        slot = lax.rem(block, 2)
        cols = pl.ds(pl.multiple_of(block * wide, wide), wide)

        @pl.when(block >= 2)
        def _():
            flush(block, out_h, slot).wait()
            flush(block, out_p, slot).wait()

        out_p[slot] = dot(g[:LIVE, cols], df[:LIVE, :], TN).astype(BF16)
        flush(block, out_p, slot).start()
        total = jnp.zeros((1, wide), F32)
        half = LIVE // 2
        for start in range(0, LIVE, half):
            at = pl.ds(start, half)
            du = (dot(df[at, :], wp[cols, :], NT) * slope[at, cols].astype(F32)).astype(BF16)
            total = total + jnp.sum(du.astype(F32), 0, keepdims=True)
            g[at, cols] = du
            f[at, :] += dot(du, wh[:, cols], NT)
        gbh[:, cols] = total
        out_h[slot] = dot(z1t[...], g[:LIVE, cols]).astype(BF16)
        flush(block, out_h, slot).start()

    half = LIVE // 5
    @pl.loop(0, LIVE // half)
    def _(part):
        at = pl.ds(pl.multiple_of(part * half, half), half)
        dz = f[at, :]
        n = n1[at, :]
        gvec[1:2, :] += jnp.sum(dz * n, 0, keepdims=True)
        gvec[2:3, :] += jnp.sum(dz, 0, keepdims=True)
        d = norm_back(dz * gain1, n, inv1[at, :1])
        dh1[at, :] = d
        low = d.astype(BF16)
        df[at, :] = low
        gvec[0:1, :] += jnp.sum(low.astype(F32), 0, keepdims=True)
        da[at, :] = dot(low, wo[...], NT).astype(BF16)

    da[LIVE:, :] = jnp.zeros((rows - LIVE, width), BF16)
    for start in range(0, width, wide):
        cols = pl.ds(start, wide)
        gwo[cols, :] = dot(att[:LIVE, cols], df[:LIVE, :], TN).astype(BF16)
    for block in (inner // wide - 2, inner // wide - 1):
        flush(block, out_h, block % 2).wait()
        flush(block, out_p, block % 2).wait()


def middle(lengths, skip, x, att, cot, wo, wh, wp, vec, bh):
    rows, width = x.shape
    inner = wh.shape[1]
    like = jax.ShapeDtypeStruct
    smem, vmem, any_ = (pl.BlockSpec(memory_space=m) for m in (pltpu.SMEM, VMEM, pl.ANY))
    pad = -(-LIVE // 128) * 128
    return pl.pallas_call(
        middle_kernel,
        out_shape=[
            like((rows, width), BF16), like((LIVE, width), F32), like((rows, width), BF16),
            like((width, width), BF16), like((width, inner), BF16), like((inner, width), BF16),
            like((8, width), F32), like((1, inner), F32),
        ],
        in_specs=[smem] * 2 + [any_] * 6 + [vmem] * 2,
        out_specs=[vmem] * 4 + [any_] * 2 + [vmem] * 2,
        scratch_shapes=[
            VMEM((rows, width), BF16), VMEM((rows, width), BF16), VMEM((rows, width), BF16),
            VMEM((width, width), BF16), VMEM((width, inner), BF16), VMEM((inner, width), BF16),
            VMEM((rows, width), BF16), VMEM((rows, width), F32), VMEM((rows, 128), F32),
            VMEM((rows, width), F32), VMEM((rows, inner), BF16), VMEM((rows, inner), BF16),
            VMEM((rows, width), BF16), VMEM((width, LIVE), BF16),
            VMEM((2, width, 256), BF16), VMEM((2, 256, width), BF16),
            pltpu.SemaphoreType.DMA((6,)), pltpu.SemaphoreType.DMA((2, 2)),
        ],
        compiler_params=pltpu.CompilerParams(vmem_limit_bytes=63 << 20),
        name="middle",
    )(lengths, skip, x, att, cot, wo, wh, wp, vec, bh)


def as_float(value):
    return value.astype(jnp.float32)


MESH = pl.DeviceIdType.MESH


def place(me, planes):
    core = lax.rem(me, 2)
    chip = me // 2
    col = lax.rem(chip, 2)
    row = lax.rem(chip // 2, 2)
    plane = chip // 4
    near = jnp.where(core == 0, row, col)
    far = jnp.where(core == 0, col, row)

    def index(plane_, near_, far_, core_):
        row_ = jnp.where(core_ == 0, near_, far_)
        col_ = jnp.where(core_ == 0, far_, near_)
        return ((plane_ * 2 + row_) * 2 + col_) * 2 + core_

    return core, near, far, plane, index


def greet(peers):
    barrier = pltpu.get_barrier_semaphore()
    for peer in peers:
        pl.semaphore_signal(barrier, inc=1, device_id=(peer,), device_id_type=MESH)
    pl.semaphore_wait(barrier, len(peers))


class Gather:
    def __init__(self, groups, planes, send_sem, recv_sem, local_sem):
        self.groups = groups
        self.planes = planes
        self.sems = send_sem, recv_sem, local_sem
        self.me = lax.axis_index("fsdp")
        self.core, self.near, self.far, self.plane, self.index = place(self.me, planes)
        self.other = self.index(self.plane, self.far, self.near, 1 - self.core)
        self.near_peer = self.index(self.plane, 1 - self.near, self.far, self.core)
        self.far_peer = self.index(self.plane, self.near, 1 - self.far, self.core)
        self.others = [lax.rem(self.plane + step, planes) for step in range(1, planes)]
        self.plane_peers = [self.index(p, self.near, self.far, self.core) for p in self.others]
        self.number = {}
        for group in groups:
            for item in group:
                self.number[id(item)] = len(self.number)
        self.sent = {key: 0 for key in self.number}
        greet([self.other, self.near_peer, self.far_peer, *self.plane_peers])

    def spot(self, item, chunk):
        own, full, cols = item
        if cols is None:
            return full.at[chunk]
        rows = own.shape[0]
        return full.at[pl.ds(pl.multiple_of(chunk * rows, 8), rows), cols]

    def push(self, item, chunk, peer, src=None):
        n = self.number[id(item)]
        where = self.spot(item, chunk)
        copy = pltpu.make_async_remote_copy(
            src_ref=where if src is None else src,
            dst_ref=where,
            send_sem=self.sems[0].at[n, self.sent[id(item)]],
            recv_sem=self.sems[1].at[n, chunk],
            device_id=(peer,),
            device_id_type=MESH,
        )
        copy.start()
        self.sent[id(item)] += 1

    def arrive(self, item, chunk):
        n = self.number[id(item)]
        where = self.spot(item, chunk)
        pltpu.make_async_copy(where, where, self.sems[1].at[n, chunk]).wait()

    def stage(self, which, g):
        for item in self.groups[g]:
            if which == 1:
                own, full, cols = item
                src = own if cols is None else own.at[:, cols]
                for peer in [*self.plane_peers, self.near_peer, self.far_peer, self.other]:
                    self.push(item, self.me, peer, src)
                copy = pltpu.make_async_copy(
                    src, self.spot(item, self.me), self.sems[2].at[self.number[id(item)]]
                )
                copy.start()
            elif which == 2:
                for p in self.others:
                    chunk = self.index(p, self.near, self.far, self.core)
                    self.arrive(item, chunk)
                    for peer in (self.near_peer, self.far_peer, self.other):
                        self.push(item, chunk, peer)
            elif which == 3:
                for p in [self.plane, *self.others]:
                    chunk = self.index(p, 1 - self.near, self.far, self.core)
                    self.arrive(item, chunk)
                    for peer in (self.far_peer, self.other):
                        self.push(item, chunk, peer)
            elif which == 4:
                for near in (self.near, 1 - self.near):
                    for p in [self.plane, *self.others]:
                        chunk = self.index(p, near, 1 - self.far, self.core)
                        self.arrive(item, chunk)
                        self.push(item, chunk, self.other)
            else:
                for chip in range(4 * self.planes):
                    self.arrive(item, chip * 2 + 1 - self.core)
                where = self.spot(item, self.me)
                pltpu.make_async_copy(where, where, self.sems[2].at[self.number[id(item)]]).wait()

    def finish(self):
        for group in self.groups:
            for item in group:
                n = self.number[id(item)]
                where = self.spot(item, self.me)
                for k in range(self.sent[id(item)]):
                    pltpu.make_async_copy(where, where, self.sems[0].at[n, k]).wait()


def unpack(packed, vec, bh, size):
    width, inner = vec.shape[1], bh.shape[1]
    piece, long = width // size, inner // size

    def pick(row, part, start):
        flat = packed[:, row, :].astype(BF16)
        lane = lax.rem(lax.broadcasted_iota(jnp.int32, (128, width), 1) + start, part)
        entry = lax.broadcasted_iota(jnp.int32, (128, width), 0)
        spread = dot(flat, jnp.where(entry == lane, 1.0, 0.0).astype(BF16))
        lane = lax.broadcasted_iota(jnp.int32, (size, width), 1) + start
        owner = lax.broadcasted_iota(jnp.int32, (size, width), 0)
        return jnp.sum(jnp.where(lane - lax.rem(lane, part) == part * owner, spread, 0.0), 0, keepdims=True)

    for k in range(8):
        vec[k : k + 1, :] = pick(k, piece, 0)
    for start in range(0, inner, width):
        bh[:, start : start + width] = pick(8, long, start)


def norm(h):
    centred = h - jnp.mean(h, -1, keepdims=True)
    inv = lax.rsqrt(jnp.mean(centred * centred, -1, keepdims=True) + EPSILON)
    return centred * inv, inv


def norm_back(e, n, inv):
    return inv * (e - jnp.mean(e, -1, keepdims=True) - n * jnp.mean(e * n, -1, keepdims=True))


def front_kernel(size, lengths, skip, x_in, cot_in, *refs):
    refs = list(refs)

    def take(n):
        out = refs[:n]
        del refs[:n]
        return out

    vectors = take(9)
    own = take(6)
    saved = take(18)
    (x, cot, q, k, v, att, z1, n1, inv1, g, slope, f, outputs, df, gvec) = take(15)
    full = take(7)
    vec, bh, keys, values, mine, send_sem, recv_sem, local_sem, load_sem, save_sem = refs
    own = [*own, mine]
    mine[...] = jnp.zeros_like(mine)
    for row, piece in enumerate(vectors):
        mine[row, : piece.shape[0]] = piece[...].astype(F32)
    wq, wk, wv, wo, wh, wp, packed = full
    rows, width = x.shape
    inner = wh.shape[1]
    dim = width // HEADS
    pair = 2 * dim
    group = 2 * pair
    step = 256
    parts = rows // step
    loads = [pltpu.make_async_copy(a, b, load_sem.at[i]) for i, (a, b) in enumerate(((x_in, x), (cot_in, cot)))]
    for load in loads:
        load.start()

    def item(which, start=None, number=None):
        return own[which], full[which], None if start is None else pl.ds(start, number)

    groups = [[item(w, c, group) for w in range(3)] for c in range(0, width, group)]
    groups[0].insert(0, item(6))
    groups.append([item(3, 0, width)])
    groups += [[item(4, c, inner // 2)] for c in (0, inner // 2)]
    groups += [[item(5, c, n)] for c, n in ((0, 2 * group), (2 * group, width - 2 * group))]
    move = Gather(groups, size // 8, send_sem, recv_sem, local_sem)

    def moves(text):
        for word in text.split():
            move.stage(int(word[0]), int(word[1]))

    saves = []

    def save(src, index):
        copy = pltpu.make_async_copy(src, saved[index], save_sem.at[index])
        copy.start()
        saves.append(copy)

    moves("10 11 12 20 13 30 21 14 40 31 22 15 16 17 50")
    unpack(packed, vec, bh, size)
    bq, bv, bo, gain1, shift1, bp, gain2, shift2 = (vec[i : i + 1, :] for i in range(8))
    loads[0].wait()
    key_lane = lax.broadcasted_iota(jnp.int32, (1, LIVE), 1)
    bias = jnp.where(key_lane < lengths[0], 0.0, NEG_FILL).astype(F32)
    for head in range(2):
        values[head, :, pair:] = jnp.ones((LIVE, pair), BF16)

    ticks = iter(
        ["41 32", "23", "51", "42 33", "52 24", "43", "34 53", "25", "35", "44", "54 26", "36"]
    )
    for number, first in enumerate(range(0, width, group)):
        cols = pl.ds(first, group)

        @pl.loop(0, parts)
        def _(part):
            at = pl.ds(pl.multiple_of(part * step, step), step)
            here = x[at, :]
            query = (dot(here, wq[:, cols]) + bq[:, first : first + group]).astype(BF16)
            q[at, cols] = (query.astype(F32) * (1.0 / math.sqrt(dim))).astype(BF16)
            k[at, cols] = dot(here, wk[:, cols]).astype(BF16)
            v[at, cols] = (dot(here, wv[:, cols]) + bv[:, first : first + group]).astype(BF16)

        for start in range(first, first + group, pair):
            wide = pl.ds(start, pair)
            whole = k[:LIVE, wide]
            for head in range(2):
                keys[head] = jnp.where(lanes_of(whole.shape, head, dim), whole, jnp.zeros_like(whole))
                values[head, :, :pair] = v[:LIVE, wide]
            now = [next(ticks), next(ticks)]

            @pl.loop(0, parts)
            def _(part):
                at = pl.ds(pl.multiple_of(part * step, step), step)
                here = q[at, wide]
                outs = []
                for head in range(2):
                    s = dot(here, keys[head], NT) + bias
                    e = jnp.exp(s - jnp.max(s, -1, keepdims=True))
                    o = dot(e.astype(BF16), values[head])
                    outs.append(o[:, :pair] / o[:, pair:])
                att[at, wide] = jnp.where(lanes_of(outs[0].shape, 0, dim), outs[0], outs[1]).astype(BF16)
                for turn, text in enumerate(now):

                    @pl.when(part == 2 * turn + 1)
                    def _():
                        moves(text)

    save(q, 0)
    save(k, 1)
    save(v, 2)
    save(att, 3)
    for n, w in enumerate((wq, wk, wv, wo)):
        save(w, 12 + n)

    @pl.loop(0, parts)
    def _(part):
        at = pl.ds(pl.multiple_of(part * step, step), step)
        h = x[at, :].astype(F32) + (dot(att[at, :], wo[...]) + bo)
        n, inv = norm(h)
        n1[at, :] = n
        inv1[at, :] = jnp.broadcast_to(inv, (step, 128))
        z1[at, :] = (n * gain1 + shift1).astype(BF16)

    save(z1, 4)
    save(n1.at[pl.ds(0, LIVE)], 5)
    save(inv1.at[pl.ds(0, LIVE)], 6)
    moves("45 27")
    later = {2: "55 37", 6: "46"}

    @pl.loop(0, inner // step)
    def _(block):
        cols = pl.ds(pl.multiple_of(block * step, step), step)
        b = bh[:, cols]
        for start in range(0, rows, step):
            at = pl.ds(start, step)
            u = dot(z1[at, :], wh[:, cols]) + b
            phi = 0.5 * (1.0 + lax.erf(u * 0.7071067811865476))
            g[at, cols] = (u * phi).astype(BF16)
            if start < LIVE:
                slope[at, cols] = (phi + u * (jnp.exp(-0.5 * u * u) * 0.3989422804014327)).astype(BF16)
        for turn, text in later.items():

            @pl.when(block == turn)
            def _():
                moves(text)

    save(g.at[pl.ds(0, LIVE)], 7)
    save(slope.at[pl.ds(0, LIVE)], 8)
    save(wh, 16)
    moves("56 47")
    for turn, (first, many) in enumerate(((0, 2 * group), (2 * group, width - 2 * group))):
        if turn:
            moves("57")
        cols = pl.ds(first, many)

        @pl.loop(0, parts)
        def _(part):
            at = pl.ds(pl.multiple_of(part * step, step), step)
            f[at, cols] = dot(g[at, :], wp[:, cols])

    save(wp, 17)
    loads[1].wait()
    gvec[...] = jnp.zeros_like(gvec)
    keep = 1.0 - skip[0].astype(F32)

    @pl.loop(0, parts)
    def _(part):
        at = pl.ds(pl.multiple_of(part * step, step), step)
        n, inv = norm(z1[at, :].astype(F32) + (f[at, :] + bp))
        outputs[at, :] = jnp.where(skip[0] == 1, x[at, :], (n * gain2 + shift2).astype(BF16))
        row = lax.broadcasted_iota(jnp.int32, (step, 1), 0) + part * step
        dy = jnp.where(row < lengths[0], cot[at, :].astype(F32), 0.0) * keep
        d = norm_back(dy * gain2, n, inv)
        low = d.astype(BF16)
        f[at, :] = d
        df[at, :] = low
        gvec[5:6, :] += jnp.sum(low.astype(F32), 0, keepdims=True)
        gvec[6:7, :] += jnp.sum(dy * n, 0, keepdims=True)
        gvec[7:8, :] += jnp.sum(dy, 0, keepdims=True)

    save(f.at[pl.ds(0, LIVE)], 9)
    save(df.at[pl.ds(0, LIVE)], 10)
    save(outputs, 11)
    for copy in saves:
        copy.wait()
    move.finish()


def front(size, lengths, skip, x, cot, weights, vectors):
    rows, width = x.shape
    inner = weights[4].shape[1]
    like = jax.ShapeDtypeStruct
    smem, vmem, any_ = (pl.BlockSpec(memory_space=m) for m in (pltpu.SMEM, VMEM, pl.ANY))
    act = like((rows, width), BF16)
    outs = [
        act, act, act, act, act,
        like((LIVE, width), F32), like((LIVE, 128), F32),
        like((LIVE, inner), BF16), like((LIVE, inner), BF16),
        like((LIVE, width), F32), like((LIVE, width), BF16), act,
        *[like((width, width), BF16)] * 4, like((width, inner), BF16), like((inner, width), BF16),
    ]
    groups_items = 3 * 3 + 1 + 1 + 2 + 2
    pair = 2 * width // HEADS
    scratch = [
        VMEM((rows, width), BF16), VMEM((rows, width), BF16),
        *[VMEM((rows, width), BF16)] * 5,
        VMEM((rows, width), F32), VMEM((rows, 128), F32),
        VMEM((rows, inner), BF16), VMEM((rows, inner), BF16),
        VMEM((rows, width), F32), VMEM((rows, width), BF16), VMEM((rows, width), BF16),
    ]
    weights_full = [*[VMEM((width, width), BF16)] * 4, VMEM((width, inner), BF16), VMEM((inner, width), BF16),
                    VMEM((size, 16, 128), F32)]
    planes = size // 8
    sends = (planes + 2) + (planes - 1) * 3 + planes * 2 + planes * 2
    return pl.pallas_call(
        functools.partial(front_wrap, size),
        out_shape=[*outs, like((8, width), F32), like((8, width), F32)],
        in_specs=[smem, smem] + [any_] * 2 + [vmem] * 9 + [any_] * 6,
        out_specs=[any_] * 18 + [vmem] * 2,
        scratch_shapes=[
            *scratch, *weights_full, VMEM((1, inner), F32),
            VMEM((2, LIVE, pair), BF16), VMEM((2, LIVE, 2 * pair), BF16), VMEM((16, 128), F32),
            pltpu.SemaphoreType.DMA((groups_items, sends)),
            pltpu.SemaphoreType.DMA((groups_items, size)),
            pltpu.SemaphoreType.DMA((groups_items,)),
            pltpu.SemaphoreType.DMA((2,)),
            pltpu.SemaphoreType.DMA((18,)),
        ],
        compiler_params=pltpu.CompilerParams(collective_id=0, has_side_effects=True, vmem_limit_bytes=64 << 20),
        name="front",
    )(lengths, skip, x, cot, *vectors, *weights)


def front_wrap(size, lengths, skip, x_in, cot_in, *refs):
    own, saved, vec, gvec, scratch = refs[:15], refs[15:33], refs[33], refs[34], refs[35:]
    body, full, rest = scratch[:14], scratch[14:21], scratch[21:]
    front_kernel(size, lengths, skip, x_in, cot_in, *own, *saved, *body, gvec, *full, vec, *rest)


class Scatter:
    def __init__(self, tensors, planes, send_sem, recv_sem, out_sem, vector):
        self.tensors = tensors
        self.planes = planes
        self.half = 4 * planes
        self.sems = send_sem, recv_sem, out_sem
        self.vector = vector
        me = lax.axis_index("fsdp")
        self.core, self.near, self.far, self.plane, self.index = place(me, planes)
        self.other = self.index(self.plane, self.far, self.near, 1 - self.core)
        self.near_peer = self.index(self.plane, 1 - self.near, self.far, self.core)
        self.far_peer = self.index(self.plane, self.near, 1 - self.far, self.core)
        self.others = [lax.rem(self.plane + step, planes) for step in range(1, planes)]
        self.plane_peers = [self.index(p, self.near, self.far, self.core) for p in self.others]
        greet([self.other, self.near_peer, self.far_peer, *self.plane_peers])

    def push(self, src, dst, number, spot, peer):
        pltpu.make_async_remote_copy(
            src_ref=src, dst_ref=dst, send_sem=self.sems[0].at[number, spot],
            recv_sem=self.sems[1].at[number, spot], device_id=(peer,), device_id_type=MESH,
        ).start()

    def landed(self, ref, number, spot):
        pltpu.make_async_copy(ref, ref, self.sems[1].at[number, spot]).wait()

    def stage(self, which, tensor, number, start, many):
        part, got0, got1, got2, got3, final, result, rows = self.tensors[tensor]
        cols = pl.ds(start, many)
        planes, half = self.planes, self.half

        def at(ref, n):
            return ref.at[pl.ds(pl.multiple_of(n * rows, 8), rows), cols]

        def mine(slot):
            far_step = 1 - slot // (2 * planes)
            near_step = 1 - lax.rem(slot // planes, 2)
            near = jnp.where(near_step == 1, 1 - self.near, self.near)
            far = jnp.where(far_step == 1, 1 - self.far, self.far)
            return self.index(lax.rem(slot, planes), near, far, self.core)

        def value(ref, n):
            return at(ref, n)[...].astype(F32)

        if which == 0:

            @pl.loop(0, half)
            def _(slot):
                far_step = 1 - slot // (2 * planes)
                near_step = 1 - lax.rem(slot // planes, 2)
                near = jnp.where(near_step == 1, 1 - self.far, self.far)
                far = jnp.where(far_step == 1, 1 - self.near, self.near)
                chunk = self.index(lax.rem(slot, planes), near, far, 1 - self.core)
                self.push(at(part, chunk), at(got0, slot), number, slot, self.other)
        elif which == 1:

            @pl.loop(0, half // 2)
            def _(slot):
                chunk = mine(slot)
                self.landed(at(got0, slot), number, slot)
                at(part, chunk)[...] = (value(part, chunk) + value(got0, slot)).astype(BF16)
                self.push(at(part, chunk), at(got1, slot), number, half + slot, self.far_peer)
        elif which == 2:

            @pl.loop(0, planes)
            def _(p):
                slot = half // 2 + p
                chunk = mine(slot)
                self.landed(at(got0, slot), number, slot)
                self.landed(at(got1, p), number, half + p)
                total = value(part, chunk) + value(got0, slot) + value(got1, p)
                at(part, chunk)[...] = total.astype(BF16)
                self.push(at(part, chunk), at(got2, p), number, half + 2 * planes + p, self.near_peer)
        elif which == 3:

            @pl.loop(0, planes)
            def _(step):
                p = lax.rem(self.plane + 1 + step, planes)
                slot = half - planes + p
                chunk = mine(slot)
                self.landed(at(got0, slot), number, slot)
                self.landed(at(got1, planes + p), number, half + planes + p)
                self.landed(at(got2, p), number, half + 2 * planes + p)
                total = value(part, chunk) + value(got0, slot) + value(got1, planes + p) + value(got2, p)

                @pl.when(step == planes - 1)
                def _():
                    final[:, cols] = total

                @pl.when(step < planes - 1)
                def _():
                    at(part, chunk)[...] = total.astype(BF16)
                    self.push(
                        at(part, chunk), at(got3, step), number, half + 3 * planes + step,
                        self.index(p, self.near, self.far, self.core),
                    )
        else:
            for step in range(planes - 1):
                self.landed(at(got3, step), number, half + 3 * planes + step)
            total = final[:, cols]
            for step in range(planes - 1):
                total = total + value(got3, step)
            final[:, cols] = total
            pltpu.make_async_copy(final.at[:, cols], result.at[:, cols], self.sems[2].at[number]).start()

    def vector_stage(self, which):
        sums, got, number, result = self.vector
        steps = [self.other, self.near_peer, self.far_peer]
        if which > 0:
            if which < 4:
                self.landed(got.at[which - 1], number, which - 1)
                sums[which] = sums[which - 1] + got[which - 1]
            else:
                total = sums[3]
                for step in range(self.planes - 1):
                    self.landed(got.at[3 + step], number, 3 + step)
                    total = total + got[3 + step]
                sums[4] = total
                pltpu.make_async_copy(sums.at[4], result, self.sems[2].at[number]).start()
        if which < 3:
            self.push(sums.at[which], got.at[which], number, which, steps[which])
        elif which == 3:
            for step, peer in enumerate(self.plane_peers):
                self.push(sums.at[3], got.at[3 + step], number, 3 + step, peer)

    def finish(self, items):
        for tensor, number, start, many in items:
            part, rows = self.tensors[tensor][0], self.tensors[tensor][-1]
            one = part.at[pl.ds(0, rows), pl.ds(start, many)]

            @pl.loop(0, self.half + 4 * self.planes - 1)
            def _(spot):
                pltpu.make_async_copy(one, one, self.sems[0].at[number, spot]).wait()

            final = self.tensors[tensor][5].at[:, pl.ds(start, many)]
            pltpu.make_async_copy(final, final, self.sems[2].at[number]).wait()
        sums, got, number, result = self.vector
        for spot in range(3 + self.planes - 1):
            pltpu.make_async_copy(got.at[0], got.at[0], self.sems[0].at[number, spot]).wait()
        pltpu.make_async_copy(got.at[0], got.at[0], self.sems[2].at[number]).wait()


BACK_INPUTS = ("df", "g", "wp", "slope", "wh", "dh2", "z1", "wo", "n1", "inv1", "att", "k", "v", "q", "x", "wq", "wk", "wv", "cot")


def back_kernel(size, lengths, skip, vec, gtop, *refs):
    refs = list(refs)

    def take(n):
        out = refs[:n]
        del refs[:n]
        return out

    count = len(BACK_INPUTS)
    source = dict(zip(BACK_INPUTS, take(count)))
    gin = take(1)[0]
    results = take(6)
    vector_result = take(1)[0]
    here = dict(zip(BACK_INPUTS, take(count)))
    z1t, keys, values, bias, dk_acc, dv_acc = take(6)
    got = [take(6) for _ in range(4)]
    final = take(6)
    sums, sums_got = take(2)
    send_sem, recv_sem, out_sem, load_sem, gin_sem = refs
    df, g, wp, slope, wh, f, z1, wo, n1, inv1, att, k, v, q, x, wq, wk, wv, cot = (here[n] for n in BACK_INPUTS)
    width, inner = wh.shape
    dim = width // HEADS
    pair = 2 * dim
    group = 2 * pair
    wide = 256
    planes = size // 8

    loads = {}
    for n, name in enumerate(BACK_INPUTS):
        dst = here[name]
        src = source[name]
        rows = min(src.shape[0], dst.shape[0]) if name not in ("wq", "wk", "wv", "wo", "wh", "wp") else dst.shape[0]
        if name in ("g", "df", "slope", "dh2"):
            rows = LIVE
        loads[name] = pltpu.make_async_copy(src.at[pl.ds(0, rows)], dst.at[pl.ds(0, rows)], load_sem.at[n])
        loads[name].start()
    grads = [wq, wk, wv, wo, wh, wp]
    tensors = [
        (grads[t], got[0][t], got[1][t], got[2][t], got[3][t], final[t], results[t], grads[t].shape[0] // size)
        for t in range(6)
    ]
    groups = width // group
    items = {"wha": (4, 0, 0, inner // 2), "whb": (4, 1, inner // 2, inner // 2),
             "wpa": (5, 2, 0, 2 * group), "wpb": (5, 3, 2 * group, width - 2 * group), "wo": (3, 4, 0, width)}
    first_group = 5
    vector_number = first_group + 3 * groups
    move = Scatter(tensors, planes, send_sem, recv_sem, out_sem, (sums, sums_got, vector_number, vector_result))

    def moves(text):
        for word in text.split():
            move.stage(int(word[0]), *items[word[1:]])

    def group_moves(which, number):
        for t in range(3):
            start = number * group
            move.stage(which, t, first_group + 3 * number + t, start if isinstance(number, int) else pl.multiple_of(start, group), group)

    gain1 = vec[3:4, :]
    gvec = sums.at[0]
    gvec[...] = jnp.zeros(gvec.shape, F32)
    gvec[0:8, :] = gtop[...]
    for name in ("df", "g", "wp", "slope", "wh", "dh2", "z1"):
        loads[name].wait()
    z1t[...] = z1[...].T

    @pl.loop(0, inner // wide)
    def _(block):
        cols = pl.ds(pl.multiple_of(block * wide, wide), wide)
        total = jnp.zeros((1, wide), F32)
        half = LIVE // 2
        for start in range(0, LIVE, half):
            at = pl.ds(start, half)
            du = (dot(df[at, :], wp[cols, :], NT) * slope[at, cols].astype(F32)).astype(BF16)
            total = total + jnp.sum(du.astype(F32), 0, keepdims=True)
            slope[at, cols] = du
            f[at, :] += dot(du, wh[:, cols], NT)
        row = 8 + (block * wide) // width
        for r in range(inner // width):

            @pl.when(row == 8 + r)
            def _():
                gvec[8 + r : 9 + r, pl.ds(pl.multiple_of(lax.rem(block * wide, width), wide), wide)] = total
        wh[:, cols] = dot(z1t[...], slope[:, cols]).astype(BF16)
        for turn, text in {5: "0wha", 10: "1wha", 11: "0whb"}.items():

            @pl.when(block == turn)
            def _():
                moves(text)

    for name, first, many in (("wpa", 0, 2 * group), ("wpb", 2 * group, width - 2 * group)):
        cols = pl.ds(first, many)

        @pl.loop(0, inner // wide)
        def _(block):
            at = pl.ds(pl.multiple_of(block * wide, wide), wide)
            wp[at, cols] = dot(g[:LIVE, at], df[:, cols], TN).astype(BF16)

        moves("0" + name)
    moves("2wha 1whb")
    for name in ("wo", "n1", "inv1", "att"):
        loads[name].wait()
    dq, dk, dv, da = (g.at[:, pl.ds(n * width, width)] for n in range(4))
    step = 160

    @pl.loop(0, LIVE // step)
    def _(part):
        at = pl.ds(pl.multiple_of(part * step, step), step)
        dz = f[at, :]
        n = n1[at, :]
        gvec[3:4, :] += jnp.sum(dz * n, 0, keepdims=True)
        gvec[4:5, :] += jnp.sum(dz, 0, keepdims=True)
        d = norm_back(dz * gain1, n, inv1[at, :1])
        f[at, :] = d
        low = d.astype(BF16)
        df[at, :] = low
        gvec[2:3, :] += jnp.sum(low.astype(F32), 0, keepdims=True)
        da[at, :] = dot(low, wo[...], NT).astype(BF16)

    padded = g.shape[0]
    da[LIVE:, :] = jnp.zeros((padded - LIVE, width), BF16)
    for start in range(0, width, wide):
        cols = pl.ds(start, wide)
        wo[cols, :] = dot(att[:, cols], df[...], TN).astype(BF16)
    moves("0wo 3wha")

    for name in ("k", "v", "q", "x", "wq", "wk", "wv"):
        loads[name].wait()
    z1t[...] = x[...].T
    xt = z1t
    chunk = 256
    key_row = lax.broadcasted_iota(jnp.int32, (LIVE, 128), 0)
    bias[...] = jnp.where(key_row < lengths[0], 0.0, NEG_FILL).astype(F32)

    def block(wide, start, size):
        at = pl.ds(start, size)
        q_c, da_c = q[at, wide], da[at, wide]
        dq_c = jnp.zeros((size, pair), F32)
        for head in range(2):
            mine = lanes_of(q_c.shape, head, dim)
            s = dot(keys[head], q_c, NT) + jnp.tile(bias[...], (1, size // 128))
            e = jnp.exp(s - jnp.max(s, 0, keepdims=True))
            p = e * (1.0 / jnp.sum(e, 0, keepdims=True))
            dp = dot(values[head], da_c, NT)
            t = p * dp
            ds = (t - p * jnp.sum(t, 0, keepdims=True)).astype(BF16)
            dv_acc[...] += dot(p.astype(BF16), jnp.where(mine, da_c, jnp.zeros_like(da_c)))
            dk_acc[...] += dot(ds, jnp.where(mine, q_c, jnp.zeros_like(q_c)))
            dq_c = dq_c + dot(ds, keys[head], TN)
        dq[at, wide] = (dq_c * (1.0 / math.sqrt(dim))).astype(BF16)

    turns = {
        (0, 0): "1wpa", (0, 1): "2whb", (0, 2): "4wha 1wpb", (0, 3): "3whb",
        (1, 0): "1wo", (1, 2): "2wpa 4whb",
        (2, 0): "3wpa", (2, 1): "2wpb", (2, 3): "3wpb 2wo",
        (3, 0): "4wpa", (3, 1): "3wo", (3, 2): "4wpb", (4, 0): "4wo",
    }

    def tick(which, part):
        for (a, b), text in turns.items():
            if isinstance(part, int) and part != b:
                continue
            test = which == a if isinstance(part, int) else jnp.logical_and(which == a, part == b)

            @pl.when(test)
            def _():
                moves(text)

        for stage, odd, spot in ((1, 0, 2), (2, 1, 1), (3, 1, 3)):
            if isinstance(part, int) and part != spot:
                continue
            test = jnp.logical_and(which >= 2, lax.rem(which, 2) == odd)
            if not isinstance(part, int):
                test = jnp.logical_and(test, part == spot)

            @pl.when(test)
            def _():
                group_moves(stage, which // 2 - 1)

    @pl.loop(0, width // pair)
    def _(which):
        wide = pl.ds(pl.multiple_of(which * pair, pair), pair)
        whole, whole_v = k[:, wide], v[:, wide]
        for head in range(2):
            mine = lanes_of(whole.shape, head, dim)
            keys[head] = jnp.where(mine, whole, jnp.zeros_like(whole))
            values[head] = jnp.where(mine, whole_v, jnp.zeros_like(whole_v))
        dk_acc[...] = jnp.zeros_like(dk_acc)
        dv_acc[...] = jnp.zeros_like(dv_acc)

        @pl.loop(0, LIVE // chunk)
        def _(part):
            block(wide, pl.multiple_of(part * chunk, chunk), chunk)
            tick(which, part)

        block(wide, LIVE // chunk * chunk, padded - LIVE // chunk * chunk)
        dk[:LIVE, wide] = dk_acc[...].astype(BF16)
        dv[:LIVE, wide] = dv_acc[...].astype(BF16)
        tick(which, LIVE // chunk)

        @pl.when(lax.rem(which, 2) == 1)
        def _():
            number = which // 2
            cols = pl.ds(pl.multiple_of(number * group, group), group)

            @pl.loop(0, LIVE // step)
            def _(part):
                at = pl.ds(pl.multiple_of(part * step, step), step)
                total = f[at, :] + dot(dq[at, cols], wq[:, cols], NT)
                total = total + dot(dk[at, cols], wk[:, cols], NT)
                f[at, :] = total + dot(dv[at, cols], wv[:, cols], NT)

            for grad, out in ((dq, wq), (dk, wk), (dv, wv)):
                out[:, cols] = dot(xt[...], grad[:LIVE, cols]).astype(BF16)
            group_moves(0, number)

    last = groups - 1
    gvec[0:1, :] = jnp.sum(dq[:LIVE, :].astype(F32), 0, keepdims=True)
    gvec[1:2, :] = jnp.sum(dv[:LIVE, :].astype(F32), 0, keepdims=True)
    move.vector_stage(0)
    for number in range(last):
        group_moves(4, number)
    group_moves(1, last)
    move.vector_stage(1)
    loads["cot"].wait()

    @pl.loop(0, LIVE // step)
    def _(part):
        at = pl.ds(pl.multiple_of(part * step, step), step)
        row = lax.broadcasted_iota(jnp.int32, (step, 1), 0) + part * step
        dropped = jnp.where(row < lengths[0], cot[at, :].astype(F32), 0.0)
        f[at, :] = jnp.where(skip[0] == 1, dropped, f[at, :])

    out = [pltpu.make_async_copy(f, gin.at[pl.ds(0, LIVE)], gin_sem.at[0])]
    n1[: gin.shape[0] - LIVE, :] = jnp.zeros((gin.shape[0] - LIVE, width), F32)
    out.append(pltpu.make_async_copy(n1.at[pl.ds(0, gin.shape[0] - LIVE)], gin.at[pl.ds(LIVE, gin.shape[0] - LIVE)], gin_sem.at[1]))
    for copy in out:
        copy.start()
    move.vector_stage(2)
    group_moves(2, last)
    move.vector_stage(3)
    group_moves(3, last)
    move.vector_stage(4)
    group_moves(4, last)
    for copy in out:
        copy.wait()
    move.finish(
        [*items.values(), *((t, first_group + 3 * number + t, number * group, group) for number in range(groups) for t in range(3))]
    )


def back(size, lengths, skip, vec, gtop, arrays):
    width, inner = arrays["wh"].shape
    rows = arrays["x"].shape[0]
    planes = size // 8
    half = size // 2
    like = jax.ShapeDtypeStruct
    smem, vmem, any_ = (pl.BlockSpec(memory_space=m) for m in (pltpu.SMEM, VMEM, pl.ANY))
    padded = -(-LIVE // 128) * 128
    keep = {"g": padded, "q": padded, **dict.fromkeys(("wq", "wk", "wv", "wo", "wh", "wp"), 0)}
    held = []
    for name in BACK_INPUTS:
        a = arrays[name]
        n = keep.get(name, LIVE) or a.shape[0]
        held.append(VMEM((n, a.shape[1]), a.dtype))
    shapes = [(width // size, width)] * 4 + [(width // size, inner), (inner // size, width)]
    lands = lambda many: [VMEM((many * r, w), BF16) for r, w in shapes]
    pair = 2 * width // HEADS
    numbers = 5 + 3 * (width // (2 * pair)) + 1
    spots = half + 4 * planes - 1
    return pl.pallas_call(
        functools.partial(back_kernel, size),
        out_shape=[like((rows, width), F32), *[like(s, F32) for s in shapes], like((16, width), F32)],
        in_specs=[smem, smem, vmem, vmem] + [any_] * len(BACK_INPUTS),
        out_specs=[any_] * 8,
        scratch_shapes=[
            *held,
            VMEM((width, LIVE), BF16), VMEM((2, LIVE, pair), BF16), VMEM((2, LIVE, pair), BF16),
            VMEM((LIVE, 128), F32), VMEM((LIVE, pair), F32), VMEM((LIVE, pair), F32),
            *lands(half), *lands(half // 2), *lands(planes), *lands(planes - 1),
            *[VMEM(s, F32) for s in shapes],
            VMEM((5, 16, width), F32), VMEM((3 + planes - 1, 16, width), F32),
            pltpu.SemaphoreType.DMA((numbers, spots)), pltpu.SemaphoreType.DMA((numbers, spots)),
            pltpu.SemaphoreType.DMA((numbers,)), pltpu.SemaphoreType.DMA((len(BACK_INPUTS),)),
            pltpu.SemaphoreType.DMA((2,)),
        ],
        compiler_params=pltpu.CompilerParams(collective_id=1, has_side_effects=True, vmem_limit_bytes=67043328),
        name="back",
    )(lengths, skip, vec, gtop, *[arrays[n] for n in BACK_INPUTS])


def finish_kernel(size, count, *refs):
    sums, matrices, pieces, outs = refs[0], refs[1 : 1 + count], refs[1 + count : 10 + count], refs[10 + count :]
    for a, b in zip(matrices, outs):
        b[...] = a[...]
    me = lax.axis_index("fsdp")
    width = sums.shape[1]
    piece = width // size

    def pick(value, first):
        lane = lax.broadcasted_iota(jnp.int32, (width, 128), 1)
        entry = lax.broadcasted_iota(jnp.int32, (width, 128), 0)
        one = jnp.where(entry == lane + first, 1.0, 0.0)
        return lax.dot_general(
            value, one, (((1,), (0,)), ((), ())), precision=lax.Precision.HIGHEST, preferred_element_type=F32
        )

    short = pick(sums[0:8, :], me * piece)
    for k in range(8):
        pieces[k][...] = short[k, :piece]
    long = pieces[8].shape[0]
    each = width // long
    row = lax.broadcasted_iota(jnp.int32, (8, width), 0)
    chosen = jnp.sum(jnp.where(row == me // each, sums[8:16, :], 0.0), 0, keepdims=True)
    spread = pick(jnp.broadcast_to(chosen, (8, width)), lax.rem(me, each) * long)
    pieces[8][...] = spread[0, :long]


def finish(size, sums, matrices):
    width = sums.shape[1]
    like = jax.ShapeDtypeStruct
    vmem = pl.BlockSpec(memory_space=VMEM)
    piece = width // size
    inner = matrices[4].shape[1]
    return pl.pallas_call(
        functools.partial(finish_kernel, size, len(matrices)),
        out_shape=[*[like((piece,), F32)] * 8, like((inner // size,), F32), *[like(m.shape, m.dtype) for m in matrices]],
        in_specs=[vmem] * (1 + len(matrices)),
        out_specs=[vmem] * (9 + len(matrices)),
        compiler_params=pltpu.CompilerParams(vmem_limit_bytes=40 << 20),
        name="finish",
    )(sums, *matrices)


def local(
    size,
    inputs,
    cotangent,
    lengths,
    skip_bit,
    w_query,
    w_key,
    w_value,
    w_out,
    b_query,
    b_value,
    b_out,
    ln1_gain,
    ln1_bias,
    w_hidden,
    b_hidden,
    w_proj,
    b_proj,
    ln2_gain,
    ln2_bias,
):
    vectors = [b_query, b_value, b_out, ln1_gain, ln1_bias, b_proj, ln2_gain, ln2_bias, b_hidden]
    weights = [w_query, w_key, w_value, w_out, w_hidden, w_proj]
    (
        q, k, v, att, z1, n1, inv1, g, slope, dh2, df, outputs,
        query_full, key_full, value_full, out_full, hidden_full, proj_full, vec, gtop,
    ) = front(size, lengths, skip_bit, inputs, cotangent, weights, vectors)
    grad_inputs, *matrices, sums = back(
        size, lengths, skip_bit, vec, gtop,
        {
            "df": df, "g": g, "wp": proj_full, "slope": slope, "wh": hidden_full, "dh2": dh2, "z1": z1,
            "wo": out_full, "n1": n1, "inv1": inv1, "att": att, "k": k, "v": v, "q": q, "x": inputs,
            "wq": query_full, "wk": key_full, "wv": value_full, "cot": cotangent,
        },
    )
    (
        g_b_query, g_b_value, g_b_out, g_ln1_gain, g_ln1_bias, g_b_proj, g_ln2_gain, g_ln2_bias, g_b_hidden,
        g_w_query, g_w_key, g_w_value, g_w_out, g_w_hidden, g_w_proj,
    ) = finish(size, sums, matrices)
    return (
        outputs,
        grad_inputs,
        g_w_query,
        g_w_key,
        g_w_value,
        g_w_out,
        g_b_query,
        g_b_value,
        g_b_out,
        g_ln1_gain,
        g_ln1_bias,
        g_w_hidden,
        g_b_hidden,
        g_w_proj,
        g_b_proj,
        g_ln2_gain,
        g_ln2_bias,
    )


def local_plain(
    inputs,
    cotangent,
    lengths,
    skip_bit,
    w_query,
    w_key,
    w_value,
    w_out,
    b_query,
    b_value,
    b_out,
    ln1_gain,
    ln1_bias,
    w_hidden,
    b_hidden,
    w_proj,
    b_proj,
    ln2_gain,
    ln2_bias,
):
    (
        query_full, key_full, value_full, out_full, hidden_full, proj_full,
        bq_full, bv_full, bo_full, gain_one, shift_one, bh_full, bp_full, gain_two, shift_two,
    ) = [
        lax.all_gather(p, "fsdp", axis=0, tiled=True)
        for p in (
            w_query, w_key, w_value, w_out, w_hidden, w_proj,
            b_query, b_value, b_out, ln1_gain, ln1_bias, b_hidden, b_proj, ln2_gain, ln2_bias,
        )
    ]
    row = lambda v: as_float(v)[None, :]
    q, k, v, att = attend(
        lengths, inputs, query_full, key_full, value_full, row(bq_full), row(bv_full)
    )
    vec = jnp.stack([as_float(v_) for v_ in (bo_full, gain_one, shift_one, bp_full, gain_two, shift_two)])
    vec = jnp.pad(vec, ((0, 2), (0, 0)))
    outputs, dh1, da, d_weight_out, d_weight_hidden, d_weight_proj, gvec, gbh = middle(
        lengths, skip_bit, inputs, att, cotangent, out_full, hidden_full, proj_full, vec, row(bh_full)
    )
    grad_inputs, d_weight_query, d_weight_key, d_weight_value, gbq, gbv = attend_back(
        lengths, inputs, dh1, q, k, v, da, query_full, key_full, value_full, cotangent, skip_bit
    )
    (
        g_w_query, g_w_key, g_w_value, g_w_out, g_w_hidden, g_w_proj,
        g_b_query, g_b_value, g_b_out, g_ln1_gain, g_ln1_bias,
        g_b_hidden, g_b_proj, g_ln2_gain, g_ln2_bias,
    ) = [
        lax.psum_scatter(lax.optimization_barrier(as_float(grad)), "fsdp", scatter_dimension=0, tiled=True)
        for grad in (
            d_weight_query, d_weight_key, d_weight_value, d_weight_out, d_weight_hidden, d_weight_proj,
            gbq[0], gbv[0], gvec[0], gvec[1], gvec[2], gbh[0], gvec[3], gvec[4], gvec[5],
        )
    ]
    return (
        outputs,
        grad_inputs,
        g_w_query,
        g_w_key,
        g_w_value,
        g_w_out,
        g_b_query,
        g_b_value,
        g_b_out,
        g_ln1_gain,
        g_ln1_bias,
        g_w_hidden,
        g_b_hidden,
        g_w_proj,
        g_b_proj,
        g_ln2_gain,
        g_ln2_bias,
    )


def solution(mesh):
    size = mesh.shape["fsdp"]
    placed = (
        P("fsdp", None),
        P("fsdp", None),
        P("fsdp"),
        P("fsdp"),
        P("fsdp", None),
        P("fsdp", None),
        P("fsdp", None),
        P("fsdp", None),
        P("fsdp"),
        P("fsdp"),
        P("fsdp"),
        P("fsdp"),
        P("fsdp"),
        P("fsdp", None),
        P("fsdp"),
        P("fsdp", None),
        P("fsdp"),
        P("fsdp"),
        P("fsdp"),
    )
    return jax.shard_map(
        functools.partial(local, size) if size == 32 else local_plain,
        mesh=mesh,
        in_specs=placed,
        out_specs=(
            P("fsdp", None),
            P("fsdp", None),
            P("fsdp", None),
            P("fsdp", None),
            P("fsdp", None),
            P("fsdp", None),
            P("fsdp"),
            P("fsdp"),
            P("fsdp"),
            P("fsdp"),
            P("fsdp"),
            P("fsdp", None),
            P("fsdp"),
            P("fsdp", None),
            P("fsdp"),
            P("fsdp"),
            P("fsdp"),
        ),
        check_vma=False,
    )
```

```python
import functools
import math

import jax
import jax.numpy as jnp
from jax import lax
from jax.experimental import pallas as pl
from jax.experimental.pallas import tpu as pltpu
from jax.sharding import PartitionSpec as P

HEADS = 12
LIVE = 800
EPSILON = 1e-05
NEG_FILL = -1e30
NT = (((1,), (1,)), ((), ()))
TN = (((0,), (0,)), ((), ()))
VMEM = pltpu.VMEM
F32, BF16 = jnp.float32, jnp.bfloat16


def dot(a, b, dims=(((1,), (0,)), ((), ()))):
    return lax.dot_general(a, b, dims, preferred_element_type=F32)


def lanes_of(shape, head, dim):
    lane = lax.broadcasted_iota(jnp.int32, shape, 1)
    return (lane < dim) if head == 0 else (lane >= dim)


def attend_kernel(lengths, x, wq, wk, wv, bq, bv, q, k, v, att, keys, values):
    rows, width = x.shape
    dim = width // HEADS
    pair = 2 * dim
    group = 2 * pair
    step = 256
    key_lane = lax.broadcasted_iota(jnp.int32, (1, LIVE), 1)
    bias = jnp.where(key_lane < lengths[0], 0.0, NEG_FILL).astype(F32)
    for head in range(2):
        values[head, :, pair:] = jnp.ones((LIVE, pair), BF16)
    for first in range(0, width, group):
        cols = pl.ds(first, group)

        @pl.loop(0, rows // step)
        def _(part):
            at = pl.ds(pl.multiple_of(part * step, step), step)
            here = x[at, :]
            q[at, cols] = ((dot(here, wq[:, cols]) + bq[:, cols]).astype(BF16).astype(F32) * (1.0 / math.sqrt(dim))).astype(BF16)
            k[at, cols] = dot(here, wk[:, cols]).astype(BF16)
            v[at, cols] = (dot(here, wv[:, cols]) + bv[:, cols]).astype(BF16)

        for start in range(first, first + group, pair):
            wide = pl.ds(start, pair)
            whole = k[:LIVE, wide]
            for head in range(2):
                keys[head] = jnp.where(lanes_of(whole.shape, head, dim), whole, jnp.zeros_like(whole))
                values[head, :, :pair] = v[:LIVE, wide]

            @pl.loop(0, rows // step)
            def _(part):
                at = pl.ds(pl.multiple_of(part * step, step), step)
                here = q[at, wide]
                outs = []
                for head in range(2):
                    s = dot(here, keys[head], NT) + bias
                    e = jnp.exp(s - jnp.max(s, -1, keepdims=True))
                    o = dot(e.astype(BF16), values[head])
                    outs.append(o[:, :pair] / o[:, pair:])
                att[at, wide] = jnp.where(lanes_of(outs[0].shape, 0, dim), outs[0], outs[1]).astype(BF16)


def attend(lengths, x, wq, wk, wv, bq, bv):
    rows, width = x.shape
    pair = 2 * width // HEADS
    return pl.pallas_call(
        attend_kernel,
        out_shape=[jax.ShapeDtypeStruct(x.shape, BF16)] * 4,
        in_specs=[pl.BlockSpec(memory_space=pltpu.SMEM)] + [pl.BlockSpec(memory_space=VMEM)] * 6,
        out_specs=[pl.BlockSpec(memory_space=VMEM)] * 4,
        scratch_shapes=[VMEM((2, LIVE, pair), BF16), VMEM((2, LIVE, 2 * pair), BF16)],
        compiler_params=pltpu.CompilerParams(vmem_limit_bytes=60 << 20),
        name="attend",
    )(lengths, x, wq, wk, wv, bq, bv)


def attend_back_kernel(lengths, x, dh1, q, k, v, da, wq, wk, wv, cot, skip, gin, gwq, gwk, gwv, gbq, gbv,
                       dq, dk, dv, keys, values, bias, dk_acc, dv_acc):
    rows, width = x.shape
    dim = width // HEADS
    pair = 2 * dim
    chunk = 256
    tops = [(c, min(chunk, -(-LIVE // 128) * 128 - c)) for c in range(0, LIVE, chunk)]
    key_row = lax.broadcasted_iota(jnp.int32, (LIVE, 128), 0)
    bias[...] = jnp.where(key_row < lengths[0], 0.0, NEG_FILL).astype(F32)
    dk[...] = jnp.zeros_like(dk)
    dv[...] = jnp.zeros_like(dv)

    def block(wide, start, size):
        at = pl.ds(start, size)
        q_c, da_c = q[at, wide], da[at, wide]
        dq_c = jnp.zeros((size, pair), F32)
        for head in range(2):
            mine = lanes_of(q_c.shape, head, dim)
            s = dot(keys[head], q_c, NT) + jnp.tile(bias[...], (1, size // 128))
            e = jnp.exp(s - jnp.max(s, 0, keepdims=True))
            p = e * (1.0 / jnp.sum(e, 0, keepdims=True))
            dp = dot(values[head], da_c, NT)
            t = p * dp
            ds = (t - p * jnp.sum(t, 0, keepdims=True)).astype(BF16)
            dv_acc[...] += dot(p.astype(BF16), jnp.where(mine, da_c, jnp.zeros_like(da_c)))
            dk_acc[...] += dot(ds, jnp.where(mine, q_c, jnp.zeros_like(q_c)))
            dq_c = dq_c + dot(ds, keys[head], TN)
        dq[at, wide] = (dq_c * (1.0 / math.sqrt(dim))).astype(BF16)

    @pl.loop(0, width // pair)
    def _(which):
        wide = pl.ds(pl.multiple_of(which * pair, pair), pair)
        whole, whole_v = k[:LIVE, wide], v[:LIVE, wide]
        for head in range(2):
            mine = lanes_of(whole.shape, head, dim)
            keys[head] = jnp.where(mine, whole, jnp.zeros_like(whole))
            values[head] = jnp.where(mine, whole_v, jnp.zeros_like(whole_v))
        dk_acc[...] = jnp.zeros_like(dk_acc)
        dv_acc[...] = jnp.zeros_like(dv_acc)

        @pl.loop(0, LIVE // chunk)
        def _(part):
            block(wide, pl.multiple_of(part * chunk, chunk), chunk)

        for start, size in tops:
            if size < chunk:
                block(wide, start, size)
        dk[:LIVE, wide] = dk_acc[...].astype(BF16)
        dv[:LIVE, wide] = dv_acc[...].astype(BF16)

    gbq[...] = jnp.sum(dq[:LIVE, :].astype(F32), 0, keepdims=True)
    gbv[...] = jnp.sum(dv[:LIVE, :].astype(F32), 0, keepdims=True)
    here = x[:LIVE, :]
    for grad, out in ((dq, gwq), (dk, gwk), (dv, gwv)):
        for start in range(0, width, 256):
            cols = pl.ds(start, 256)
            out[:, cols] = dot(here, grad[:LIVE, cols], TN).astype(BF16)
    step = 160

    @pl.loop(0, LIVE // step)
    def _(part):
        at = pl.ds(pl.multiple_of(part * step, step), step)
        total = dh1[at, :] + dot(dq[at, :], wq[...], NT)
        total = total + dot(dk[at, :], wk[...], NT)
        total = total + dot(dv[at, :], wv[...], NT)
        row = lax.broadcasted_iota(jnp.int32, (step, 1), 0) + part * step
        dropped = jnp.where(row < lengths[0], cot[at, :].astype(F32), 0.0)
        gin[at, :] = jnp.where(skip[0] == 1, dropped, total)

    gin[LIVE:, :] = jnp.zeros((rows - LIVE, width), F32)


def attend_back(lengths, x, dh1, q, k, v, da, wq, wk, wv, cot, skip):
    rows, width = x.shape
    pair = 2 * width // HEADS
    like = jax.ShapeDtypeStruct
    smem = pl.BlockSpec(memory_space=pltpu.SMEM)
    return pl.pallas_call(
        attend_back_kernel,
        out_shape=[like((rows, width), F32)] + [like((width, width), BF16)] * 3 + [like((1, width), F32)] * 2,
        in_specs=[smem] + [pl.BlockSpec(memory_space=VMEM)] * 10 + [smem],
        out_specs=[pl.BlockSpec(memory_space=VMEM)] * 6,
        scratch_shapes=[VMEM(x.shape, BF16)] * 3
        + [VMEM((2, LIVE, pair), BF16)] * 2
        + [VMEM((LIVE, 128), F32)]
        + [VMEM((LIVE, pair), F32)] * 2,
        compiler_params=pltpu.CompilerParams(vmem_limit_bytes=62 << 20),
        name="attend_back",
    )(lengths, x, dh1, q, k, v, da, wq, wk, wv, cot, skip)


def middle_kernel(lengths, skip, x_in, att_in, cot_in, wo_in, wh_in, wp_in, vec, bh,
                  outputs, dh1, da, gwo, gwh, gwp, gvec, gbh,
                  x, att, cot, wo, wh, wp, z1, n1, inv1, f, g, slope, df, z1t, out_h, out_p, load_sem, out_sem):
    rows, width = x.shape
    inner = wh.shape[1]
    loads = [
        pltpu.make_async_copy(a, b, load_sem.at[i])
        for i, (a, b) in enumerate(
            ((x_in, x), (att_in, att), (wo_in, wo), (wh_in, wh), (wp_in, wp), (cot_in, cot))
        )
    ]
    for load in loads:
        load.start()
    bo, gain1, shift1, bp, gain2, shift2 = (vec[i : i + 1, :] for i in range(6))
    for load in loads[:3]:
        load.wait()
    step = 256

    def norm(h):
        centred = h - jnp.mean(h, -1, keepdims=True)
        inv = lax.rsqrt(jnp.mean(centred * centred, -1, keepdims=True) + EPSILON)
        return centred * inv, inv

    def norm_back(e, n, inv):
        return inv * (e - jnp.mean(e, -1, keepdims=True) - n * jnp.mean(e * n, -1, keepdims=True))

    @pl.loop(0, rows // step)
    def _(part):
        at = pl.ds(pl.multiple_of(part * step, step), step)
        h = x[at, :].astype(F32) + (dot(att[at, :], wo[...]) + bo)
        n, inv = norm(h)
        n1[at, :] = n
        inv1[at, :] = jnp.broadcast_to(inv, (step, 128))
        z1[at, :] = (n * gain1 + shift1).astype(BF16)

    loads[3].wait()
    loads[4].wait()
    f[...] = jnp.zeros_like(f)
    wide = 256

    @pl.loop(0, inner // wide)
    def _(block):
        cols = pl.ds(pl.multiple_of(block * wide, wide), wide)
        b = bh[:, cols]
        for start in range(0, rows, step):
            at = pl.ds(start, step)
            u = dot(z1[at, :], wh[:, cols]) + b
            phi = 0.5 * (1.0 + lax.erf(u * 0.7071067811865476))
            g[at, cols] = (u * phi).astype(BF16)
            slope[at, cols] = (phi + u * (jnp.exp(-0.5 * u * u) * 0.3989422804014327)).astype(BF16)
            f[at, :] += dot(g[at, cols], wp[cols, :])

    loads[5].wait()
    gvec[...] = jnp.zeros_like(gvec)
    keep = 1.0 - skip[0].astype(F32)

    @pl.loop(0, rows // step)
    def _(part):
        at = pl.ds(pl.multiple_of(part * step, step), step)
        n, inv = norm(z1[at, :].astype(F32) + (f[at, :] + bp))
        outputs[at, :] = jnp.where(skip[0] == 1, x[at, :], (n * gain2 + shift2).astype(BF16))
        row = lax.broadcasted_iota(jnp.int32, (step, 1), 0) + part * step
        dy = jnp.where(row < lengths[0], cot[at, :].astype(F32), 0.0) * keep
        d = norm_back(dy * gain2, n, inv)
        low = d.astype(BF16)
        f[at, :] = d
        df[at, :] = low
        gvec[3:4, :] += jnp.sum(low.astype(F32), 0, keepdims=True)
        gvec[4:5, :] += jnp.sum(dy * n, 0, keepdims=True)
        gvec[5:6, :] += jnp.sum(dy, 0, keepdims=True)

    z1t[...] = z1[:LIVE, :].T

    def flush(block, buf, slot):
        cols = pl.ds(pl.multiple_of(block * wide, wide), wide)
        if buf is out_h:
            return pltpu.make_async_copy(buf.at[slot], gwh.at[:, cols], out_sem.at[0, slot])
        return pltpu.make_async_copy(buf.at[slot], gwp.at[cols, :], out_sem.at[1, slot])

    @pl.loop(0, inner // wide)
    def _(block):
        slot = lax.rem(block, 2)
        cols = pl.ds(pl.multiple_of(block * wide, wide), wide)

        @pl.when(block >= 2)
        def _():
            flush(block, out_h, slot).wait()
            flush(block, out_p, slot).wait()

        out_p[slot] = dot(g[:LIVE, cols], df[:LIVE, :], TN).astype(BF16)
        flush(block, out_p, slot).start()
        total = jnp.zeros((1, wide), F32)
        half = LIVE // 2
        for start in range(0, LIVE, half):
            at = pl.ds(start, half)
            du = (dot(df[at, :], wp[cols, :], NT) * slope[at, cols].astype(F32)).astype(BF16)
            total = total + jnp.sum(du.astype(F32), 0, keepdims=True)
            g[at, cols] = du
            f[at, :] += dot(du, wh[:, cols], NT)
        gbh[:, cols] = total
        out_h[slot] = dot(z1t[...], g[:LIVE, cols]).astype(BF16)
        flush(block, out_h, slot).start()

    half = LIVE // 5
    @pl.loop(0, LIVE // half)
    def _(part):
        at = pl.ds(pl.multiple_of(part * half, half), half)
        dz = f[at, :]
        n = n1[at, :]
        gvec[1:2, :] += jnp.sum(dz * n, 0, keepdims=True)
        gvec[2:3, :] += jnp.sum(dz, 0, keepdims=True)
        d = norm_back(dz * gain1, n, inv1[at, :1])
        dh1[at, :] = d
        low = d.astype(BF16)
        df[at, :] = low
        gvec[0:1, :] += jnp.sum(low.astype(F32), 0, keepdims=True)
        da[at, :] = dot(low, wo[...], NT).astype(BF16)

    da[LIVE:, :] = jnp.zeros((rows - LIVE, width), BF16)
    for start in range(0, width, wide):
        cols = pl.ds(start, wide)
        gwo[cols, :] = dot(att[:LIVE, cols], df[:LIVE, :], TN).astype(BF16)
    for block in (inner // wide - 2, inner // wide - 1):
        flush(block, out_h, block % 2).wait()
        flush(block, out_p, block % 2).wait()


def middle(lengths, skip, x, att, cot, wo, wh, wp, vec, bh):
    rows, width = x.shape
    inner = wh.shape[1]
    like = jax.ShapeDtypeStruct
    smem, vmem, any_ = (pl.BlockSpec(memory_space=m) for m in (pltpu.SMEM, VMEM, pl.ANY))
    pad = -(-LIVE // 128) * 128
    return pl.pallas_call(
        middle_kernel,
        out_shape=[
            like((rows, width), BF16), like((LIVE, width), F32), like((rows, width), BF16),
            like((width, width), BF16), like((width, inner), BF16), like((inner, width), BF16),
            like((8, width), F32), like((1, inner), F32),
        ],
        in_specs=[smem] * 2 + [any_] * 6 + [vmem] * 2,
        out_specs=[vmem] * 4 + [any_] * 2 + [vmem] * 2,
        scratch_shapes=[
            VMEM((rows, width), BF16), VMEM((rows, width), BF16), VMEM((rows, width), BF16),
            VMEM((width, width), BF16), VMEM((width, inner), BF16), VMEM((inner, width), BF16),
            VMEM((rows, width), BF16), VMEM((rows, width), F32), VMEM((rows, 128), F32),
            VMEM((rows, width), F32), VMEM((rows, inner), BF16), VMEM((rows, inner), BF16),
            VMEM((rows, width), BF16), VMEM((width, LIVE), BF16),
            VMEM((2, width, 256), BF16), VMEM((2, 256, width), BF16),
            pltpu.SemaphoreType.DMA((6,)), pltpu.SemaphoreType.DMA((2, 2)),
        ],
        compiler_params=pltpu.CompilerParams(vmem_limit_bytes=63 << 20),
        name="middle",
    )(lengths, skip, x, att, cot, wo, wh, wp, vec, bh)


def as_float(value):
    return value.astype(jnp.float32)


MESH = pl.DeviceIdType.MESH


def place(me, planes):
    core = lax.rem(me, 2)
    chip = me // 2
    col = lax.rem(chip, 2)
    row = lax.rem(chip // 2, 2)
    plane = chip // 4
    near = jnp.where(core == 0, row, col)
    far = jnp.where(core == 0, col, row)

    def index(plane_, near_, far_, core_):
        row_ = jnp.where(core_ == 0, near_, far_)
        col_ = jnp.where(core_ == 0, far_, near_)
        return ((plane_ * 2 + row_) * 2 + col_) * 2 + core_

    return core, near, far, plane, index


def greet(peers):
    barrier = pltpu.get_barrier_semaphore()
    for peer in peers:
        pl.semaphore_signal(barrier, inc=1, device_id=(peer,), device_id_type=MESH)
    pl.semaphore_wait(barrier, len(peers))


class Gather:
    def __init__(self, items, planes, send_sem, recv_sem, local_sem):
        self.items = items
        self.planes = planes
        self.sems = send_sem, recv_sem, local_sem
        me = lax.axis_index("fsdp")
        self.core, self.near, self.far, self.plane, self.index = place(me, planes)
        self.other = self.index(self.plane, self.far, self.near, 1 - self.core)
        self.near_peer = self.index(self.plane, 1 - self.near, self.far, self.core)
        self.far_peer = self.index(self.plane, self.near, 1 - self.far, self.core)
        self.plane_peers = [
            self.index(lax.rem(self.plane + step, planes), self.near, self.far, self.core) for step in range(1, planes)
        ]
        self.spots = [
            self.index(0, n, f, self.core) for n, f in (
                (self.near, self.far), (1 - self.near, self.far), (self.near, 1 - self.far), (1 - self.near, 1 - self.far)
            )
        ]
        greet([self.other, self.near_peer, self.far_peer, *self.plane_peers])

    def column(self, number, spot, plane=slice(None)):
        own, full, cols = self.items[number]
        if cols is None:
            return full.at[plane, spot]
        rows = own.shape[0]
        view = full.reshape(self.planes, full.shape[0] // self.planes, full.shape[1])
        return view.at[plane, pl.ds(pl.multiple_of(spot * rows, 8), rows), cols]

    def push(self, number, src, dst, spot, peer):
        pltpu.make_async_remote_copy(
            src_ref=src, dst_ref=dst, send_sem=self.sems[0].at[number, spot], recv_sem=self.sems[1].at[number, spot],
            device_id=(peer,), device_id_type=MESH,
        ).start()

    def landed(self, number, spot, whole=False):
        where = self.column(number, self.spots[0], slice(None) if whole else 0)
        pltpu.make_async_copy(where, where, self.sems[1].at[number, spot]).wait()

    def stage(self, which, number):
        planes = self.planes
        near0, far0, other0, wide0 = (planes - 1 + n * planes for n in range(4))
        mine, near, far, both = self.spots
        own, full, cols = self.items[number]
        src = own if cols is None else own.at[:, cols]
        sides = ((near0, self.near_peer), (far0, self.far_peer), (other0, self.other))
        if which == 1:
            here = self.column(number, mine, self.plane)
            for step, peer in enumerate(self.plane_peers):
                self.push(number, src, here, step, peer)
            pltpu.make_async_copy(src, here, self.sems[2].at[number]).start()
        elif which == 6:
            for base, peer in sides:
                self.push(number, src, self.column(number, mine, self.plane), base, peer)
        elif which == 2:
            for step in range(1, planes):
                self.landed(number, step - 1)
                here = self.column(number, mine, lax.rem(self.plane + planes - step, planes))
                for base, peer in sides:
                    self.push(number, here, here, base + step, peer)
        elif which == 3:
            for step in range(planes):
                self.landed(number, near0 + step)
            where = self.column(number, near)
            self.push(number, where, where, wide0, self.far_peer)
            self.push(number, where, where, wide0 + 1, self.other)
        elif which == 4:
            for step in range(planes):
                self.landed(number, far0 + step)
            where = self.column(number, far)
            self.push(number, where, where, wide0 + 2, self.other)
            self.landed(number, wide0, True)
            where = self.column(number, both)
            self.push(number, where, where, wide0 + 3, self.other)
        else:
            for step in range(planes):
                self.landed(number, other0 + step)
            for spot in range(1, 4):
                self.landed(number, wide0 + spot, True)
            here = self.column(number, mine, 0)
            pltpu.make_async_copy(here, here, self.sems[2].at[number]).wait()

    def finish(self):
        for number in range(len(self.items)):
            for spot in range(4 * self.planes + 3):
                where = self.column(number, self.spots[0], 0 if spot < 4 * self.planes - 1 else slice(None))
                pltpu.make_async_copy(where, where, self.sems[0].at[number, spot]).wait()


def unpack(packed, vec, bh, size):
    width, inner = vec.shape[1], bh.shape[1]
    piece, long = width // size, inner // size

    def pick(row, part, start):
        flat = packed[:, :, row, :].reshape(size, 128).astype(BF16)
        lane = lax.rem(lax.broadcasted_iota(jnp.int32, (128, width), 1) + start, part)
        entry = lax.broadcasted_iota(jnp.int32, (128, width), 0)
        spread = dot(flat, jnp.where(entry == lane, 1.0, 0.0).astype(BF16))
        lane = lax.broadcasted_iota(jnp.int32, (size, width), 1) + start
        owner = lax.broadcasted_iota(jnp.int32, (size, width), 0)
        return jnp.sum(jnp.where(lane - lax.rem(lane, part) == part * owner, spread, 0.0), 0, keepdims=True)

    for k in range(8):
        vec[k : k + 1, :] = pick(k, piece, 0)
    for start in range(0, inner, width):
        bh[:, start : start + width] = pick(8, long, start)


def norm(h):
    centred = h - jnp.mean(h, -1, keepdims=True)
    inv = lax.rsqrt(jnp.mean(centred * centred, -1, keepdims=True) + EPSILON)
    return centred * inv, inv


def norm_back(e, n, inv):
    return inv * (e - jnp.mean(e, -1, keepdims=True) - n * jnp.mean(e * n, -1, keepdims=True))


FRONT_SAVED = ("qkv", "att_t", "z1_t", "x_t", "n1", "inv1", "g_t", "slope", "dh2", "df", "outputs", "wqkv", "wo", "wh", "wp")


TURNS = {
    "init": "60 61 62 63 64 65 66 67 68 69 610 611 20 21 22 30 31 23 32 40 33 41 50",
    "proj0": "24", "p0.0": "51", "p0.3": "42 34 25", "p1.1": "52 43", "p1.3": "35 26", "proj2": "53", "p2.0": "44",
    "p2.2": "36 27", "p2.3": "54", "p3.0": "45", "p3.2": "37 28", "p3.3": "55", "p4.0": "46 29", "p4.1": "38",
    "p4.3": "56", "p5.0": "210", "p5.1": "47 39", "p5.3": "211", "tr": "57", "out": "310", "ff0": "311", "ff1": "48",
    "ff4": "58", "ff6": "49", "ff9": "59", "ff11": "410", "fp0": "411 510", "fp1": "511",
}


def front_kernel(size, lengths, skip, x_in, cot_in, *refs):
    refs = list(refs)

    def take(n):
        out = refs[:n]
        del refs[:n]
        return out

    vectors = take(9)
    wq_own, wk_own, wv_own, wo_own, wh_own, wp_own = take(6)
    saved = dict(zip(FRONT_SAVED, take(len(FRONT_SAVED))))
    vec, gvec = take(2)
    (x, cot, qkv, att, z1, n1, inv1, g, slope, f, outputs, df, x_t, att_t, z1_t, g_t) = take(16)
    wqkv, wo, wh, wp, packed = take(5)
    bh, keys, values, mine, qkv_own, send_sem, recv_sem, local_sem, load_sem, save_sem = refs
    rows, width = x.shape
    inner = wh.shape[1]
    dim = width // HEADS
    pair = 2 * dim
    group = 2 * pair
    count = width // pair
    step = 256
    parts = rows // step
    loads = [(x_in, x), (cot_in, cot)]
    for number in range(count):
        for w, own in enumerate((wq_own, wk_own, wv_own)):
            loads.append((own.at[:, pl.ds(number * pair, pair)], qkv_own.at[:, pl.ds((3 * number + w) * pair, pair)]))
    loads = [pltpu.make_async_copy(a, b, load_sem.at[i]) for i, (a, b) in enumerate(loads)]
    for load in [*loads[2:], *loads[:2]]:
        load.start()
    mine[...] = jnp.zeros_like(mine)
    for row, piece in enumerate(vectors):
        mine[row, : piece.shape[0]] = piece[...].astype(F32)
    for load in loads[2:]:
        load.wait()
    spans = [(0, 1), (1, 1), *((p, 2) for p in range(2, count, 2))]
    items = [(qkv_own, wqkv, pl.ds(p * 3 * pair, n * 3 * pair)) for p, n in spans]
    items.append((wo_own, wo, pl.ds(0, width)))
    items += [(wh_own, wh, pl.ds(c, width)) for c in range(0, inner, width)]
    items += [(wp_own, wp, pl.ds(c, group)) for c in range(0, width, group)]
    vector_item = len(items)
    items.append((mine, packed, None))
    move = Gather(items, size // 8, send_sem, recv_sem, local_sem)

    def moves(text):
        for word in text.split():
            move.stage(int(word[0]), int(word[1:]))
            if word[1:] == "0":
                move.stage(int(word[0]), vector_item)

    saves = []

    def save(src, name):
        n = FRONT_SAVED.index(name)
        pltpu.make_async_copy(src, saved[name], save_sem.at[n]).start()
        saves.append((src, n))

    for number in range(vector_item):
        moves("1%d" % number)
    moves(TURNS["init"])
    unpack(packed, vec, bh, size)
    bq, bv, bo, gain1, shift1, bp, gain2, shift2 = (vec[i : i + 1, :] for i in range(8))
    loads[0].wait()
    key_lane = lax.broadcasted_iota(jnp.int32, (1, LIVE), 1)
    bias = jnp.where(key_lane < lengths[0], 0.0, NEG_FILL).astype(F32)
    for head in range(2):
        values[head, :, pair:] = jnp.ones((LIVE, pair), BF16)

    for first, many in spans:
        base = 3 * first * pair

        @pl.loop(0, parts)
        def _(part):
            at = pl.ds(pl.multiple_of(part * step, step), step)
            out = dot(x[at, :], wqkv[:, base : base + 3 * many * pair])
            for n in range(many):
                lane = 3 * n * pair
                to = base + lane
                real = (first + n) * pair
                query = (out[:, lane : lane + pair] + bq[:, real : real + pair]).astype(BF16)
                qkv[at, to : to + pair] = (query.astype(F32) * (1.0 / math.sqrt(dim))).astype(BF16)
                qkv[at, to + pair : to + 2 * pair] = out[:, lane + pair : lane + 2 * pair].astype(BF16)
                qkv[at, to + 2 * pair : to + 3 * pair] = (
                    out[:, lane + 2 * pair : lane + 3 * pair] + bv[:, real : real + pair]
                ).astype(BF16)

        moves(TURNS.get("proj%d" % first, ""))
        for number in range(first, first + many):
            start = 3 * number * pair
            wide = pl.ds(start, pair)
            whole = qkv[:LIVE, start + pair : start + 2 * pair]
            for head in range(2):
                keys[head] = jnp.where(lanes_of(whole.shape, head, dim), whole, jnp.zeros_like(whole))
                values[head, :, :pair] = qkv[:LIVE, start + 2 * pair : start + 3 * pair]
            to = pl.ds(number * pair, pair)

            @pl.loop(0, parts)
            def _(part):
                at = pl.ds(pl.multiple_of(part * step, step), step)
                here = qkv[at, wide]
                outs = []
                for head in range(2):
                    s = dot(here, keys[head], NT) + bias
                    e = jnp.exp(s - jnp.max(s, -1, keepdims=True))
                    o = dot(e.astype(BF16), values[head])
                    outs.append(o[:, :pair] / o[:, pair:])
                att[at, to] = jnp.where(lanes_of(outs[0].shape, 0, dim), outs[0], outs[1]).astype(BF16)
                for spot in range(parts):
                    if text := TURNS.get("p%d.%d" % (number, spot)):

                        @pl.when(part == spot)
                        def _():
                            moves(text)

    x_t[...] = x[:LIVE, :].T
    att_t[...] = att[:LIVE, :].T
    save(qkv, "qkv")
    save(x_t, "x_t")
    save(att_t, "att_t")
    save(wqkv, "wqkv")
    save(wo, "wo")
    moves(TURNS.get("tr", ""))

    @pl.loop(0, parts)
    def _(part):
        at = pl.ds(pl.multiple_of(part * step, step), step)
        h = x[at, :].astype(F32) + (dot(att[at, :], wo[...]) + bo)
        n, inv = norm(h)
        n1[at, :] = n
        inv1[at, :] = jnp.broadcast_to(inv, (step, 128))
        z1[at, :] = (n * gain1 + shift1).astype(BF16)

    z1_t[...] = z1[:LIVE, :].T
    save(z1_t, "z1_t")
    save(n1.at[pl.ds(0, LIVE)], "n1")
    save(inv1.at[pl.ds(0, LIVE)], "inv1")
    moves(TURNS.get("out", ""))

    @pl.loop(0, inner // step)
    def _(block):
        cols = pl.ds(pl.multiple_of(block * step, step), step)
        b = bh[:, cols]
        for start in range(0, rows, step):
            at = pl.ds(start, step)
            u = dot(z1[at, :], wh[:, cols]) + b
            phi = 0.5 * (1.0 + lax.erf(u * 0.7071067811865476))
            g[at, cols] = (u * phi).astype(BF16)
            if start < LIVE:
                slope[at, cols] = (phi + u * (jnp.exp(-0.5 * u * u) * 0.3989422804014327)).astype(BF16)
        g_t[cols, :] = g[:LIVE, cols].T

        for spot in range(inner // step):
            if text := TURNS.get("ff%d" % spot):

                @pl.when(block == spot)
                def _():
                    moves(text)

    save(g_t, "g_t")
    save(slope.at[pl.ds(0, LIVE)], "slope")
    save(wh, "wh")
    for first in range(0, width, group):
        moves(TURNS.get("fp%d" % (first // group - 1), ""))
        cols = pl.ds(first, group)

        @pl.loop(0, parts)
        def _(part):
            at = pl.ds(pl.multiple_of(part * step, step), step)
            f[at, cols] = dot(g[at, :], wp[:, cols])

    save(wp, "wp")
    loads[1].wait()
    gvec[...] = jnp.zeros_like(gvec)
    keep = 1.0 - skip[0].astype(F32)

    @pl.loop(0, parts)
    def _(part):
        at = pl.ds(pl.multiple_of(part * step, step), step)
        n, inv = norm(z1[at, :].astype(F32) + (f[at, :] + bp))
        outputs[at, :] = jnp.where(skip[0] == 1, x[at, :], (n * gain2 + shift2).astype(BF16))
        row = lax.broadcasted_iota(jnp.int32, (step, 1), 0) + part * step
        dy = jnp.where(row < lengths[0], cot[at, :].astype(F32), 0.0) * keep
        d = norm_back(dy * gain2, n, inv)
        low = d.astype(BF16)
        f[at, :] = d
        df[at, :] = low
        gvec[5:6, :] += jnp.sum(low.astype(F32), 0, keepdims=True)
        gvec[6:7, :] += jnp.sum(dy * n, 0, keepdims=True)
        gvec[7:8, :] += jnp.sum(dy, 0, keepdims=True)

    save(f.at[pl.ds(0, LIVE)], "dh2")
    save(df.at[pl.ds(0, LIVE)], "df")
    save(outputs, "outputs")
    for src, n in saves:
        pltpu.make_async_copy(src, src, save_sem.at[n]).wait()
    move.finish()


def front(size, lengths, skip, x, cot, weights, vectors):
    rows, width = x.shape
    inner = weights[4].shape[1]
    like = jax.ShapeDtypeStruct
    smem, vmem, any_ = (pl.BlockSpec(memory_space=m) for m in (pltpu.SMEM, VMEM, pl.ANY))
    saved = {
        "qkv": ((rows, 3 * width), BF16), "att_t": ((width, LIVE), BF16), "z1_t": ((width, LIVE), BF16),
        "x_t": ((width, LIVE), BF16), "n1": ((LIVE, width), F32), "inv1": ((LIVE, 128), F32),
        "g_t": ((inner, LIVE), BF16), "slope": ((LIVE, inner), BF16), "dh2": ((LIVE, width), F32),
        "df": ((LIVE, width), BF16), "outputs": ((rows, width), BF16), "wqkv": ((width, 3 * width), BF16),
        "wo": ((width, width), BF16), "wh": ((width, inner), BF16), "wp": ((inner, width), BF16),
    }
    pair = 2 * width // HEADS
    full = VMEM((rows, width), BF16)
    single = VMEM((rows, width), F32)
    turned = VMEM((width, LIVE), BF16)
    planes = size // 8
    items = 1 + width // (2 * pair) + 2 + inner // width + width // (2 * pair)
    out = pl.pallas_call(
        functools.partial(front_kernel, size),
        out_shape=[*[like(*saved[n]) for n in FRONT_SAVED], like((8, width), F32), like((8, width), F32)],
        in_specs=[smem, smem] + [any_] * 2 + [vmem] * 9 + [any_] * 6,
        out_specs=[any_] * len(FRONT_SAVED) + [vmem] * 2,
        scratch_shapes=[
            full, full, VMEM((rows, 3 * width), BF16), full, full, single, VMEM((rows, 128), F32),
            VMEM((rows, inner), BF16), VMEM((rows, inner), BF16), single, full, full,
            turned, turned, turned, VMEM((inner, LIVE), BF16),
            *[VMEM(saved[n][0], BF16) for n in ("wqkv", "wo", "wh", "wp")], VMEM((planes, size // planes, 16, 128), F32),
            VMEM((1, inner), F32), VMEM((2, LIVE, pair), BF16), VMEM((2, LIVE, 2 * pair), BF16),
            VMEM((16, 128), F32), VMEM((width // size, 3 * width), BF16),
            pltpu.SemaphoreType.DMA((items, 4 * planes + 3)),
            pltpu.SemaphoreType.DMA((items, 4 * planes + 3)),
            pltpu.SemaphoreType.DMA((items,)),
            pltpu.SemaphoreType.DMA((2 + 3 * (width // pair),)),
            pltpu.SemaphoreType.DMA((len(FRONT_SAVED),)),
        ],
        compiler_params=pltpu.CompilerParams(collective_id=0, has_side_effects=True, vmem_limit_bytes=67043328),
        name="front",
    )(lengths, skip, x, cot, *vectors, *weights)
    return dict(zip(FRONT_SAVED, out)), out[-2], out[-1]


class Scatter:
    def __init__(self, tensors, planes, send_sem, recv_sem, out_sem, vector):
        self.tensors = tensors
        self.planes = planes
        self.sems = send_sem, recv_sem, out_sem
        self.vector = vector
        me = lax.axis_index("fsdp")
        self.core, self.near, self.far, self.plane, self.index = place(me, planes)
        self.other = self.index(self.plane, self.far, self.near, 1 - self.core)
        self.near_peer = self.index(self.plane, 1 - self.near, self.far, self.core)
        self.far_peer = self.index(self.plane, self.near, 1 - self.far, self.core)
        self.others = [lax.rem(self.plane + step, planes) for step in range(1, planes)]
        self.plane_peers = [self.index(p, self.near, self.far, self.core) for p in self.others]
        away = ((1, 1), (0, 1), (1, 0), (0, 0))
        flip = lambda step, value: 1 - value if step else value
        self.ours = [self.index(0, flip(n, self.near), flip(f, self.far), self.core) for n, f in away]
        self.theirs = [self.index(0, flip(n, self.far), flip(f, self.near), 1 - self.core) for n, f in away]
        greet([self.other, self.near_peer, self.far_peer, *self.plane_peers])

    def push(self, src, dst, number, spot, peer):
        pltpu.make_async_remote_copy(
            src_ref=src, dst_ref=dst, send_sem=self.sems[0].at[number, spot],
            recv_sem=self.sems[1].at[number, spot], device_id=(peer,), device_id_type=MESH,
        ).start()

    def landed(self, ref, number, spot):
        pltpu.make_async_copy(ref, ref, self.sems[1].at[number, spot]).wait()

    def stage(self, which, tensor, number, start, many):
        part, got0, got1, got2, got3, final, result, rows = self.tensors[tensor]
        cols = pl.ds(start, many)
        planes = self.planes
        view = part.reshape(planes, part.shape[0] // planes, part.shape[1])

        def mine(place_, plane=slice(None)):
            return view.at[plane, pl.ds(pl.multiple_of(place_ * rows, 8), rows), cols]

        def land(ref, column):
            return ref.at[pl.ds(column * planes, planes), :, cols]

        def value(ref):
            return ref[...].astype(F32)

        if which == 0:
            for column in range(4):
                self.push(mine(self.theirs[column]), land(got0, column), number, column, self.other)
        elif which == 1:
            for column in range(2):
                self.landed(land(got0, column), number, column)
                here = mine(self.ours[column])
                here[...] = (value(here) + value(land(got0, column))).astype(BF16)
                self.push(here, land(got1, column), number, 4 + column, self.far_peer)
        elif which == 2:
            self.landed(land(got0, 2), number, 2)
            self.landed(land(got1, 0), number, 4)
            here = mine(self.ours[2])
            here[...] = (value(here) + value(land(got0, 2)) + value(land(got1, 0))).astype(BF16)
            self.push(here, land(got2, 0), number, 6, self.near_peer)
        elif which == 3:
            self.landed(land(got0, 3), number, 3)
            self.landed(land(got1, 1), number, 5)
            self.landed(land(got2, 0), number, 6)
            for step in range(planes):
                p = lax.rem(self.plane + 1 + step, planes)
                here = mine(self.ours[3], p)
                total = value(here) + value(got0.at[3 * planes + p, :, cols])
                total = total + value(got1.at[planes + p, :, cols]) + value(got2.at[p, :, cols])
                if step == planes - 1:
                    final[:, cols] = total
                else:
                    here[...] = total.astype(BF16)
                    self.push(here, got3.at[step, :, cols], number, 7 + step, self.plane_peers[step])
        else:
            for step in range(planes - 1):
                self.landed(got3.at[step, :, cols], number, 7 + step)
            total = final[:, cols]
            for step in range(planes - 1):
                total = total + value(got3.at[step, :, cols])
            final[:, cols] = total
            pltpu.make_async_copy(final.at[:, cols], result.at[:, cols], self.sems[2].at[number]).start()

    def vector_stage(self, which):
        sums, got, number, result = self.vector
        steps = [self.other, self.near_peer, self.far_peer]
        if which > 0:
            if which < 4:
                self.landed(got.at[which - 1], number, which - 1)
                sums[which] = sums[which - 1] + got[which - 1]
            else:
                total = sums[3]
                for step in range(self.planes - 1):
                    self.landed(got.at[3 + step], number, 3 + step)
                    total = total + got[3 + step]
                sums[4] = total
                pltpu.make_async_copy(sums.at[4], result, self.sems[2].at[number]).start()
        if which < 3:
            self.push(sums.at[which], got.at[which], number, which, steps[which])
        elif which == 3:
            for step, peer in enumerate(self.plane_peers):
                self.push(sums.at[3], got.at[3 + step], number, 3 + step, peer)

    def finish(self, items):
        for tensor, number, start, many in items:
            got = self.tensors[tensor][1]
            one = got.at[0, :, pl.ds(start, many)]
            column = got.at[pl.ds(0, self.planes), :, pl.ds(start, many)]
            for spot in range(6 + self.planes):
                ref = column if spot < 7 else one
                pltpu.make_async_copy(ref, ref, self.sems[0].at[number, spot]).wait()
            final = self.tensors[tensor][5].at[:, pl.ds(start, many)]
            pltpu.make_async_copy(final, final, self.sems[2].at[number]).wait()
        sums, got, number, result = self.vector
        for spot in range(3 + self.planes - 1):
            pltpu.make_async_copy(got.at[0], got.at[0], self.sems[0].at[number, spot]).wait()
        pltpu.make_async_copy(got.at[0], got.at[0], self.sems[2].at[number]).wait()


BACK_INPUTS = ("df", "wp", "slope", "g_t", "dh2", "wh", "z1_t", "wo", "n1", "inv1", "att_t", "qkv", "x_t", "wqkv", "cot")


def back_kernel(size, lengths, skip, vec, gtop, *refs):
    refs = list(refs)

    def take(n):
        out = refs[:n]
        del refs[:n]
        return out

    count = len(BACK_INPUTS)
    source = dict(zip(BACK_INPUTS, take(count)))
    gin = take(1)[0]
    results = take(4)
    vector_result = take(1)[0]
    here = dict(zip(BACK_INPUTS, take(count)))
    dwqkv, keys, values, bias, dk_acc, dv_acc = take(6)
    got = [take(4) for _ in range(4)]
    final = take(4)
    sums, sums_got = take(2)
    send_sem, recv_sem, out_sem, load_sem, gin_sem = refs
    df, wp, slope, g_t, f, wh, z1_t, wo, n1, inv1, att_t, qkv, x_t, wqkv, cot = (here[n] for n in BACK_INPUTS)
    width, inner = wh.shape
    dim = width // HEADS
    pair = 2 * dim
    group = 2 * pair
    wide = 256
    planes = size // 8
    pieces = inner // width

    loads = {}
    for name in BACK_INPUTS:
        dst, src = here[name], source[name]
        rows = min(src.shape[0], dst.shape[0])
        if name == "wp":
            cuts = [(pl.ds(n * width, width), pl.ds(0, width)) for n in range(pieces)]
        elif name == "slope":
            cuts = [(pl.ds(0, rows), pl.ds(n * width, width)) for n in range(pieces)]
        else:
            cuts = [(pl.ds(0, rows), pl.ds(0, dst.shape[1]))]
        loads[name] = [
            pltpu.make_async_copy(src.at[cut], dst.at[cut], load_sem.at[BACK_INPUTS.index(name), n])
            for n, cut in enumerate(cuts)
        ]
    for n in range(pieces):
        if n == 0:
            loads["df"][0].start()
        loads["wp"][n].start()
        loads["slope"][n].start()
    for name in BACK_INPUTS:
        if name not in ("df", "wp", "slope"):
            loads[name][0].start()
    grads = [dwqkv, wo, wh, wp]
    tensors = [
        (grads[t], got[0][t], got[1][t], got[2][t], got[3][t], final[t], results[t], grads[t].shape[0] // size)
        for t in range(4)
    ]
    groups = width // group
    items = [(3, c, group) for c in range(0, width, group)] + [(2, c, width) for c in range(0, inner, width)]
    items.append((1, 0, width))
    fixed = len(items)
    singles = 2
    items += [(0, n * 3 * group, 3 * group) for n in range(groups - 1)]
    items += [(0, (2 * groups - singles + n) * 3 * pair, 3 * pair) for n in range(singles)]
    move = Scatter(tensors, planes, send_sem, recv_sem, out_sem, (sums, sums_got, len(items), vector_result))

    def begin(number):
        tensor, start, many = items[number]
        move.stage(0, tensor, number, start, many)

    def moves(text):
        for word in text.split():
            if word[0] == "v":
                move.vector_stage(int(word[1:]))
            else:
                number = int(word[1:])
                tensor, start, many = items[number]
                move.stage(int(word[0]), tensor, number, start, many)

    gain1 = vec[3:4, :]
    gvec = sums.at[0]
    gvec[...] = jnp.zeros(gvec.shape, F32)
    gvec[0:8, :] = gtop[...]
    loads["df"][0].wait()

    @pl.loop(0, inner // wide)
    def _(block):
        for n in range(pieces):

            @pl.when(block == n * (width // wide))
            def _():
                loads["wp"][n].wait()
                loads["slope"][n].wait()

        cols = pl.ds(pl.multiple_of(block * wide, wide), wide)
        total = jnp.zeros((1, wide), F32)
        half = LIVE // 2
        for start in range(0, LIVE, half):
            at = pl.ds(start, half)
            du = (dot(df[at, :], wp[cols, :], NT) * slope[at, cols].astype(F32)).astype(BF16)
            total = total + jnp.sum(du.astype(F32), 0, keepdims=True)
            slope[at, cols] = du
        row = (block * wide) // width
        for r in range(pieces):

            @pl.when(row == r)
            def _():
                gvec[8 + r : 9 + r, pl.ds(pl.multiple_of(lax.rem(block * wide, width), wide), wide)] = total

    loads["g_t"][0].wait()
    for number, first in enumerate(range(0, width, group)):
        cols = pl.ds(first, group)

        @pl.loop(0, pieces)
        def _(part):
            at = pl.ds(pl.multiple_of(part * width, width), width)
            wp[at, cols] = dot(g_t[at, :], df[:, cols]).astype(BF16)

        begin(number)
    loads["dh2"][0].wait()
    loads["wh"][0].wait()
    step = 160

    moves("10")

    @pl.loop(0, LIVE // step)
    def _(part):
        at = pl.ds(pl.multiple_of(part * step, step), step)
        f[at, :] += dot(slope[at, :], wh[...], NT)

        for spot, text in ((1, "11"), (2, "20"), (3, "12")):

            @pl.when(part == spot)
            def _():
                moves(text)

    loads["z1_t"][0].wait()
    for number in range(pieces):
        for first in range(number * width, (number + 1) * width, wide):
            cols = pl.ds(first, wide)
            wh[:, cols] = dot(z1_t[...], slope[:LIVE, cols]).astype(BF16)
        begin(groups + number)
        if number == 2:
            moves("13 21 30")
    for name in ("wo", "n1", "inv1", "att_t"):
        loads[name][0].wait()
    da = slope.at[:, pl.ds(3 * width, width)]

    @pl.loop(0, LIVE // step)
    def _(part):
        at = pl.ds(pl.multiple_of(part * step, step), step)
        dz = f[at, :]
        n = n1[at, :]
        gvec[3:4, :] += jnp.sum(dz * n, 0, keepdims=True)
        gvec[4:5, :] += jnp.sum(dz, 0, keepdims=True)
        d = norm_back(dz * gain1, n, inv1[at, :1])
        f[at, :] = d
        low = d.astype(BF16)
        df[at, :] = low
        gvec[2:3, :] += jnp.sum(low.astype(F32), 0, keepdims=True)
        da[at, :] = dot(low, wo[...], NT).astype(BF16)
        for spot, text in ((0, "14"), (3, "15")):

            @pl.when(part == spot)
            def _():
                moves(text)

    padded = slope.shape[0]
    da[LIVE:, :] = jnp.zeros((padded - LIVE, width), BF16)
    for start in range(0, width, wide):
        cols = pl.ds(start, wide)
        wo[:, cols] = dot(att_t[...], df[:, cols]).astype(BF16)
    begin(fixed - 1)
    moves("22 31 40")

    loads["qkv"][0].wait()
    chunk = 256
    key_row = lax.broadcasted_iota(jnp.int32, (LIVE, 128), 0)
    bias[...] = jnp.where(key_row < lengths[0], 0.0, NEG_FILL).astype(F32)

    def block(base, to, start, size):
        at = pl.ds(start, size)
        q_c = qkv[at, pl.ds(base, pair)]
        da_c = da[at, pl.ds(to, pair)]
        dq_c = jnp.zeros((size, pair), F32)
        for head in range(2):
            mine = lanes_of(q_c.shape, head, dim)
            s = dot(keys[head], q_c, NT) + jnp.tile(bias[...], (1, size // 128))
            e = jnp.exp(s - jnp.max(s, 0, keepdims=True))
            p = e * (1.0 / jnp.sum(e, 0, keepdims=True))
            dp = dot(values[head], da_c, NT)
            t = p * dp
            ds = (t - p * jnp.sum(t, 0, keepdims=True)).astype(BF16)
            dv_acc[...] += dot(p.astype(BF16), jnp.where(mine, da_c, jnp.zeros_like(da_c)))
            dk_acc[...] += dot(ds, jnp.where(mine, q_c, jnp.zeros_like(q_c)))
            dq_c = dq_c + dot(ds, keys[head], TN)
        slope[at, pl.ds(base, pair)] = (dq_c * (1.0 / math.sqrt(dim))).astype(BF16)

    turns = {
        (0, 0): "16", (0, 1): "17", (0, 2): "23 32", (0, 3): "41", (1, 1): "24 33", (1, 2): "42", (1, 3): "34",
        (2, 0): "25 43", (2, 1): "18", (2, 2): "26 44", (2, 3): "35", (3, 0): "28", (3, 1): "27 36", (3, 2): "45",
        (4, 0): "46 37", (4, 1): "19 38", (4, 2): "47", (4, 3): "29", (5, 0): "110 48", (5, 1): "39", (5, 2): "210", (5, 3): "310",
    }

    def tick(which, part):
        for (a, spot), text in turns.items():
            if isinstance(part, int) and part != spot:
                continue
            now = which == a if isinstance(part, int) else jnp.logical_and(which == a, part == spot)

            @pl.when(now)
            def _():
                moves(text)

    @pl.loop(0, width // pair)
    def _(which):
        base = pl.multiple_of(which * 3 * pair, pair)
        to = pl.multiple_of(which * pair, pair)
        whole = qkv[:LIVE, pl.ds(base + pair, pair)]
        whole_v = qkv[:LIVE, pl.ds(base + 2 * pair, pair)]
        for head in range(2):
            mine = lanes_of(whole.shape, head, dim)
            keys[head] = jnp.where(mine, whole, jnp.zeros_like(whole))
            values[head] = jnp.where(mine, whole_v, jnp.zeros_like(whole_v))
        dk_acc[...] = jnp.zeros_like(dk_acc)
        dv_acc[...] = jnp.zeros_like(dv_acc)

        @pl.loop(0, LIVE // chunk)
        def _(part):
            block(base, to, pl.multiple_of(part * chunk, chunk), chunk)
            tick(which, part)

        block(base, to, LIVE // chunk * chunk, padded - LIVE // chunk * chunk)
        slope[:LIVE, pl.ds(base + pair, pair)] = dk_acc[...].astype(BF16)
        low = dv_acc[...].astype(BF16)
        slope[:LIVE, pl.ds(base + 2 * pair, pair)] = low
        gvec[0:1, pl.ds(to, pair)] = jnp.sum(slope[:LIVE, pl.ds(base, pair)].astype(F32), 0, keepdims=True)
        gvec[1:2, pl.ds(to, pair)] = jnp.sum(low.astype(F32), 0, keepdims=True)
        tick(which, LIVE // chunk)

        @pl.when(which == 1)
        def _():
            loads["x_t"][0].wait()

        for number in range(fixed, len(items)):
            start, many = items[number][1:]

            @pl.when(which == (start + many) // (3 * pair) - 1)
            def _():
                @pl.loop(0, many // (3 * pair))
                def _(part):
                    cols = pl.ds(pl.multiple_of(start + part * 3 * pair, pair), 3 * pair)
                    dwqkv[:, cols] = dot(x_t[...], slope[:LIVE, cols]).astype(BF16)

                begin(number)

    moves("v0 111")
    loads["wqkv"][0].wait()
    loads["cot"][0].wait()

    @pl.loop(0, LIVE // step)
    def _(part):
        at = pl.ds(pl.multiple_of(part * step, step), step)
        row = lax.broadcasted_iota(jnp.int32, (step, 1), 0) + part * step
        dropped = jnp.where(row < lengths[0], cot[at, :].astype(F32), 0.0)
        total = f[at, :] + dot(slope[at, : 3 * width], wqkv[...], NT)
        f[at, :] = jnp.where(skip[0] == 1, dropped, total)

        for spot, text in ((0, "v1 49"), (2, "211 v2"), (3, "410"), (LIVE // step - 1, "311 v3")):

            @pl.when(part == spot)
            def _():
                moves(text)

    out = [pltpu.make_async_copy(f, gin.at[pl.ds(0, LIVE)], gin_sem.at[0])]
    n1[: gin.shape[0] - LIVE, :] = jnp.zeros((gin.shape[0] - LIVE, width), F32)
    out.append(pltpu.make_async_copy(n1.at[pl.ds(0, gin.shape[0] - LIVE)], gin.at[pl.ds(LIVE, gin.shape[0] - LIVE)], gin_sem.at[1]))
    for copy in out:
        copy.start()
    moves("411 v4")
    for copy in out:
        copy.wait()
    move.finish([(tensor, number, start, many) for number, (tensor, start, many) in enumerate(items)])


def back(size, lengths, skip, vec, gtop, arrays):
    rows, width = arrays["cot"].shape
    inner = arrays["wh"].shape[1]
    planes = size // 8
    half = size // 2
    like = jax.ShapeDtypeStruct
    smem, vmem, any_ = (pl.BlockSpec(memory_space=m) for m in (pltpu.SMEM, VMEM, pl.ANY))
    padded = -(-LIVE // 128) * 128
    keep = {"slope": padded, "qkv": padded, "cot": LIVE}
    held = [
        VMEM((keep.get(name, arrays[name].shape[0]), arrays[name].shape[1]), arrays[name].dtype)
        for name in BACK_INPUTS
    ]
    shapes = [(width // size, 3 * width), (width // size, width), (width // size, inner), (inner // size, width)]
    lands = lambda many: [VMEM((many, r, w), BF16) for r, w in shapes]
    pair = 2 * width // HEADS
    numbers = 2 * (width // (2 * pair)) + inner // width + 1 + 1 + 1
    spots = 6 + planes
    return pl.pallas_call(
        functools.partial(back_kernel, size),
        out_shape=[like((rows, width), F32), *[like(s, F32) for s in shapes], like((16, width), F32)],
        in_specs=[smem, smem, vmem, vmem] + [any_] * len(BACK_INPUTS),
        out_specs=[any_] * 6,
        scratch_shapes=[
            *held,
            VMEM((width, 3 * width), BF16), VMEM((2, LIVE, pair), BF16), VMEM((2, LIVE, pair), BF16),
            VMEM((LIVE, 128), F32), VMEM((LIVE, pair), F32), VMEM((LIVE, pair), F32),
            *lands(half), *lands(half // 2), *lands(planes), *lands(planes - 1),
            *[VMEM(s, F32) for s in shapes],
            VMEM((5, 16, width), F32), VMEM((3 + planes - 1, 16, width), F32),
            pltpu.SemaphoreType.DMA((numbers, spots)), pltpu.SemaphoreType.DMA((numbers, spots)),
            pltpu.SemaphoreType.DMA((numbers,)), pltpu.SemaphoreType.DMA((len(BACK_INPUTS), inner // width)),
            pltpu.SemaphoreType.DMA((2,)),
        ],
        compiler_params=pltpu.CompilerParams(collective_id=1, has_side_effects=True, vmem_limit_bytes=67043328),
        name="back",
    )(lengths, skip, vec, gtop, *[arrays[n] for n in BACK_INPUTS])


def finish_kernel(size, sums_in, qkv_in, wo_in, wh_in, wp_in, gin_in, outputs_in, *refs):
    pieces, (gq, gk, gv, go, gh, gp, gin, outputs), (sums, sem) = refs[:9], refs[9:17], refs[17:]
    width = sums.shape[1]
    pair = 2 * width // HEADS
    moves = [(sums_in, sums), (wo_in, go), (wh_in, gh), (wp_in, gp), (gin_in, gin), (outputs_in, outputs)]
    for number in range(width // pair):
        to = pl.ds(number * pair, pair)
        for w, out in enumerate((gq, gk, gv)):
            moves.append((qkv_in.at[:, pl.ds((3 * number + w) * pair, pair)], out.at[:, to]))
    moves = [pltpu.make_async_copy(a, b, sem.at[n]) for n, (a, b) in enumerate(moves)]
    for copy in moves:
        copy.start()
    me = lax.axis_index("fsdp")
    piece = width // size

    def pick(value, first):
        lane = lax.broadcasted_iota(jnp.int32, (width, 128), 1)
        entry = lax.broadcasted_iota(jnp.int32, (width, 128), 0)
        one = jnp.where(entry == lane + first, 1.0, 0.0)
        return lax.dot_general(
            value, one, (((1,), (0,)), ((), ())), precision=lax.Precision.HIGHEST, preferred_element_type=F32
        )

    moves[0].wait()
    short = pick(sums[0:8, :], me * piece)
    for k in range(8):
        pieces[k][...] = short[k, :piece]
    long = pieces[8].shape[0]
    each = width // long
    row = lax.broadcasted_iota(jnp.int32, (8, width), 0)
    chosen = jnp.sum(jnp.where(row == me // each, sums[8:16, :], 0.0), 0, keepdims=True)
    spread = pick(jnp.broadcast_to(chosen, (8, width)), lax.rem(me, each) * long)
    pieces[8][...] = spread[0, :long]
    for copy in moves[1:]:
        copy.wait()


def finish(size, sums, matrices, gin, outputs):
    width = sums.shape[1]
    like = jax.ShapeDtypeStruct
    vmem, any_ = pl.BlockSpec(memory_space=VMEM), pl.BlockSpec(memory_space=pl.ANY)
    piece = width // size
    inner = matrices[2].shape[1]
    row = like((piece, width), F32)
    return pl.pallas_call(
        functools.partial(finish_kernel, size),
        out_shape=[
            *[like((piece,), F32)] * 8, like((inner // size,), F32),
            row, row, row, *[like(m.shape, F32) for m in matrices[1:]], like(gin.shape, F32), like(outputs.shape, BF16),
        ],
        in_specs=[any_] * 7,
        out_specs=[vmem] * 17,
        scratch_shapes=[VMEM(sums.shape, F32), pltpu.SemaphoreType.DMA((6 + 3 * HEADS // 2,))],
        compiler_params=pltpu.CompilerParams(vmem_limit_bytes=67043328),
        name="finish",
    )(sums, *matrices, gin, outputs)


def local(
    size,
    inputs,
    cotangent,
    lengths,
    skip_bit,
    w_query,
    w_key,
    w_value,
    w_out,
    b_query,
    b_value,
    b_out,
    ln1_gain,
    ln1_bias,
    w_hidden,
    b_hidden,
    w_proj,
    b_proj,
    ln2_gain,
    ln2_bias,
):
    vectors = [b_query, b_value, b_out, ln1_gain, ln1_bias, b_proj, ln2_gain, ln2_bias, b_hidden]
    weights = [w_query, w_key, w_value, w_out, w_hidden, w_proj]
    saved, vec, gtop = front(size, lengths, skip_bit, inputs, cotangent, weights, vectors)
    grad_inputs, *matrices, sums = back(size, lengths, skip_bit, vec, gtop, {**saved, "cot": cotangent})
    (
        g_b_query, g_b_value, g_b_out, g_ln1_gain, g_ln1_bias, g_b_proj, g_ln2_gain, g_ln2_bias, g_b_hidden,
        g_w_query, g_w_key, g_w_value, g_w_out, g_w_hidden, g_w_proj, grad_inputs, outputs,
    ) = finish(size, sums, matrices, grad_inputs, saved["outputs"])
    return (
        outputs,
        grad_inputs,
        g_w_query,
        g_w_key,
        g_w_value,
        g_w_out,
        g_b_query,
        g_b_value,
        g_b_out,
        g_ln1_gain,
        g_ln1_bias,
        g_w_hidden,
        g_b_hidden,
        g_w_proj,
        g_b_proj,
        g_ln2_gain,
        g_ln2_bias,
    )


def local_plain(
    inputs,
    cotangent,
    lengths,
    skip_bit,
    w_query,
    w_key,
    w_value,
    w_out,
    b_query,
    b_value,
    b_out,
    ln1_gain,
    ln1_bias,
    w_hidden,
    b_hidden,
    w_proj,
    b_proj,
    ln2_gain,
    ln2_bias,
):
    (
        query_full, key_full, value_full, out_full, hidden_full, proj_full,
        bq_full, bv_full, bo_full, gain_one, shift_one, bh_full, bp_full, gain_two, shift_two,
    ) = [
        lax.all_gather(p, "fsdp", axis=0, tiled=True)
        for p in (
            w_query, w_key, w_value, w_out, w_hidden, w_proj,
            b_query, b_value, b_out, ln1_gain, ln1_bias, b_hidden, b_proj, ln2_gain, ln2_bias,
        )
    ]
    row = lambda v: as_float(v)[None, :]
    q, k, v, att = attend(
        lengths, inputs, query_full, key_full, value_full, row(bq_full), row(bv_full)
    )
    vec = jnp.stack([as_float(v_) for v_ in (bo_full, gain_one, shift_one, bp_full, gain_two, shift_two)])
    vec = jnp.pad(vec, ((0, 2), (0, 0)))
    outputs, dh1, da, d_weight_out, d_weight_hidden, d_weight_proj, gvec, gbh = middle(
        lengths, skip_bit, inputs, att, cotangent, out_full, hidden_full, proj_full, vec, row(bh_full)
    )
    grad_inputs, d_weight_query, d_weight_key, d_weight_value, gbq, gbv = attend_back(
        lengths, inputs, dh1, q, k, v, da, query_full, key_full, value_full, cotangent, skip_bit
    )
    (
        g_w_query, g_w_key, g_w_value, g_w_out, g_w_hidden, g_w_proj,
        g_b_query, g_b_value, g_b_out, g_ln1_gain, g_ln1_bias,
        g_b_hidden, g_b_proj, g_ln2_gain, g_ln2_bias,
    ) = [
        lax.psum_scatter(lax.optimization_barrier(as_float(grad)), "fsdp", scatter_dimension=0, tiled=True)
        for grad in (
            d_weight_query, d_weight_key, d_weight_value, d_weight_out, d_weight_hidden, d_weight_proj,
            gbq[0], gbv[0], gvec[0], gvec[1], gvec[2], gbh[0], gvec[3], gvec[4], gvec[5],
        )
    ]
    return (
        outputs,
        grad_inputs,
        g_w_query,
        g_w_key,
        g_w_value,
        g_w_out,
        g_b_query,
        g_b_value,
        g_b_out,
        g_ln1_gain,
        g_ln1_bias,
        g_w_hidden,
        g_b_hidden,
        g_w_proj,
        g_b_proj,
        g_ln2_gain,
        g_ln2_bias,
    )


def solution(mesh):
    size = mesh.shape["fsdp"]
    placed = (
        P("fsdp", None),
        P("fsdp", None),
        P("fsdp"),
        P("fsdp"),
        P("fsdp", None),
        P("fsdp", None),
        P("fsdp", None),
        P("fsdp", None),
        P("fsdp"),
        P("fsdp"),
        P("fsdp"),
        P("fsdp"),
        P("fsdp"),
        P("fsdp", None),
        P("fsdp"),
        P("fsdp", None),
        P("fsdp"),
        P("fsdp"),
        P("fsdp"),
    )
    return jax.shard_map(
        functools.partial(local, size) if size == 32 else local_plain,
        mesh=mesh,
        in_specs=placed,
        out_specs=(
            P("fsdp", None),
            P("fsdp", None),
            P("fsdp", None),
            P("fsdp", None),
            P("fsdp", None),
            P("fsdp", None),
            P("fsdp"),
            P("fsdp"),
            P("fsdp"),
            P("fsdp"),
            P("fsdp"),
            P("fsdp", None),
            P("fsdp"),
            P("fsdp", None),
            P("fsdp"),
            P("fsdp"),
            P("fsdp"),
        ),
        check_vma=False,
    )
```

```python
import functools
import math

import jax
import jax.numpy as jnp
from jax import lax
from jax.experimental import pallas as pl
from jax.experimental.pallas import tpu as pltpu
from jax.sharding import PartitionSpec as P

HEADS = 12
LIVE = 800
EPSILON = 1e-05
NEG_FILL = -1e30
NT = (((1,), (1,)), ((), ()))
TN = (((0,), (0,)), ((), ()))
VMEM = pltpu.VMEM
F32, BF16 = jnp.float32, jnp.bfloat16


def dot(a, b, dims=(((1,), (0,)), ((), ()))):
    return lax.dot_general(a, b, dims, preferred_element_type=F32)


def lanes_of(shape, head, dim):
    lane = lax.broadcasted_iota(jnp.int32, shape, 1)
    return (lane < dim) if head == 0 else (lane >= dim)


def attend_kernel(lengths, x, wq, wk, wv, bq, bv, q, k, v, att, keys, values):
    rows, width = x.shape
    dim = width // HEADS
    pair = 2 * dim
    group = 2 * pair
    step = 256
    key_lane = lax.broadcasted_iota(jnp.int32, (1, LIVE), 1)
    bias = jnp.where(key_lane < lengths[0], 0.0, NEG_FILL).astype(F32)
    for head in range(2):
        values[head, :, pair:] = jnp.ones((LIVE, pair), BF16)
    for first in range(0, width, group):
        cols = pl.ds(first, group)

        @pl.loop(0, rows // step)
        def _(part):
            at = pl.ds(pl.multiple_of(part * step, step), step)
            here = x[at, :]
            q[at, cols] = ((dot(here, wq[:, cols]) + bq[:, cols]).astype(BF16).astype(F32) * (1.0 / math.sqrt(dim))).astype(BF16)
            k[at, cols] = dot(here, wk[:, cols]).astype(BF16)
            v[at, cols] = (dot(here, wv[:, cols]) + bv[:, cols]).astype(BF16)

        for start in range(first, first + group, pair):
            wide = pl.ds(start, pair)
            whole = k[:LIVE, wide]
            for head in range(2):
                keys[head] = jnp.where(lanes_of(whole.shape, head, dim), whole, jnp.zeros_like(whole))
                values[head, :, :pair] = v[:LIVE, wide]

            @pl.loop(0, rows // step)
            def _(part):
                at = pl.ds(pl.multiple_of(part * step, step), step)
                here = q[at, wide]
                outs = []
                for head in range(2):
                    s = dot(here, keys[head], NT) + bias
                    e = jnp.exp(s - jnp.max(s, -1, keepdims=True))
                    o = dot(e.astype(BF16), values[head])
                    outs.append(o[:, :pair] / o[:, pair:])
                att[at, wide] = jnp.where(lanes_of(outs[0].shape, 0, dim), outs[0], outs[1]).astype(BF16)


def attend(lengths, x, wq, wk, wv, bq, bv):
    rows, width = x.shape
    pair = 2 * width // HEADS
    return pl.pallas_call(
        attend_kernel,
        out_shape=[jax.ShapeDtypeStruct(x.shape, BF16)] * 4,
        in_specs=[pl.BlockSpec(memory_space=pltpu.SMEM)] + [pl.BlockSpec(memory_space=VMEM)] * 6,
        out_specs=[pl.BlockSpec(memory_space=VMEM)] * 4,
        scratch_shapes=[VMEM((2, LIVE, pair), BF16), VMEM((2, LIVE, 2 * pair), BF16)],
        compiler_params=pltpu.CompilerParams(vmem_limit_bytes=60 << 20),
        name="attend",
    )(lengths, x, wq, wk, wv, bq, bv)


def attend_back_kernel(lengths, x, dh1, q, k, v, da, wq, wk, wv, cot, skip, gin, gwq, gwk, gwv, gbq, gbv,
                       dq, dk, dv, keys, values, bias, dk_acc, dv_acc):
    rows, width = x.shape
    dim = width // HEADS
    pair = 2 * dim
    chunk = 256
    tops = [(c, min(chunk, -(-LIVE // 128) * 128 - c)) for c in range(0, LIVE, chunk)]
    key_row = lax.broadcasted_iota(jnp.int32, (LIVE, 128), 0)
    bias[...] = jnp.where(key_row < lengths[0], 0.0, NEG_FILL).astype(F32)
    dk[...] = jnp.zeros_like(dk)
    dv[...] = jnp.zeros_like(dv)

    def block(wide, start, size):
        at = pl.ds(start, size)
        q_c, da_c = q[at, wide], da[at, wide]
        dq_c = jnp.zeros((size, pair), F32)
        for head in range(2):
            mine = lanes_of(q_c.shape, head, dim)
            s = dot(keys[head], q_c, NT) + jnp.tile(bias[...], (1, size // 128))
            e = jnp.exp(s - jnp.max(s, 0, keepdims=True))
            p = e * (1.0 / jnp.sum(e, 0, keepdims=True))
            dp = dot(values[head], da_c, NT)
            t = p * dp
            ds = (t - p * jnp.sum(t, 0, keepdims=True)).astype(BF16)
            dv_acc[...] += dot(p.astype(BF16), jnp.where(mine, da_c, jnp.zeros_like(da_c)))
            dk_acc[...] += dot(ds, jnp.where(mine, q_c, jnp.zeros_like(q_c)))
            dq_c = dq_c + dot(ds, keys[head], TN)
        dq[at, wide] = (dq_c * (1.0 / math.sqrt(dim))).astype(BF16)

    @pl.loop(0, width // pair)
    def _(which):
        wide = pl.ds(pl.multiple_of(which * pair, pair), pair)
        whole, whole_v = k[:LIVE, wide], v[:LIVE, wide]
        for head in range(2):
            mine = lanes_of(whole.shape, head, dim)
            keys[head] = jnp.where(mine, whole, jnp.zeros_like(whole))
            values[head] = jnp.where(mine, whole_v, jnp.zeros_like(whole_v))
        dk_acc[...] = jnp.zeros_like(dk_acc)
        dv_acc[...] = jnp.zeros_like(dv_acc)

        @pl.loop(0, LIVE // chunk)
        def _(part):
            block(wide, pl.multiple_of(part * chunk, chunk), chunk)

        for start, size in tops:
            if size < chunk:
                block(wide, start, size)
        dk[:LIVE, wide] = dk_acc[...].astype(BF16)
        dv[:LIVE, wide] = dv_acc[...].astype(BF16)

    gbq[...] = jnp.sum(dq[:LIVE, :].astype(F32), 0, keepdims=True)
    gbv[...] = jnp.sum(dv[:LIVE, :].astype(F32), 0, keepdims=True)
    here = x[:LIVE, :]
    for grad, out in ((dq, gwq), (dk, gwk), (dv, gwv)):
        for start in range(0, width, 256):
            cols = pl.ds(start, 256)
            out[:, cols] = dot(here, grad[:LIVE, cols], TN).astype(BF16)
    step = 160

    @pl.loop(0, LIVE // step)
    def _(part):
        at = pl.ds(pl.multiple_of(part * step, step), step)
        total = dh1[at, :] + dot(dq[at, :], wq[...], NT)
        total = total + dot(dk[at, :], wk[...], NT)
        total = total + dot(dv[at, :], wv[...], NT)
        row = lax.broadcasted_iota(jnp.int32, (step, 1), 0) + part * step
        dropped = jnp.where(row < lengths[0], cot[at, :].astype(F32), 0.0)
        gin[at, :] = jnp.where(skip[0] == 1, dropped, total)

    gin[LIVE:, :] = jnp.zeros((rows - LIVE, width), F32)


def attend_back(lengths, x, dh1, q, k, v, da, wq, wk, wv, cot, skip):
    rows, width = x.shape
    pair = 2 * width // HEADS
    like = jax.ShapeDtypeStruct
    smem = pl.BlockSpec(memory_space=pltpu.SMEM)
    return pl.pallas_call(
        attend_back_kernel,
        out_shape=[like((rows, width), F32)] + [like((width, width), BF16)] * 3 + [like((1, width), F32)] * 2,
        in_specs=[smem] + [pl.BlockSpec(memory_space=VMEM)] * 10 + [smem],
        out_specs=[pl.BlockSpec(memory_space=VMEM)] * 6,
        scratch_shapes=[VMEM(x.shape, BF16)] * 3
        + [VMEM((2, LIVE, pair), BF16)] * 2
        + [VMEM((LIVE, 128), F32)]
        + [VMEM((LIVE, pair), F32)] * 2,
        compiler_params=pltpu.CompilerParams(vmem_limit_bytes=62 << 20),
        name="attend_back",
    )(lengths, x, dh1, q, k, v, da, wq, wk, wv, cot, skip)


def middle_kernel(lengths, skip, x_in, att_in, cot_in, wo_in, wh_in, wp_in, vec, bh,
                  outputs, dh1, da, gwo, gwh, gwp, gvec, gbh,
                  x, att, cot, wo, wh, wp, z1, n1, inv1, f, g, slope, df, z1t, out_h, out_p, load_sem, out_sem):
    rows, width = x.shape
    inner = wh.shape[1]
    loads = [
        pltpu.make_async_copy(a, b, load_sem.at[i])
        for i, (a, b) in enumerate(
            ((x_in, x), (att_in, att), (wo_in, wo), (wh_in, wh), (wp_in, wp), (cot_in, cot))
        )
    ]
    for load in loads:
        load.start()
    bo, gain1, shift1, bp, gain2, shift2 = (vec[i : i + 1, :] for i in range(6))
    for load in loads[:3]:
        load.wait()
    step = 256

    def norm(h):
        centred = h - jnp.mean(h, -1, keepdims=True)
        inv = lax.rsqrt(jnp.mean(centred * centred, -1, keepdims=True) + EPSILON)
        return centred * inv, inv

    def norm_back(e, n, inv):
        return inv * (e - jnp.mean(e, -1, keepdims=True) - n * jnp.mean(e * n, -1, keepdims=True))

    @pl.loop(0, rows // step)
    def _(part):
        at = pl.ds(pl.multiple_of(part * step, step), step)
        h = x[at, :].astype(F32) + (dot(att[at, :], wo[...]) + bo)
        n, inv = norm(h)
        n1[at, :] = n
        inv1[at, :] = jnp.broadcast_to(inv, (step, 128))
        z1[at, :] = (n * gain1 + shift1).astype(BF16)

    loads[3].wait()
    loads[4].wait()
    f[...] = jnp.zeros_like(f)
    wide = 256

    @pl.loop(0, inner // wide)
    def _(block):
        cols = pl.ds(pl.multiple_of(block * wide, wide), wide)
        b = bh[:, cols]
        for start in range(0, rows, step):
            at = pl.ds(start, step)
            u = dot(z1[at, :], wh[:, cols]) + b
            phi = 0.5 * (1.0 + lax.erf(u * 0.7071067811865476))
            g[at, cols] = (u * phi).astype(BF16)
            slope[at, cols] = (phi + u * (jnp.exp(-0.5 * u * u) * 0.3989422804014327)).astype(BF16)
            f[at, :] += dot(g[at, cols], wp[cols, :])

    loads[5].wait()
    gvec[...] = jnp.zeros_like(gvec)
    keep = 1.0 - skip[0].astype(F32)

    @pl.loop(0, rows // step)
    def _(part):
        at = pl.ds(pl.multiple_of(part * step, step), step)
        n, inv = norm(z1[at, :].astype(F32) + (f[at, :] + bp))
        outputs[at, :] = jnp.where(skip[0] == 1, x[at, :], (n * gain2 + shift2).astype(BF16))
        row = lax.broadcasted_iota(jnp.int32, (step, 1), 0) + part * step
        dy = jnp.where(row < lengths[0], cot[at, :].astype(F32), 0.0) * keep
        d = norm_back(dy * gain2, n, inv)
        low = d.astype(BF16)
        f[at, :] = d
        df[at, :] = low
        gvec[3:4, :] += jnp.sum(low.astype(F32), 0, keepdims=True)
        gvec[4:5, :] += jnp.sum(dy * n, 0, keepdims=True)
        gvec[5:6, :] += jnp.sum(dy, 0, keepdims=True)

    z1t[...] = z1[:LIVE, :].T

    def flush(block, buf, slot):
        cols = pl.ds(pl.multiple_of(block * wide, wide), wide)
        if buf is out_h:
            return pltpu.make_async_copy(buf.at[slot], gwh.at[:, cols], out_sem.at[0, slot])
        return pltpu.make_async_copy(buf.at[slot], gwp.at[cols, :], out_sem.at[1, slot])

    @pl.loop(0, inner // wide)
    def _(block):
        slot = lax.rem(block, 2)
        cols = pl.ds(pl.multiple_of(block * wide, wide), wide)

        @pl.when(block >= 2)
        def _():
            flush(block, out_h, slot).wait()
            flush(block, out_p, slot).wait()

        out_p[slot] = dot(g[:LIVE, cols], df[:LIVE, :], TN).astype(BF16)
        flush(block, out_p, slot).start()
        total = jnp.zeros((1, wide), F32)
        half = LIVE // 2
        for start in range(0, LIVE, half):
            at = pl.ds(start, half)
            du = (dot(df[at, :], wp[cols, :], NT) * slope[at, cols].astype(F32)).astype(BF16)
            total = total + jnp.sum(du.astype(F32), 0, keepdims=True)
            g[at, cols] = du
            f[at, :] += dot(du, wh[:, cols], NT)
        gbh[:, cols] = total
        out_h[slot] = dot(z1t[...], g[:LIVE, cols]).astype(BF16)
        flush(block, out_h, slot).start()

    half = LIVE // 5
    @pl.loop(0, LIVE // half)
    def _(part):
        at = pl.ds(pl.multiple_of(part * half, half), half)
        dz = f[at, :]
        n = n1[at, :]
        gvec[1:2, :] += jnp.sum(dz * n, 0, keepdims=True)
        gvec[2:3, :] += jnp.sum(dz, 0, keepdims=True)
        d = norm_back(dz * gain1, n, inv1[at, :1])
        dh1[at, :] = d
        low = d.astype(BF16)
        df[at, :] = low
        gvec[0:1, :] += jnp.sum(low.astype(F32), 0, keepdims=True)
        da[at, :] = dot(low, wo[...], NT).astype(BF16)

    da[LIVE:, :] = jnp.zeros((rows - LIVE, width), BF16)
    for start in range(0, width, wide):
        cols = pl.ds(start, wide)
        gwo[cols, :] = dot(att[:LIVE, cols], df[:LIVE, :], TN).astype(BF16)
    for block in (inner // wide - 2, inner // wide - 1):
        flush(block, out_h, block % 2).wait()
        flush(block, out_p, block % 2).wait()


def middle(lengths, skip, x, att, cot, wo, wh, wp, vec, bh):
    rows, width = x.shape
    inner = wh.shape[1]
    like = jax.ShapeDtypeStruct
    smem, vmem, any_ = (pl.BlockSpec(memory_space=m) for m in (pltpu.SMEM, VMEM, pl.ANY))
    pad = -(-LIVE // 128) * 128
    return pl.pallas_call(
        middle_kernel,
        out_shape=[
            like((rows, width), BF16), like((LIVE, width), F32), like((rows, width), BF16),
            like((width, width), BF16), like((width, inner), BF16), like((inner, width), BF16),
            like((8, width), F32), like((1, inner), F32),
        ],
        in_specs=[smem] * 2 + [any_] * 6 + [vmem] * 2,
        out_specs=[vmem] * 4 + [any_] * 2 + [vmem] * 2,
        scratch_shapes=[
            VMEM((rows, width), BF16), VMEM((rows, width), BF16), VMEM((rows, width), BF16),
            VMEM((width, width), BF16), VMEM((width, inner), BF16), VMEM((inner, width), BF16),
            VMEM((rows, width), BF16), VMEM((rows, width), F32), VMEM((rows, 128), F32),
            VMEM((rows, width), F32), VMEM((rows, inner), BF16), VMEM((rows, inner), BF16),
            VMEM((rows, width), BF16), VMEM((width, LIVE), BF16),
            VMEM((2, width, 256), BF16), VMEM((2, 256, width), BF16),
            pltpu.SemaphoreType.DMA((6,)), pltpu.SemaphoreType.DMA((2, 2)),
        ],
        compiler_params=pltpu.CompilerParams(vmem_limit_bytes=63 << 20),
        name="middle",
    )(lengths, skip, x, att, cot, wo, wh, wp, vec, bh)


def as_float(value):
    return value.astype(jnp.float32)


MESH = pl.DeviceIdType.MESH


def place(me, planes):
    core = lax.rem(me, 2)
    chip = me // 2
    col = lax.rem(chip, 2)
    row = lax.rem(chip // 2, 2)
    plane = chip // 4
    near = jnp.where(core == 0, row, col)
    far = jnp.where(core == 0, col, row)

    def index(plane_, near_, far_, core_):
        row_ = jnp.where(core_ == 0, near_, far_)
        col_ = jnp.where(core_ == 0, far_, near_)
        return ((plane_ * 2 + row_) * 2 + col_) * 2 + core_

    return core, near, far, plane, index


def greet(peers):
    barrier = pltpu.get_barrier_semaphore()
    for peer in peers:
        pl.semaphore_signal(barrier, inc=1, device_id=(peer,), device_id_type=MESH)
    pl.semaphore_wait(barrier, len(peers))


class Gather:
    def __init__(self, items, planes, send_sem, recv_sem, local_sem):
        self.items = items
        self.planes = planes
        self.sems = send_sem, recv_sem, local_sem
        me = lax.axis_index("fsdp")
        self.core, self.near, self.far, self.plane, self.index = place(me, planes)
        self.other = self.index(self.plane, self.far, self.near, 1 - self.core)
        self.near_peer = self.index(self.plane, 1 - self.near, self.far, self.core)
        self.far_peer = self.index(self.plane, self.near, 1 - self.far, self.core)
        self.plane_peers = [
            self.index(lax.rem(self.plane + step, planes), self.near, self.far, self.core) for step in range(1, planes)
        ]
        self.spots = [
            self.index(0, n, f, self.core) for n, f in (
                (self.near, self.far), (1 - self.near, self.far), (self.near, 1 - self.far), (1 - self.near, 1 - self.far)
            )
        ]
        greet([self.other, self.near_peer, self.far_peer, *self.plane_peers])

    def column(self, number, spot, plane=slice(None)):
        own, full, cols = self.items[number]
        if cols is None:
            return full.at[plane, spot]
        rows = own.shape[0]
        view = full.reshape(self.planes, full.shape[0] // self.planes, full.shape[1])
        return view.at[plane, pl.ds(pl.multiple_of(spot * rows, 8), rows), cols]

    def push(self, number, src, dst, spot, peer):
        pltpu.make_async_remote_copy(
            src_ref=src, dst_ref=dst, send_sem=self.sems[0].at[number, spot], recv_sem=self.sems[1].at[number, spot],
            device_id=(peer,), device_id_type=MESH,
        ).start()

    def landed(self, number, spot, whole=False):
        where = self.column(number, self.spots[0], slice(None) if whole else 0)
        pltpu.make_async_copy(where, where, self.sems[1].at[number, spot]).wait()

    def stage(self, which, number):
        planes = self.planes
        near0, far0, other0, wide0 = (planes - 1 + n * planes for n in range(4))
        mine, near, far, both = self.spots
        own, full, cols = self.items[number]
        src = own if cols is None else own.at[:, cols]
        sides = ((near0, self.near_peer), (far0, self.far_peer), (other0, self.other))
        if which == 1:
            here = self.column(number, mine, self.plane)
            for step, peer in enumerate(self.plane_peers):
                self.push(number, src, here, step, peer)
            pltpu.make_async_copy(src, here, self.sems[2].at[number]).start()
        elif which == 6:
            for base, peer in sides:
                self.push(number, src, self.column(number, mine, self.plane), base, peer)
        elif which == 2:
            for step in range(1, planes):
                self.landed(number, step - 1)
                here = self.column(number, mine, lax.rem(self.plane + planes - step, planes))
                for base, peer in sides:
                    self.push(number, here, here, base + step, peer)
        elif which == 3:
            for step in range(planes):
                self.landed(number, near0 + step)
            where = self.column(number, near)
            self.push(number, where, where, wide0, self.far_peer)
            self.push(number, where, where, wide0 + 1, self.other)
        elif which == 4:
            for step in range(planes):
                self.landed(number, far0 + step)
            where = self.column(number, far)
            self.push(number, where, where, wide0 + 2, self.other)
            self.landed(number, wide0, True)
            where = self.column(number, both)
            self.push(number, where, where, wide0 + 3, self.other)
        else:
            for step in range(planes):
                self.landed(number, other0 + step)
            for spot in range(1, 4):
                self.landed(number, wide0 + spot, True)
            here = self.column(number, mine, 0)
            pltpu.make_async_copy(here, here, self.sems[2].at[number]).wait()

    def finish(self):
        for number in range(len(self.items)):
            for spot in range(4 * self.planes + 3):
                where = self.column(number, self.spots[0], 0 if spot < 4 * self.planes - 1 else slice(None))
                pltpu.make_async_copy(where, where, self.sems[0].at[number, spot]).wait()


def unpack(packed, vec, bh, size):
    width, inner = vec.shape[1], bh.shape[1]
    piece, long = width // size, inner // size

    def pick(row, part, start):
        flat = packed[:, :, row, :].reshape(size, 128).astype(BF16)
        lane = lax.rem(lax.broadcasted_iota(jnp.int32, (128, width), 1) + start, part)
        entry = lax.broadcasted_iota(jnp.int32, (128, width), 0)
        spread = dot(flat, jnp.where(entry == lane, 1.0, 0.0).astype(BF16))
        lane = lax.broadcasted_iota(jnp.int32, (size, width), 1) + start
        owner = lax.broadcasted_iota(jnp.int32, (size, width), 0)
        return jnp.sum(jnp.where(lane - lax.rem(lane, part) == part * owner, spread, 0.0), 0, keepdims=True)

    for k in range(8):
        vec[k : k + 1, :] = pick(k, piece, 0)
    for start in range(0, inner, width):
        bh[:, start : start + width] = pick(8, long, start)


def parts_of(value):
    high = value.astype(BF16).astype(F32)
    rest = value - high
    middle = rest.astype(BF16).astype(F32)
    return high, middle, rest - middle


def fill(base, head, dim, values):
    lane = lax.broadcasted_iota(jnp.int32, base.shape, 1) - (dim if head == 0 else 0)
    for n, value in enumerate(values):
        base = jnp.where(lane == n, value, base)
    return base


def own_lanes(value, head, dim):
    return jnp.where(lanes_of(value.shape, head, dim), value, jnp.zeros_like(value))


def norm(h):
    centred = h - jnp.mean(h, -1, keepdims=True)
    inv = lax.rsqrt(jnp.mean(centred * centred, -1, keepdims=True) + EPSILON)
    return centred * inv, inv


def norm_back(e, n, inv):
    return inv * (e - jnp.mean(e, -1, keepdims=True) - n * jnp.mean(e * n, -1, keepdims=True))


FRONT_SAVED = ("qkv", "att", "att_t", "z1_t", "x_t", "n1", "inv1", "g_t", "slope", "dh2", "df", "outputs", "wqkv", "wo", "wh", "wp")


TURNS = {
    "init": "60 61 62 63 64 65 66 67 68 69 610 611 20 21 22 30 31 23 32 40 33 41 50",
    "proj0": "24", "p0.0": "51", "p0.3": "42 34 25", "p1.1": "52 43", "p1.3": "35 26", "proj2": "53", "p2.0": "44",
    "p2.2": "36 27", "p2.3": "54", "p3.0": "45", "p3.2": "37 28", "p3.3": "55", "p4.0": "46 29", "p4.1": "38",
    "p4.3": "56", "p5.0": "210", "p5.1": "47 39", "p5.3": "211", "tr": "57", "out": "310", "ff0": "311", "ff1": "48",
    "ff4": "58", "ff6": "49", "ff9": "59", "ff11": "410", "fp0": "411 510", "fp1": "511",
}


def front_kernel(size, lengths, skip, x_in, cot_in, *refs):
    refs = list(refs)

    def take(n):
        out = refs[:n]
        del refs[:n]
        return out

    vectors = take(9)
    wq_own, wk_own, wv_own, wo_own, wh_own, wp_own = take(6)
    saved = dict(zip(FRONT_SAVED, take(len(FRONT_SAVED))))
    vec, gvec = take(2)
    (x, cot, qkv, att, z1, n1, inv1, g, slope, f, outputs, df, x_t, att_t, z1_t, g_t) = take(16)
    wqkv, wo, wh, wp, packed = take(5)
    bh, keys, values, mine, qkv_own, send_sem, recv_sem, local_sem, load_sem, save_sem = refs
    rows, width = x.shape
    inner = wh.shape[1]
    dim = width // HEADS
    pair = 2 * dim
    group = 2 * pair
    count = width // pair
    step = 256
    parts = rows // step
    loads = [(x_in, x), (cot_in, cot)]
    for number in range(count):
        for w, own in enumerate((wq_own, wk_own, wv_own)):
            loads.append((own.at[:, pl.ds(number * pair, pair)], qkv_own.at[:, pl.ds((3 * number + w) * pair, pair)]))
    loads = [pltpu.make_async_copy(a, b, load_sem.at[i]) for i, (a, b) in enumerate(loads)]
    for load in [*loads[2:], *loads[:2]]:
        load.start()
    mine[...] = jnp.zeros_like(mine)
    for row, piece in enumerate(vectors):
        mine[row, : piece.shape[0]] = piece[...].astype(F32)
    for load in loads[2:]:
        load.wait()
    spans = [(0, 1), (1, 1), *((p, 2) for p in range(2, count, 2))]
    items = [(qkv_own, wqkv, pl.ds(p * 3 * pair, n * 3 * pair)) for p, n in spans]
    items.append((wo_own, wo, pl.ds(0, width)))
    items += [(wh_own, wh, pl.ds(c, width)) for c in range(0, inner, width)]
    items += [(wp_own, wp, pl.ds(c, group)) for c in range(0, width, group)]
    vector_item = len(items)
    items.append((mine, packed, None))
    move = Gather(items, size // 8, send_sem, recv_sem, local_sem)

    def moves(text):
        for word in text.split():
            move.stage(int(word[0]), int(word[1:]))
            if word[1:] == "0":
                move.stage(int(word[0]), vector_item)

    saves = []

    def save(src, name):
        n = FRONT_SAVED.index(name)
        pltpu.make_async_copy(src, saved[name], save_sem.at[n]).start()
        saves.append((src, n))

    for number in range(vector_item):
        moves("1%d" % number)
    moves(TURNS["init"])
    unpack(packed, vec, bh, size)
    bq, bv, bo, gain1, shift1, bp, gain2, shift2 = (vec[i : i + 1, :] for i in range(8))
    loads[0].wait()
    bias = jnp.where(lax.broadcasted_iota(jnp.int32, (LIVE, 1), 0) < lengths[0], 0.0, NEG_FILL).astype(F32)
    for head in range(2):
        values[head, :, pair:] = jnp.ones((LIVE, pair), BF16)

    for first, many in spans:
        base = 3 * first * pair

        @pl.loop(0, parts)
        def _(part):
            at = pl.ds(pl.multiple_of(part * step, step), step)
            out = dot(x[at, :], wqkv[:, base : base + 3 * many * pair])
            for n in range(many):
                lane = 3 * n * pair
                real = (first + n) * pair
                to = 4 * real
                query = (out[:, lane : lane + pair] + bq[:, real : real + pair]).astype(BF16)
                query = query.astype(F32) * (1.0 / math.sqrt(dim))
                for head in range(2):
                    held = fill(own_lanes(query, head, dim), head, dim, (0.0, 0.0, 0.0, 1.0))
                    qkv[at, to + head * pair : to + (head + 1) * pair] = held.astype(BF16)
                qkv[at, to + 2 * pair : to + 3 * pair] = out[:, lane + pair : lane + 2 * pair].astype(BF16)
                qkv[at, to + 3 * pair : to + 4 * pair] = (
                    out[:, lane + 2 * pair : lane + 3 * pair] + bv[:, real : real + pair]
                ).astype(BF16)

        moves(TURNS.get("proj%d" % first, ""))
        for number in range(first, first + many):
            start = 4 * number * pair
            whole = qkv[:LIVE, start + 2 * pair : start + 3 * pair].astype(F32)
            for head in range(2):
                keys[head] = fill(own_lanes(whole, head, dim), head, dim, (1.0, 1.0, 1.0, bias)).astype(BF16)
                values[head, :, :pair] = qkv[:LIVE, start + 3 * pair : start + 4 * pair]
            to = pl.ds(number * pair, pair)

            @pl.loop(0, parts)
            def _(part):
                at = pl.ds(pl.multiple_of(part * step, step), step)
                outs = []
                for head in range(2):
                    wide = pl.ds(start + head * pair, pair)
                    here = qkv[at, wide]
                    s = dot(here, keys[head], NT)
                    peak = jnp.max(s, -1, keepdims=True)
                    o = dot(jnp.exp(s - peak).astype(BF16), values[head])
                    total = o[:, pair:]
                    outs.append(o[:, :pair] / total)
                    log_sum = parts_of(-(peak + jnp.log(total)))
                    qkv[at, wide] = fill(here.astype(F32), head, dim, log_sum).astype(BF16)
                att[at, to] = jnp.where(lanes_of(outs[0].shape, 0, dim), outs[0], outs[1]).astype(BF16)
                for spot in range(parts):
                    if text := TURNS.get("p%d.%d" % (number, spot)):

                        @pl.when(part == spot)
                        def _():
                            moves(text)

    x_t[...] = x[:LIVE, :].T
    att_t[...] = att[:LIVE, :].T
    save(qkv, "qkv")
    save(x_t, "x_t")
    save(att, "att")
    save(att_t, "att_t")
    save(wqkv, "wqkv")
    save(wo, "wo")
    moves(TURNS.get("tr", ""))

    @pl.loop(0, parts)
    def _(part):
        at = pl.ds(pl.multiple_of(part * step, step), step)
        h = x[at, :].astype(F32) + (dot(att[at, :], wo[...]) + bo)
        n, inv = norm(h)
        n1[at, :] = n
        inv1[at, :] = jnp.broadcast_to(inv, (step, 128))
        z1[at, :] = (n * gain1 + shift1).astype(BF16)

    z1_t[...] = z1[:LIVE, :].T
    save(z1_t, "z1_t")
    save(n1.at[pl.ds(0, LIVE)], "n1")
    save(inv1.at[pl.ds(0, LIVE)], "inv1")
    moves(TURNS.get("out", ""))

    @pl.loop(0, inner // step)
    def _(block):
        cols = pl.ds(pl.multiple_of(block * step, step), step)
        b = bh[:, cols]
        for start in range(0, rows, step):
            at = pl.ds(start, step)
            u = dot(z1[at, :], wh[:, cols]) + b
            phi = 0.5 * (1.0 + lax.erf(u * 0.7071067811865476))
            g[at, cols] = (u * phi).astype(BF16)
            if start < LIVE:
                slope[at, cols] = (phi + u * (jnp.exp(-0.5 * u * u) * 0.3989422804014327)).astype(BF16)
        g_t[cols, :] = g[:LIVE, cols].T

        for spot in range(inner // step):
            if text := TURNS.get("ff%d" % spot):

                @pl.when(block == spot)
                def _():
                    moves(text)

    save(g_t, "g_t")
    save(slope.at[pl.ds(0, LIVE)], "slope")
    save(wh, "wh")
    for first in range(0, width, group):
        moves(TURNS.get("fp%d" % (first // group - 1), ""))
        cols = pl.ds(first, group)

        @pl.loop(0, parts)
        def _(part):
            at = pl.ds(pl.multiple_of(part * step, step), step)
            f[at, cols] = dot(g[at, :], wp[:, cols])

    save(wp, "wp")
    loads[1].wait()
    gvec[...] = jnp.zeros_like(gvec)
    keep = 1.0 - skip[0].astype(F32)

    @pl.loop(0, parts)
    def _(part):
        at = pl.ds(pl.multiple_of(part * step, step), step)
        n, inv = norm(z1[at, :].astype(F32) + (f[at, :] + bp))
        outputs[at, :] = jnp.where(skip[0] == 1, x[at, :], (n * gain2 + shift2).astype(BF16))
        row = lax.broadcasted_iota(jnp.int32, (step, 1), 0) + part * step
        dy = jnp.where(row < lengths[0], cot[at, :].astype(F32), 0.0) * keep
        d = norm_back(dy * gain2, n, inv)
        low = d.astype(BF16)
        f[at, :] = d
        df[at, :] = low
        gvec[5:6, :] += jnp.sum(low.astype(F32), 0, keepdims=True)
        gvec[6:7, :] += jnp.sum(dy * n, 0, keepdims=True)
        gvec[7:8, :] += jnp.sum(dy, 0, keepdims=True)

    save(f.at[pl.ds(0, LIVE)], "dh2")
    save(df.at[pl.ds(0, LIVE)], "df")
    save(outputs, "outputs")
    for src, n in saves:
        pltpu.make_async_copy(src, src, save_sem.at[n]).wait()
    move.finish()


def front(size, lengths, skip, x, cot, weights, vectors):
    rows, width = x.shape
    inner = weights[4].shape[1]
    like = jax.ShapeDtypeStruct
    smem, vmem, any_ = (pl.BlockSpec(memory_space=m) for m in (pltpu.SMEM, VMEM, pl.ANY))
    saved = {
        "qkv": ((rows, 4 * width), BF16), "att": ((rows, width), BF16), "att_t": ((width, LIVE), BF16), "z1_t": ((width, LIVE), BF16),
        "x_t": ((width, LIVE), BF16), "n1": ((LIVE, width), F32), "inv1": ((LIVE, 128), F32),
        "g_t": ((inner, LIVE), BF16), "slope": ((LIVE, inner), BF16), "dh2": ((LIVE, width), F32),
        "df": ((LIVE, width), BF16), "outputs": ((rows, width), BF16), "wqkv": ((width, 3 * width), BF16),
        "wo": ((width, width), BF16), "wh": ((width, inner), BF16), "wp": ((inner, width), BF16),
    }
    pair = 2 * width // HEADS
    full = VMEM((rows, width), BF16)
    single = VMEM((rows, width), F32)
    turned = VMEM((width, LIVE), BF16)
    planes = size // 8
    items = 1 + width // (2 * pair) + 2 + inner // width + width // (2 * pair)
    out = pl.pallas_call(
        functools.partial(front_kernel, size),
        out_shape=[*[like(*saved[n]) for n in FRONT_SAVED], like((8, width), F32), like((8, width), F32)],
        in_specs=[smem, smem] + [any_] * 2 + [vmem] * 9 + [any_] * 6,
        out_specs=[any_] * len(FRONT_SAVED) + [vmem] * 2,
        scratch_shapes=[
            full, full, VMEM((rows, 4 * width), BF16), full, full, single, VMEM((rows, 128), F32),
            VMEM((rows, inner), BF16), VMEM((rows, inner), BF16), single, full, full,
            turned, turned, turned, VMEM((inner, LIVE), BF16),
            *[VMEM(saved[n][0], BF16) for n in ("wqkv", "wo", "wh", "wp")], VMEM((planes, size // planes, 16, 128), F32),
            VMEM((1, inner), F32), VMEM((2, LIVE, pair), BF16), VMEM((2, LIVE, 2 * pair), BF16),
            VMEM((16, 128), F32), VMEM((width // size, 3 * width), BF16),
            pltpu.SemaphoreType.DMA((items, 4 * planes + 3)),
            pltpu.SemaphoreType.DMA((items, 4 * planes + 3)),
            pltpu.SemaphoreType.DMA((items,)),
            pltpu.SemaphoreType.DMA((2 + 3 * (width // pair),)),
            pltpu.SemaphoreType.DMA((len(FRONT_SAVED),)),
        ],
        compiler_params=pltpu.CompilerParams(collective_id=0, has_side_effects=True, vmem_limit_bytes=67043328),
        name="front",
    )(lengths, skip, x, cot, *vectors, *weights)
    return dict(zip(FRONT_SAVED, out)), out[-2], out[-1]


class Scatter:
    def __init__(self, tensors, planes, send_sem, recv_sem, out_sem, vector):
        self.tensors = tensors
        self.planes = planes
        self.sems = send_sem, recv_sem, out_sem
        self.vector = vector
        me = lax.axis_index("fsdp")
        self.core, self.near, self.far, self.plane, self.index = place(me, planes)
        self.other = self.index(self.plane, self.far, self.near, 1 - self.core)
        self.near_peer = self.index(self.plane, 1 - self.near, self.far, self.core)
        self.far_peer = self.index(self.plane, self.near, 1 - self.far, self.core)
        self.others = [lax.rem(self.plane + step, planes) for step in range(1, planes)]
        self.plane_peers = [self.index(p, self.near, self.far, self.core) for p in self.others]
        away = ((1, 1), (0, 1), (1, 0), (0, 0))
        flip = lambda step, value: 1 - value if step else value
        self.ours = [self.index(0, flip(n, self.near), flip(f, self.far), self.core) for n, f in away]
        self.theirs = [self.index(0, flip(n, self.far), flip(f, self.near), 1 - self.core) for n, f in away]
        greet([self.other, self.near_peer, self.far_peer, *self.plane_peers])

    def push(self, src, dst, number, spot, peer):
        pltpu.make_async_remote_copy(
            src_ref=src, dst_ref=dst, send_sem=self.sems[0].at[number, spot],
            recv_sem=self.sems[1].at[number, spot], device_id=(peer,), device_id_type=MESH,
        ).start()

    def landed(self, ref, number, spot):
        pltpu.make_async_copy(ref, ref, self.sems[1].at[number, spot]).wait()

    def stage(self, which, tensor, number, start, many):
        part, got0, got1, got2, got3, final, result, rows = self.tensors[tensor]
        cols = pl.ds(start, many)
        planes = self.planes
        view = part.reshape(planes, part.shape[0] // planes, part.shape[1])

        def mine(place_, plane=slice(None)):
            return view.at[plane, pl.ds(pl.multiple_of(place_ * rows, 8), rows), cols]

        def land(ref, column):
            return ref.at[pl.ds(column * planes, planes), :, cols]

        def value(ref):
            return ref[...].astype(F32)

        if which == 0:
            for column in range(4):
                self.push(mine(self.theirs[column]), land(got0, column), number, column, self.other)
        elif which == 1:
            for column in range(2):
                self.landed(land(got0, column), number, column)
                here = mine(self.ours[column])
                here[...] = (value(here) + value(land(got0, column))).astype(BF16)
                self.push(here, land(got1, column), number, 4 + column, self.far_peer)
        elif which == 2:
            self.landed(land(got0, 2), number, 2)
            self.landed(land(got1, 0), number, 4)
            here = mine(self.ours[2])
            here[...] = (value(here) + value(land(got0, 2)) + value(land(got1, 0))).astype(BF16)
            self.push(here, land(got2, 0), number, 6, self.near_peer)
        elif which == 3:
            self.landed(land(got0, 3), number, 3)
            self.landed(land(got1, 1), number, 5)
            self.landed(land(got2, 0), number, 6)
            for step in range(planes):
                p = lax.rem(self.plane + 1 + step, planes)
                here = mine(self.ours[3], p)
                total = value(here) + value(got0.at[3 * planes + p, :, cols])
                total = total + value(got1.at[planes + p, :, cols]) + value(got2.at[p, :, cols])
                if step == planes - 1:
                    final[:, cols] = total
                else:
                    here[...] = total.astype(BF16)
                    self.push(here, got3.at[step, :, cols], number, 7 + step, self.plane_peers[step])
        else:
            for step in range(planes - 1):
                self.landed(got3.at[step, :, cols], number, 7 + step)
            total = final[:, cols]
            for step in range(planes - 1):
                total = total + value(got3.at[step, :, cols])
            final[:, cols] = total
            pltpu.make_async_copy(final.at[:, cols], result.at[:, cols], self.sems[2].at[number]).start()

    def vector_stage(self, which):
        sums, got, number, result = self.vector
        steps = [self.other, self.near_peer, self.far_peer]
        if which > 0:
            if which < 4:
                self.landed(got.at[which - 1], number, which - 1)
                sums[which] = sums[which - 1] + got[which - 1]
            else:
                total = sums[3]
                for step in range(self.planes - 1):
                    self.landed(got.at[3 + step], number, 3 + step)
                    total = total + got[3 + step]
                sums[4] = total
                pltpu.make_async_copy(sums.at[4], result, self.sems[2].at[number]).start()
        if which < 3:
            self.push(sums.at[which], got.at[which], number, which, steps[which])
        elif which == 3:
            for step, peer in enumerate(self.plane_peers):
                self.push(sums.at[3], got.at[3 + step], number, 3 + step, peer)

    def finish(self, items):
        for tensor, number, start, many in items:
            got = self.tensors[tensor][1]
            one = got.at[0, :, pl.ds(start, many)]
            column = got.at[pl.ds(0, self.planes), :, pl.ds(start, many)]
            for spot in range(6 + self.planes):
                ref = column if spot < 7 else one
                pltpu.make_async_copy(ref, ref, self.sems[0].at[number, spot]).wait()
            final = self.tensors[tensor][5].at[:, pl.ds(start, many)]
            pltpu.make_async_copy(final, final, self.sems[2].at[number]).wait()
        sums, got, number, result = self.vector
        for spot in range(3 + self.planes - 1):
            pltpu.make_async_copy(got.at[0], got.at[0], self.sems[0].at[number, spot]).wait()
        pltpu.make_async_copy(got.at[0], got.at[0], self.sems[2].at[number]).wait()


BACK_INPUTS = ("df", "g_t", "wp", "slope", "dh2", "wh", "z1_t", "wo", "n1", "inv1", "att_t", "qkv", "att", "x_t", "wqkv", "cot")


LATE_INPUTS = ("wqkv", "cot")

BACK_TURNS = {
    "wp2": "10", "a4": "11", "a9": "20", "dz0": "12", "dz3": "30", "dz4": "21", "wh2": "13", "c0": "14 22 31 40", "c3": "15",
    "0.0": "16 23 32", "0.1": "41", "0.2": "17", "1.0": "24 33", "1.2": "42", "f1": "25 34", "2.0": "43", "2.1": "18",
    "2.3": "35", "3.0": "26 44", "3.3": "27", "f3": "36 45", "4.1": "19", "4.2": "28 37", "f4": "46", "5.1": "110 38",
    "5.2": "29 47", "v": "v0", "e0": "111 210 v1", "e1": "39 48", "e2": "v2", "e3": "211 310 v3", "e4": "311 49",
    "end": "410 v4 411",
}


def back_kernel(size, lengths, skip, vec, gtop, *refs):
    refs = list(refs)

    def take(n):
        out = refs[:n]
        del refs[:n]
        return out

    count = len(BACK_INPUTS)
    source = dict(zip(BACK_INPUTS, take(count)))
    gin = take(1)[0]
    results = take(4)
    vector_result = take(1)[0]
    held = [n for n in BACK_INPUTS if n not in LATE_INPUTS]
    here = dict(zip(held, take(len(held))))
    dwqkv, dwp, keys, values, dk_acc, dv_acc = take(6)
    got = [take(4) for _ in range(4)]
    final = take(4)
    sums, sums_got = take(2)
    send_sem, recv_sem, out_sem, load_sem, gin_sem = refs
    df, g_t, wp, slope, f, wh, z1_t, wo, n1, inv1, att_t, qkv, att, x_t = (here[n] for n in held)
    width, inner = wh.shape
    dim = width // HEADS
    pair = 2 * dim
    group = 2 * pair
    wide = 256
    planes = size // 8
    pieces = inner // width

    loads = {}
    for name in held:
        dst, src = here[name], source[name]
        rows = min(src.shape[0], dst.shape[0])
        if name in ("wp", "g_t"):
            cuts = [(pl.ds(n * width, width), pl.ds(0, dst.shape[1])) for n in range(pieces)]
        elif name == "slope":
            cuts = [(pl.ds(0, rows), pl.ds(n * width, width)) for n in range(pieces)]
        else:
            cuts = [(pl.ds(0, rows), pl.ds(0, dst.shape[1]))]
        loads[name] = [
            pltpu.make_async_copy(src.at[cut], dst.at[cut], load_sem.at[BACK_INPUTS.index(name), n])
            for n, cut in enumerate(cuts)
        ]
    for name in held:
        for load in loads[name]:
            load.start()
    late = [
        pltpu.make_async_copy(
            source["wqkv"].at[:, pl.ds(n * width, width)], g_t.at[pl.ds(n * width, width), pl.ds(0, width)],
            load_sem.at[BACK_INPUTS.index("wqkv"), n],
        )
        for n in range(3)
    ]
    cot = df
    cot_load = pltpu.make_async_copy(
        source["cot"].at[pl.ds(0, LIVE)], cot, load_sem.at[BACK_INPUTS.index("cot"), 0]
    )
    grads = [dwqkv, wo, wh, dwp]
    tensors = [
        (grads[t], got[0][t], got[1][t], got[2][t], got[3][t], final[t], results[t], grads[t].shape[0] // size)
        for t in range(4)
    ]
    groups = width // group
    items = [(3, c, group) for c in range(0, width, group)] + [(2, c, width) for c in range(0, inner, width)]
    items.append((1, 0, width))
    fixed = len(items)
    singles = 2
    items += [(0, n * 3 * group, 3 * group) for n in range(groups - 1)]
    items += [(0, (2 * groups - singles + n) * 3 * pair, 3 * pair) for n in range(singles)]
    move = Scatter(tensors, planes, send_sem, recv_sem, out_sem, (sums, sums_got, len(items), vector_result))

    def begin(number):
        tensor, start, many = items[number]
        move.stage(0, tensor, number, start, many)

    def moves(text):
        for word in text.split():
            if word[0] == "v":
                move.vector_stage(int(word[1:]))
            else:
                number = int(word[1:])
                tensor, start, many = items[number]
                move.stage(int(word[0]), tensor, number, start, many)

    gain1 = vec[3:4, :]
    gvec = sums.at[0]
    gvec[...] = jnp.zeros(gvec.shape, F32)
    gvec[0:8, :] = gtop[...]
    loads["df"][0].wait()
    for number, first in enumerate(range(0, width, group)):
        cols = pl.ds(first, group)

        @pl.loop(0, pieces)
        def _(part):
            if number == 0:
                for n in range(pieces):

                    @pl.when(part == n)
                    def _():
                        loads["g_t"][n].wait()

            at = pl.ds(pl.multiple_of(part * width, width), width)
            dwp[at, cols] = dot(g_t[at, :], df[:, cols]).astype(BF16)

        begin(number)
        moves(BACK_TURNS.get("wp%d" % number, ""))
    for load in late:
        load.start()

    @pl.loop(0, inner // wide)
    def _(block):
        for n in range(pieces):

            @pl.when(block == n * (width // wide))
            def _():
                loads["wp"][n].wait()
                loads["slope"][n].wait()

        cols = pl.ds(pl.multiple_of(block * wide, wide), wide)
        total = jnp.zeros((1, wide), F32)
        half = LIVE // 2
        for start in range(0, LIVE, half):
            at = pl.ds(start, half)
            du = (dot(df[at, :], wp[cols, :], NT) * slope[at, cols].astype(F32)).astype(BF16)
            total = total + jnp.sum(du.astype(F32), 0, keepdims=True)
            slope[at, cols] = du
        for spot in range(inner // wide):
            if text := BACK_TURNS.get("a%d" % spot):

                @pl.when(block == spot)
                def _():
                    moves(text)

        row = (block * wide) // width
        for r in range(pieces):

            @pl.when(row == r)
            def _():
                gvec[8 + r : 9 + r, pl.ds(pl.multiple_of(lax.rem(block * wide, width), wide), wide)] = total

    loads["dh2"][0].wait()
    loads["wh"][0].wait()
    step = 160

    @pl.loop(0, LIVE // step)
    def _(part):
        at = pl.ds(pl.multiple_of(part * step, step), step)
        f[at, :] += dot(slope[at, :], wh[...], NT)

        for spot in range(LIVE // step):
            if text := BACK_TURNS.get("dz%d" % spot):

                @pl.when(part == spot)
                def _():
                    moves(text)

    loads["z1_t"][0].wait()
    for number in range(pieces):
        for first in range(number * width, (number + 1) * width, wide):
            cols = pl.ds(first, wide)
            wh[:, cols] = dot(z1_t[...], slope[:LIVE, cols]).astype(BF16)
        begin(groups + number)
        moves(BACK_TURNS.get("wh%d" % number, ""))
    for name in ("wo", "n1", "inv1", "att_t"):
        loads[name][0].wait()
    da = slope.at[:, pl.ds(3 * width, width)]

    @pl.loop(0, LIVE // step)
    def _(part):
        at = pl.ds(pl.multiple_of(part * step, step), step)
        dz = f[at, :]
        n = n1[at, :]
        gvec[3:4, :] += jnp.sum(dz * n, 0, keepdims=True)
        gvec[4:5, :] += jnp.sum(dz, 0, keepdims=True)
        d = norm_back(dz * gain1, n, inv1[at, :1])
        f[at, :] = d
        low = d.astype(BF16)
        df[at, :] = low
        gvec[2:3, :] += jnp.sum(low.astype(F32), 0, keepdims=True)
        da[at, :] = dot(low, wo[...], NT).astype(BF16)
        for spot in range(LIVE // step):
            if text := BACK_TURNS.get("c%d" % spot):

                @pl.when(part == spot)
                def _():
                    moves(text)

    padded = slope.shape[0]
    da[LIVE:, :] = jnp.zeros((padded - LIVE, width), BF16)
    for start in range(0, width, wide):
        cols = pl.ds(start, wide)
        wo[:, cols] = dot(att_t[...], df[:, cols]).astype(BF16)
    begin(fixed - 1)
    cot_load.start()
    moves(BACK_TURNS.get("dwo", ""))

    loads["qkv"][0].wait()
    loads["att"][0].wait()
    chunk = 256
    bias = jnp.where(lax.broadcasted_iota(jnp.int32, (LIVE, 1), 0) < lengths[0], 0.0, NEG_FILL).astype(F32)

    def block(which, start, size):
        at = pl.ds(start, size)
        base = pl.multiple_of(which * 3 * pair, pair)
        to = pl.ds(pl.multiple_of(which * pair, pair), pair)
        da_c = da[at, to].astype(F32)
        product = da_c * att[at, to].astype(F32)
        outs = []
        for head in range(2):
            q_c = qkv[at, pl.ds(pl.multiple_of((which * 4 + head) * pair, pair), pair)]
            mean = jnp.sum(own_lanes(product, head, dim), -1, keepdims=True)
            da_h = own_lanes(da_c, head, dim)
            p = jnp.exp(dot(keys[head], q_c, NT))
            dp = dot(values[head], fill(da_h, head, dim, parts_of(-mean)).astype(BF16), NT)
            ds = (p * dp).astype(BF16)
            dv_acc[...] += dot(p.astype(BF16), da_h.astype(BF16))
            dk_acc[...] += dot(ds, own_lanes(q_c, head, dim))
            outs.append(dot(ds, keys[head], TN))
        dq_c = jnp.where(lanes_of(outs[0].shape, 0, dim), outs[0], outs[1])
        slope[at, pl.ds(base, pair)] = (dq_c * (1.0 / math.sqrt(dim))).astype(BF16)

    turns = {
        (a, spot): text for a in range(width // pair) for spot in range(LIVE // chunk + 1)
        if (text := BACK_TURNS.get("%d.%d" % (a, spot)))
    }

    def tick(which, part):
        for (a, spot), text in turns.items():
            if isinstance(part, int) and part != spot:
                continue
            now = which == a if isinstance(part, int) else jnp.logical_and(which == a, part == spot)

            @pl.when(now)
            def _():
                moves(text)

    @pl.loop(0, width // pair)
    def _(which):
        base = pl.multiple_of(which * 3 * pair, pair)
        to = pl.multiple_of(which * pair, pair)
        four = pl.multiple_of(which * 4 * pair, pair)
        whole = qkv[:LIVE, pl.ds(four + 2 * pair, pair)].astype(F32)
        whole_v = qkv[:LIVE, pl.ds(four + 3 * pair, pair)].astype(F32)
        for head in range(2):
            keys[head] = fill(own_lanes(whole, head, dim), head, dim, (1.0, 1.0, 1.0, bias)).astype(BF16)
            values[head] = fill(own_lanes(whole_v, head, dim), head, dim, (1.0, 1.0, 1.0)).astype(BF16)
        dk_acc[...] = jnp.zeros_like(dk_acc)
        dv_acc[...] = jnp.zeros_like(dv_acc)

        @pl.loop(0, LIVE // chunk)
        def _(part):
            block(which, pl.multiple_of(part * chunk, chunk), chunk)
            tick(which, part)

        block(which, LIVE // chunk * chunk, padded - LIVE // chunk * chunk)
        slope[:LIVE, pl.ds(base + pair, pair)] = dk_acc[...].astype(BF16)
        low = dv_acc[...].astype(BF16)
        slope[:LIVE, pl.ds(base + 2 * pair, pair)] = low
        gvec[0:1, pl.ds(to, pair)] = jnp.sum(slope[:LIVE, pl.ds(base, pair)].astype(F32), 0, keepdims=True)
        gvec[1:2, pl.ds(to, pair)] = jnp.sum(low.astype(F32), 0, keepdims=True)
        tick(which, LIVE // chunk)

        @pl.when(which == 1)
        def _():
            loads["x_t"][0].wait()

        for number in range(fixed, len(items)):
            start, many = items[number][1:]

            @pl.when(which == (start + many) // (3 * pair) - 1)
            def _():
                @pl.loop(0, many // (3 * pair))
                def _(part):
                    cols = pl.ds(pl.multiple_of(start + part * 3 * pair, pair), 3 * pair)
                    dwqkv[:, cols] = dot(x_t[...], slope[:LIVE, cols]).astype(BF16)

                begin(number)
                moves(BACK_TURNS.get("f%d" % ((start + many) // (3 * pair) - 1), ""))

    moves(BACK_TURNS.get("v", ""))
    for load in late:
        load.wait()
    cot_load.wait()

    @pl.loop(0, LIVE // step)
    def _(part):
        at = pl.ds(pl.multiple_of(part * step, step), step)
        row = lax.broadcasted_iota(jnp.int32, (step, 1), 0) + part * step
        dropped = jnp.where(row < lengths[0], cot[at, :].astype(F32), 0.0)
        total = f[at, :]
        for n in range(3):
            total = total + dot(slope[at, n * width : (n + 1) * width], g_t[n * width : (n + 1) * width, :width], NT)
        f[at, :] = jnp.where(skip[0] == 1, dropped, total)

        for spot in range(LIVE // step):
            text = BACK_TURNS.get("e%d" % spot, "")

            @pl.when(part == spot)
            def _():
                moves(text)

    out = [pltpu.make_async_copy(f, gin.at[pl.ds(0, LIVE)], gin_sem.at[0])]
    n1[: gin.shape[0] - LIVE, :] = jnp.zeros((gin.shape[0] - LIVE, width), F32)
    out.append(pltpu.make_async_copy(n1.at[pl.ds(0, gin.shape[0] - LIVE)], gin.at[pl.ds(LIVE, gin.shape[0] - LIVE)], gin_sem.at[1]))
    for copy in out:
        copy.start()
    moves(BACK_TURNS.get("end", ""))
    for copy in out:
        copy.wait()
    move.finish([(tensor, number, start, many) for number, (tensor, start, many) in enumerate(items)])


def back(size, lengths, skip, vec, gtop, arrays):
    rows, width = arrays["cot"].shape
    inner = arrays["wh"].shape[1]
    planes = size // 8
    half = size // 2
    like = jax.ShapeDtypeStruct
    smem, vmem, any_ = (pl.BlockSpec(memory_space=m) for m in (pltpu.SMEM, VMEM, pl.ANY))
    padded = -(-LIVE // 128) * 128
    keep = {"slope": padded, "qkv": padded, "att": padded}
    held = [
        VMEM((keep.get(name, arrays[name].shape[0]), arrays[name].shape[1]), arrays[name].dtype)
        for name in BACK_INPUTS
        if name not in LATE_INPUTS
    ]
    shapes = [(width // size, 3 * width), (width // size, width), (width // size, inner), (inner // size, width)]
    lands = lambda many: [VMEM((many, r, w), BF16) for r, w in shapes]
    pair = 2 * width // HEADS
    numbers = 2 * (width // (2 * pair)) + inner // width + 1 + 1 + 1
    spots = 6 + planes
    return pl.pallas_call(
        functools.partial(back_kernel, size),
        out_shape=[like((rows, width), F32), *[like(s, F32) for s in shapes], like((16, width), F32)],
        in_specs=[smem, smem, vmem, vmem] + [any_] * len(BACK_INPUTS),
        out_specs=[any_] * 6,
        scratch_shapes=[
            *held,
            VMEM((width, 3 * width), BF16), VMEM((inner, width), BF16), VMEM((2, LIVE, pair), BF16), VMEM((2, LIVE, pair), BF16),
            VMEM((LIVE, pair), F32), VMEM((LIVE, pair), F32),
            *lands(half), *lands(half // 2), *lands(planes), *lands(planes - 1),
            *[VMEM(s, F32) for s in shapes],
            VMEM((5, 16, width), F32), VMEM((3 + planes - 1, 16, width), F32),
            pltpu.SemaphoreType.DMA((numbers, spots)), pltpu.SemaphoreType.DMA((numbers, spots)),
            pltpu.SemaphoreType.DMA((numbers,)), pltpu.SemaphoreType.DMA((len(BACK_INPUTS), inner // width)),
            pltpu.SemaphoreType.DMA((2,)),
        ],
        compiler_params=pltpu.CompilerParams(collective_id=1, has_side_effects=True, vmem_limit_bytes=67043328),
        name="back",
    )(lengths, skip, vec, gtop, *[arrays[n] for n in BACK_INPUTS])


def finish_kernel(size, sums_in, qkv_in, wo_in, wh_in, wp_in, gin_in, outputs_in, *refs):
    pieces, (gq, gk, gv, go, gh, gp, gin, outputs), (sums, sem) = refs[:9], refs[9:17], refs[17:]
    width = sums.shape[1]
    pair = 2 * width // HEADS
    moves = [(sums_in, sums), (wo_in, go), (wh_in, gh), (wp_in, gp), (gin_in, gin), (outputs_in, outputs)]
    for number in range(width // pair):
        to = pl.ds(number * pair, pair)
        for w, out in enumerate((gq, gk, gv)):
            moves.append((qkv_in.at[:, pl.ds((3 * number + w) * pair, pair)], out.at[:, to]))
    moves = [pltpu.make_async_copy(a, b, sem.at[n]) for n, (a, b) in enumerate(moves)]
    for copy in moves:
        copy.start()
    me = lax.axis_index("fsdp")
    piece = width // size

    def pick(value, first):
        lane = lax.broadcasted_iota(jnp.int32, (width, 128), 1)
        entry = lax.broadcasted_iota(jnp.int32, (width, 128), 0)
        one = jnp.where(entry == lane + first, 1.0, 0.0)
        return lax.dot_general(
            value, one, (((1,), (0,)), ((), ())), precision=lax.Precision.HIGHEST, preferred_element_type=F32
        )

    moves[0].wait()
    short = pick(sums[0:8, :], me * piece)
    for k in range(8):
        pieces[k][...] = short[k, :piece]
    long = pieces[8].shape[0]
    each = width // long
    row = lax.broadcasted_iota(jnp.int32, (8, width), 0)
    chosen = jnp.sum(jnp.where(row == me // each, sums[8:16, :], 0.0), 0, keepdims=True)
    spread = pick(jnp.broadcast_to(chosen, (8, width)), lax.rem(me, each) * long)
    pieces[8][...] = spread[0, :long]
    for copy in moves[1:]:
        copy.wait()


def finish(size, sums, matrices, gin, outputs):
    width = sums.shape[1]
    like = jax.ShapeDtypeStruct
    vmem, any_ = pl.BlockSpec(memory_space=VMEM), pl.BlockSpec(memory_space=pl.ANY)
    piece = width // size
    inner = matrices[2].shape[1]
    row = like((piece, width), F32)
    return pl.pallas_call(
        functools.partial(finish_kernel, size),
        out_shape=[
            *[like((piece,), F32)] * 8, like((inner // size,), F32),
            row, row, row, *[like(m.shape, F32) for m in matrices[1:]], like(gin.shape, F32), like(outputs.shape, BF16),
        ],
        in_specs=[any_] * 7,
        out_specs=[vmem] * 17,
        scratch_shapes=[VMEM(sums.shape, F32), pltpu.SemaphoreType.DMA((6 + 3 * HEADS // 2,))],
        compiler_params=pltpu.CompilerParams(vmem_limit_bytes=67043328),
        name="finish",
    )(sums, *matrices, gin, outputs)


def local(
    size,
    inputs,
    cotangent,
    lengths,
    skip_bit,
    w_query,
    w_key,
    w_value,
    w_out,
    b_query,
    b_value,
    b_out,
    ln1_gain,
    ln1_bias,
    w_hidden,
    b_hidden,
    w_proj,
    b_proj,
    ln2_gain,
    ln2_bias,
):
    vectors = [b_query, b_value, b_out, ln1_gain, ln1_bias, b_proj, ln2_gain, ln2_bias, b_hidden]
    weights = [w_query, w_key, w_value, w_out, w_hidden, w_proj]
    saved, vec, gtop = front(size, lengths, skip_bit, inputs, cotangent, weights, vectors)
    grad_inputs, *matrices, sums = back(size, lengths, skip_bit, vec, gtop, {**saved, "cot": cotangent})
    (
        g_b_query, g_b_value, g_b_out, g_ln1_gain, g_ln1_bias, g_b_proj, g_ln2_gain, g_ln2_bias, g_b_hidden,
        g_w_query, g_w_key, g_w_value, g_w_out, g_w_hidden, g_w_proj, grad_inputs, outputs,
    ) = finish(size, sums, matrices, grad_inputs, saved["outputs"])
    return (
        outputs,
        grad_inputs,
        g_w_query,
        g_w_key,
        g_w_value,
        g_w_out,
        g_b_query,
        g_b_value,
        g_b_out,
        g_ln1_gain,
        g_ln1_bias,
        g_w_hidden,
        g_b_hidden,
        g_w_proj,
        g_b_proj,
        g_ln2_gain,
        g_ln2_bias,
    )


def local_plain(
    inputs,
    cotangent,
    lengths,
    skip_bit,
    w_query,
    w_key,
    w_value,
    w_out,
    b_query,
    b_value,
    b_out,
    ln1_gain,
    ln1_bias,
    w_hidden,
    b_hidden,
    w_proj,
    b_proj,
    ln2_gain,
    ln2_bias,
):
    (
        query_full, key_full, value_full, out_full, hidden_full, proj_full,
        bq_full, bv_full, bo_full, gain_one, shift_one, bh_full, bp_full, gain_two, shift_two,
    ) = [
        lax.all_gather(p, "fsdp", axis=0, tiled=True)
        for p in (
            w_query, w_key, w_value, w_out, w_hidden, w_proj,
            b_query, b_value, b_out, ln1_gain, ln1_bias, b_hidden, b_proj, ln2_gain, ln2_bias,
        )
    ]
    row = lambda v: as_float(v)[None, :]
    q, k, v, att = attend(
        lengths, inputs, query_full, key_full, value_full, row(bq_full), row(bv_full)
    )
    vec = jnp.stack([as_float(v_) for v_ in (bo_full, gain_one, shift_one, bp_full, gain_two, shift_two)])
    vec = jnp.pad(vec, ((0, 2), (0, 0)))
    outputs, dh1, da, d_weight_out, d_weight_hidden, d_weight_proj, gvec, gbh = middle(
        lengths, skip_bit, inputs, att, cotangent, out_full, hidden_full, proj_full, vec, row(bh_full)
    )
    grad_inputs, d_weight_query, d_weight_key, d_weight_value, gbq, gbv = attend_back(
        lengths, inputs, dh1, q, k, v, da, query_full, key_full, value_full, cotangent, skip_bit
    )
    (
        g_w_query, g_w_key, g_w_value, g_w_out, g_w_hidden, g_w_proj,
        g_b_query, g_b_value, g_b_out, g_ln1_gain, g_ln1_bias,
        g_b_hidden, g_b_proj, g_ln2_gain, g_ln2_bias,
    ) = [
        lax.psum_scatter(lax.optimization_barrier(as_float(grad)), "fsdp", scatter_dimension=0, tiled=True)
        for grad in (
            d_weight_query, d_weight_key, d_weight_value, d_weight_out, d_weight_hidden, d_weight_proj,
            gbq[0], gbv[0], gvec[0], gvec[1], gvec[2], gbh[0], gvec[3], gvec[4], gvec[5],
        )
    ]
    return (
        outputs,
        grad_inputs,
        g_w_query,
        g_w_key,
        g_w_value,
        g_w_out,
        g_b_query,
        g_b_value,
        g_b_out,
        g_ln1_gain,
        g_ln1_bias,
        g_w_hidden,
        g_b_hidden,
        g_w_proj,
        g_b_proj,
        g_ln2_gain,
        g_ln2_bias,
    )


def solution(mesh):
    size = mesh.shape["fsdp"]
    placed = (
        P("fsdp", None),
        P("fsdp", None),
        P("fsdp"),
        P("fsdp"),
        P("fsdp", None),
        P("fsdp", None),
        P("fsdp", None),
        P("fsdp", None),
        P("fsdp"),
        P("fsdp"),
        P("fsdp"),
        P("fsdp"),
        P("fsdp"),
        P("fsdp", None),
        P("fsdp"),
        P("fsdp", None),
        P("fsdp"),
        P("fsdp"),
        P("fsdp"),
    )
    return jax.shard_map(
        functools.partial(local, size) if size == 32 else local_plain,
        mesh=mesh,
        in_specs=placed,
        out_specs=(
            P("fsdp", None),
            P("fsdp", None),
            P("fsdp", None),
            P("fsdp", None),
            P("fsdp", None),
            P("fsdp", None),
            P("fsdp"),
            P("fsdp"),
            P("fsdp"),
            P("fsdp"),
            P("fsdp"),
            P("fsdp", None),
            P("fsdp"),
            P("fsdp", None),
            P("fsdp"),
            P("fsdp"),
            P("fsdp"),
        ),
        check_vma=False,
    )
```

```python
import functools
import math

import jax
import jax.numpy as jnp
from jax import lax
from jax.experimental import pallas as pl
from jax.experimental.pallas import tpu as pltpu
from jax.sharding import PartitionSpec as P

HEADS = 12
LIVE = 800
EPSILON = 1e-05
NEG_FILL = -1e30
NT = (((1,), (1,)), ((), ()))
TN = (((0,), (0,)), ((), ()))
VMEM = pltpu.VMEM
F32, BF16 = jnp.float32, jnp.bfloat16


def dot(a, b, dims=(((1,), (0,)), ((), ()))):
    return lax.dot_general(a, b, dims, preferred_element_type=F32)


def lanes_of(shape, head, dim):
    lane = lax.broadcasted_iota(jnp.int32, shape, 1)
    return (lane < dim) if head == 0 else (lane >= dim)


def attend_kernel(lengths, x, wq, wk, wv, bq, bv, q, k, v, att, keys, values):
    rows, width = x.shape
    dim = width // HEADS
    pair = 2 * dim
    group = 2 * pair
    step = 256
    key_lane = lax.broadcasted_iota(jnp.int32, (1, LIVE), 1)
    bias = jnp.where(key_lane < lengths[0], 0.0, NEG_FILL).astype(F32)
    for head in range(2):
        values[head, :, pair:] = jnp.ones((LIVE, pair), BF16)
    for first in range(0, width, group):
        cols = pl.ds(first, group)

        @pl.loop(0, rows // step)
        def _(part):
            at = pl.ds(pl.multiple_of(part * step, step), step)
            here = x[at, :]
            q[at, cols] = ((dot(here, wq[:, cols]) + bq[:, cols]).astype(BF16).astype(F32) * (1.0 / math.sqrt(dim))).astype(BF16)
            k[at, cols] = dot(here, wk[:, cols]).astype(BF16)
            v[at, cols] = (dot(here, wv[:, cols]) + bv[:, cols]).astype(BF16)

        for start in range(first, first + group, pair):
            wide = pl.ds(start, pair)
            whole = k[:LIVE, wide]
            for head in range(2):
                keys[head] = jnp.where(lanes_of(whole.shape, head, dim), whole, jnp.zeros_like(whole))
                values[head, :, :pair] = v[:LIVE, wide]

            @pl.loop(0, rows // step)
            def _(part):
                at = pl.ds(pl.multiple_of(part * step, step), step)
                here = q[at, wide]
                outs = []
                for head in range(2):
                    s = dot(here, keys[head], NT) + bias
                    e = jnp.exp(s - jnp.max(s, -1, keepdims=True))
                    o = dot(e.astype(BF16), values[head])
                    outs.append(o[:, :pair] / o[:, pair:])
                att[at, wide] = jnp.where(lanes_of(outs[0].shape, 0, dim), outs[0], outs[1]).astype(BF16)


def attend(lengths, x, wq, wk, wv, bq, bv):
    rows, width = x.shape
    pair = 2 * width // HEADS
    return pl.pallas_call(
        attend_kernel,
        out_shape=[jax.ShapeDtypeStruct(x.shape, BF16)] * 4,
        in_specs=[pl.BlockSpec(memory_space=pltpu.SMEM)] + [pl.BlockSpec(memory_space=VMEM)] * 6,
        out_specs=[pl.BlockSpec(memory_space=VMEM)] * 4,
        scratch_shapes=[VMEM((2, LIVE, pair), BF16), VMEM((2, LIVE, 2 * pair), BF16)],
        compiler_params=pltpu.CompilerParams(vmem_limit_bytes=60 << 20),
        name="attend",
    )(lengths, x, wq, wk, wv, bq, bv)


def attend_back_kernel(lengths, x, dh1, q, k, v, da, wq, wk, wv, cot, skip, gin, gwq, gwk, gwv, gbq, gbv,
                       dq, dk, dv, keys, values, bias, dk_acc, dv_acc):
    rows, width = x.shape
    dim = width // HEADS
    pair = 2 * dim
    chunk = 256
    tops = [(c, min(chunk, -(-LIVE // 128) * 128 - c)) for c in range(0, LIVE, chunk)]
    key_row = lax.broadcasted_iota(jnp.int32, (LIVE, 128), 0)
    bias[...] = jnp.where(key_row < lengths[0], 0.0, NEG_FILL).astype(F32)
    dk[...] = jnp.zeros_like(dk)
    dv[...] = jnp.zeros_like(dv)

    def block(wide, start, size):
        at = pl.ds(start, size)
        q_c, da_c = q[at, wide], da[at, wide]
        dq_c = jnp.zeros((size, pair), F32)
        for head in range(2):
            mine = lanes_of(q_c.shape, head, dim)
            s = dot(keys[head], q_c, NT) + jnp.tile(bias[...], (1, size // 128))
            e = jnp.exp(s - jnp.max(s, 0, keepdims=True))
            p = e * (1.0 / jnp.sum(e, 0, keepdims=True))
            dp = dot(values[head], da_c, NT)
            t = p * dp
            ds = (t - p * jnp.sum(t, 0, keepdims=True)).astype(BF16)
            dv_acc[...] += dot(p.astype(BF16), jnp.where(mine, da_c, jnp.zeros_like(da_c)))
            dk_acc[...] += dot(ds, jnp.where(mine, q_c, jnp.zeros_like(q_c)))
            dq_c = dq_c + dot(ds, keys[head], TN)
        dq[at, wide] = (dq_c * (1.0 / math.sqrt(dim))).astype(BF16)

    @pl.loop(0, width // pair)
    def _(which):
        wide = pl.ds(pl.multiple_of(which * pair, pair), pair)
        whole, whole_v = k[:LIVE, wide], v[:LIVE, wide]
        for head in range(2):
            mine = lanes_of(whole.shape, head, dim)
            keys[head] = jnp.where(mine, whole, jnp.zeros_like(whole))
            values[head] = jnp.where(mine, whole_v, jnp.zeros_like(whole_v))
        dk_acc[...] = jnp.zeros_like(dk_acc)
        dv_acc[...] = jnp.zeros_like(dv_acc)

        @pl.loop(0, LIVE // chunk)
        def _(part):
            block(wide, pl.multiple_of(part * chunk, chunk), chunk)

        for start, size in tops:
            if size < chunk:
                block(wide, start, size)
        dk[:LIVE, wide] = dk_acc[...].astype(BF16)
        dv[:LIVE, wide] = dv_acc[...].astype(BF16)

    gbq[...] = jnp.sum(dq[:LIVE, :].astype(F32), 0, keepdims=True)
    gbv[...] = jnp.sum(dv[:LIVE, :].astype(F32), 0, keepdims=True)
    here = x[:LIVE, :]
    for grad, out in ((dq, gwq), (dk, gwk), (dv, gwv)):
        for start in range(0, width, 256):
            cols = pl.ds(start, 256)
            out[:, cols] = dot(here, grad[:LIVE, cols], TN).astype(BF16)
    step = 160

    @pl.loop(0, LIVE // step)
    def _(part):
        at = pl.ds(pl.multiple_of(part * step, step), step)
        total = dh1[at, :] + dot(dq[at, :], wq[...], NT)
        total = total + dot(dk[at, :], wk[...], NT)
        total = total + dot(dv[at, :], wv[...], NT)
        row = lax.broadcasted_iota(jnp.int32, (step, 1), 0) + part * step
        dropped = jnp.where(row < lengths[0], cot[at, :].astype(F32), 0.0)
        gin[at, :] = jnp.where(skip[0] == 1, dropped, total)

    gin[LIVE:, :] = jnp.zeros((rows - LIVE, width), F32)


def attend_back(lengths, x, dh1, q, k, v, da, wq, wk, wv, cot, skip):
    rows, width = x.shape
    pair = 2 * width // HEADS
    like = jax.ShapeDtypeStruct
    smem = pl.BlockSpec(memory_space=pltpu.SMEM)
    return pl.pallas_call(
        attend_back_kernel,
        out_shape=[like((rows, width), F32)] + [like((width, width), BF16)] * 3 + [like((1, width), F32)] * 2,
        in_specs=[smem] + [pl.BlockSpec(memory_space=VMEM)] * 10 + [smem],
        out_specs=[pl.BlockSpec(memory_space=VMEM)] * 6,
        scratch_shapes=[VMEM(x.shape, BF16)] * 3
        + [VMEM((2, LIVE, pair), BF16)] * 2
        + [VMEM((LIVE, 128), F32)]
        + [VMEM((LIVE, pair), F32)] * 2,
        compiler_params=pltpu.CompilerParams(vmem_limit_bytes=62 << 20),
        name="attend_back",
    )(lengths, x, dh1, q, k, v, da, wq, wk, wv, cot, skip)


def middle_kernel(lengths, skip, x_in, att_in, cot_in, wo_in, wh_in, wp_in, vec, bh,
                  outputs, dh1, da, gwo, gwh, gwp, gvec, gbh,
                  x, att, cot, wo, wh, wp, z1, n1, inv1, f, g, slope, df, z1t, out_h, out_p, load_sem, out_sem):
    rows, width = x.shape
    inner = wh.shape[1]
    loads = [
        pltpu.make_async_copy(a, b, load_sem.at[i])
        for i, (a, b) in enumerate(
            ((x_in, x), (att_in, att), (wo_in, wo), (wh_in, wh), (wp_in, wp), (cot_in, cot))
        )
    ]
    for load in loads:
        load.start()
    bo, gain1, shift1, bp, gain2, shift2 = (vec[i : i + 1, :] for i in range(6))
    for load in loads[:3]:
        load.wait()
    step = 256

    def norm(h):
        centred = h - jnp.mean(h, -1, keepdims=True)
        inv = lax.rsqrt(jnp.mean(centred * centred, -1, keepdims=True) + EPSILON)
        return centred * inv, inv

    def norm_back(e, n, inv):
        return inv * (e - jnp.mean(e, -1, keepdims=True) - n * jnp.mean(e * n, -1, keepdims=True))

    @pl.loop(0, rows // step)
    def _(part):
        at = pl.ds(pl.multiple_of(part * step, step), step)
        h = x[at, :].astype(F32) + (dot(att[at, :], wo[...]) + bo)
        n, inv = norm(h)
        n1[at, :] = n
        inv1[at, :] = jnp.broadcast_to(inv, (step, 128))
        z1[at, :] = (n * gain1 + shift1).astype(BF16)

    loads[3].wait()
    loads[4].wait()
    f[...] = jnp.zeros_like(f)
    wide = 256

    @pl.loop(0, inner // wide)
    def _(block):
        cols = pl.ds(pl.multiple_of(block * wide, wide), wide)
        b = bh[:, cols]
        for start in range(0, rows, step):
            at = pl.ds(start, step)
            u = dot(z1[at, :], wh[:, cols]) + b
            phi = 0.5 * (1.0 + lax.erf(u * 0.7071067811865476))
            g[at, cols] = (u * phi).astype(BF16)
            slope[at, cols] = (phi + u * (jnp.exp(-0.5 * u * u) * 0.3989422804014327)).astype(BF16)
            f[at, :] += dot(g[at, cols], wp[cols, :])

    loads[5].wait()
    gvec[...] = jnp.zeros_like(gvec)
    keep = 1.0 - skip[0].astype(F32)

    @pl.loop(0, rows // step)
    def _(part):
        at = pl.ds(pl.multiple_of(part * step, step), step)
        n, inv = norm(z1[at, :].astype(F32) + (f[at, :] + bp))
        outputs[at, :] = jnp.where(skip[0] == 1, x[at, :], (n * gain2 + shift2).astype(BF16))
        row = lax.broadcasted_iota(jnp.int32, (step, 1), 0) + part * step
        dy = jnp.where(row < lengths[0], cot[at, :].astype(F32), 0.0) * keep
        d = norm_back(dy * gain2, n, inv)
        low = d.astype(BF16)
        f[at, :] = d
        df[at, :] = low
        gvec[3:4, :] += jnp.sum(low.astype(F32), 0, keepdims=True)
        gvec[4:5, :] += jnp.sum(dy * n, 0, keepdims=True)
        gvec[5:6, :] += jnp.sum(dy, 0, keepdims=True)

    z1t[...] = z1[:LIVE, :].T

    def flush(block, buf, slot):
        cols = pl.ds(pl.multiple_of(block * wide, wide), wide)
        if buf is out_h:
            return pltpu.make_async_copy(buf.at[slot], gwh.at[:, cols], out_sem.at[0, slot])
        return pltpu.make_async_copy(buf.at[slot], gwp.at[cols, :], out_sem.at[1, slot])

    @pl.loop(0, inner // wide)
    def _(block):
        slot = lax.rem(block, 2)
        cols = pl.ds(pl.multiple_of(block * wide, wide), wide)

        @pl.when(block >= 2)
        def _():
            flush(block, out_h, slot).wait()
            flush(block, out_p, slot).wait()

        out_p[slot] = dot(g[:LIVE, cols], df[:LIVE, :], TN).astype(BF16)
        flush(block, out_p, slot).start()
        total = jnp.zeros((1, wide), F32)
        half = LIVE // 2
        for start in range(0, LIVE, half):
            at = pl.ds(start, half)
            du = (dot(df[at, :], wp[cols, :], NT) * slope[at, cols].astype(F32)).astype(BF16)
            total = total + jnp.sum(du.astype(F32), 0, keepdims=True)
            g[at, cols] = du
            f[at, :] += dot(du, wh[:, cols], NT)
        gbh[:, cols] = total
        out_h[slot] = dot(z1t[...], g[:LIVE, cols]).astype(BF16)
        flush(block, out_h, slot).start()

    half = LIVE // 5
    @pl.loop(0, LIVE // half)
    def _(part):
        at = pl.ds(pl.multiple_of(part * half, half), half)
        dz = f[at, :]
        n = n1[at, :]
        gvec[1:2, :] += jnp.sum(dz * n, 0, keepdims=True)
        gvec[2:3, :] += jnp.sum(dz, 0, keepdims=True)
        d = norm_back(dz * gain1, n, inv1[at, :1])
        dh1[at, :] = d
        low = d.astype(BF16)
        df[at, :] = low
        gvec[0:1, :] += jnp.sum(low.astype(F32), 0, keepdims=True)
        da[at, :] = dot(low, wo[...], NT).astype(BF16)

    da[LIVE:, :] = jnp.zeros((rows - LIVE, width), BF16)
    for start in range(0, width, wide):
        cols = pl.ds(start, wide)
        gwo[cols, :] = dot(att[:LIVE, cols], df[:LIVE, :], TN).astype(BF16)
    for block in (inner // wide - 2, inner // wide - 1):
        flush(block, out_h, block % 2).wait()
        flush(block, out_p, block % 2).wait()


def middle(lengths, skip, x, att, cot, wo, wh, wp, vec, bh):
    rows, width = x.shape
    inner = wh.shape[1]
    like = jax.ShapeDtypeStruct
    smem, vmem, any_ = (pl.BlockSpec(memory_space=m) for m in (pltpu.SMEM, VMEM, pl.ANY))
    pad = -(-LIVE // 128) * 128
    return pl.pallas_call(
        middle_kernel,
        out_shape=[
            like((rows, width), BF16), like((LIVE, width), F32), like((rows, width), BF16),
            like((width, width), BF16), like((width, inner), BF16), like((inner, width), BF16),
            like((8, width), F32), like((1, inner), F32),
        ],
        in_specs=[smem] * 2 + [any_] * 6 + [vmem] * 2,
        out_specs=[vmem] * 4 + [any_] * 2 + [vmem] * 2,
        scratch_shapes=[
            VMEM((rows, width), BF16), VMEM((rows, width), BF16), VMEM((rows, width), BF16),
            VMEM((width, width), BF16), VMEM((width, inner), BF16), VMEM((inner, width), BF16),
            VMEM((rows, width), BF16), VMEM((rows, width), F32), VMEM((rows, 128), F32),
            VMEM((rows, width), F32), VMEM((rows, inner), BF16), VMEM((rows, inner), BF16),
            VMEM((rows, width), BF16), VMEM((width, LIVE), BF16),
            VMEM((2, width, 256), BF16), VMEM((2, 256, width), BF16),
            pltpu.SemaphoreType.DMA((6,)), pltpu.SemaphoreType.DMA((2, 2)),
        ],
        compiler_params=pltpu.CompilerParams(vmem_limit_bytes=63 << 20),
        name="middle",
    )(lengths, skip, x, att, cot, wo, wh, wp, vec, bh)


def as_float(value):
    return value.astype(jnp.float32)


MESH = pl.DeviceIdType.MESH


def place(me, planes):
    core = lax.rem(me, 2)
    chip = me // 2
    col = lax.rem(chip, 2)
    row = lax.rem(chip // 2, 2)
    plane = chip // 4
    near = jnp.where(core == 0, row, col)
    far = jnp.where(core == 0, col, row)

    def index(plane_, near_, far_, core_):
        row_ = jnp.where(core_ == 0, near_, far_)
        col_ = jnp.where(core_ == 0, far_, near_)
        return ((plane_ * 2 + row_) * 2 + col_) * 2 + core_

    return core, near, far, plane, index


def greet(peers):
    barrier = pltpu.get_barrier_semaphore()
    for peer in peers:
        pl.semaphore_signal(barrier, inc=1, device_id=(peer,), device_id_type=MESH)
    pl.semaphore_wait(barrier, len(peers))


class Gather:
    def __init__(self, items, planes, send_sem, recv_sem, local_sem):
        self.items = items
        self.planes = planes
        self.sems = send_sem, recv_sem, local_sem
        me = lax.axis_index("fsdp")
        self.core, self.near, self.far, self.plane, self.index = place(me, planes)
        self.other = self.index(self.plane, self.far, self.near, 1 - self.core)
        self.near_peer = self.index(self.plane, 1 - self.near, self.far, self.core)
        self.far_peer = self.index(self.plane, self.near, 1 - self.far, self.core)
        self.plane_peers = [
            self.index(lax.rem(self.plane + step, planes), self.near, self.far, self.core) for step in range(1, planes)
        ]
        self.spots = [
            self.index(0, n, f, self.core) for n, f in (
                (self.near, self.far), (1 - self.near, self.far), (self.near, 1 - self.far), (1 - self.near, 1 - self.far)
            )
        ]
        greet([self.other, self.near_peer, self.far_peer, *self.plane_peers])

    def column(self, number, spot, plane=slice(None)):
        own, full, cols = self.items[number]
        if cols is None:
            return full.at[plane, spot]
        rows = own.shape[0]
        view = full.reshape(self.planes, full.shape[0] // self.planes, full.shape[1])
        return view.at[plane, pl.ds(pl.multiple_of(spot * rows, 8), rows), cols]

    def push(self, number, src, dst, spot, peer):
        pltpu.make_async_remote_copy(
            src_ref=src, dst_ref=dst, send_sem=self.sems[0].at[number, spot], recv_sem=self.sems[1].at[number, spot],
            device_id=(peer,), device_id_type=MESH,
        ).start()

    def landed(self, number, spot, whole=False):
        where = self.column(number, self.spots[0], slice(None) if whole else 0)
        pltpu.make_async_copy(where, where, self.sems[1].at[number, spot]).wait()

    def stage(self, which, number):
        planes = self.planes
        near0, far0, other0, wide0 = (planes - 1 + n * planes for n in range(4))
        mine, near, far, both = self.spots
        own, full, cols = self.items[number]
        src = own if cols is None else own.at[:, cols]
        sides = ((near0, self.near_peer), (far0, self.far_peer), (other0, self.other))
        if which == 1:
            here = self.column(number, mine, self.plane)
            for step, peer in enumerate(self.plane_peers):
                self.push(number, src, here, step, peer)
            pltpu.make_async_copy(src, here, self.sems[2].at[number]).start()
        elif which == 6:
            for base, peer in sides:
                self.push(number, src, self.column(number, mine, self.plane), base, peer)
        elif which == 2:
            for step in range(1, planes):
                self.landed(number, step - 1)
                here = self.column(number, mine, lax.rem(self.plane + planes - step, planes))
                for base, peer in sides:
                    self.push(number, here, here, base + step, peer)
        elif which == 3:
            for step in range(planes):
                self.landed(number, near0 + step)
            where = self.column(number, near)
            self.push(number, where, where, wide0, self.far_peer)
            self.push(number, where, where, wide0 + 1, self.other)
        elif which == 4:
            for step in range(planes):
                self.landed(number, far0 + step)
            where = self.column(number, far)
            self.push(number, where, where, wide0 + 2, self.other)
            self.landed(number, wide0, True)
            where = self.column(number, both)
            self.push(number, where, where, wide0 + 3, self.other)
        else:
            for step in range(planes):
                self.landed(number, other0 + step)
            for spot in range(1, 4):
                self.landed(number, wide0 + spot, True)
            here = self.column(number, mine, 0)
            pltpu.make_async_copy(here, here, self.sems[2].at[number]).wait()

    def finish(self):
        for number in range(len(self.items)):
            for spot in range(4 * self.planes + 3):
                where = self.column(number, self.spots[0], 0 if spot < 4 * self.planes - 1 else slice(None))
                pltpu.make_async_copy(where, where, self.sems[0].at[number, spot]).wait()


def unpack(packed, vec, bh, size):
    width, inner = vec.shape[1], bh.shape[1]
    piece, long = width // size, inner // size

    def spread(part, start):
        lane = lax.rem(lax.broadcasted_iota(jnp.int32, (128, width), 1) + start, part)
        entry = lax.broadcasted_iota(jnp.int32, (128, width), 0)
        column = lax.broadcasted_iota(jnp.int32, (size, width), 1) + start
        owner = lax.broadcasted_iota(jnp.int32, (size, width), 0)
        return jnp.where(entry == lane, 1.0, 0.0).astype(BF16), column - lax.rem(column, part) == part * owner

    def pick(row, chosen, owned):
        flat = packed[:, :, row, :].reshape(size, 128).astype(BF16)
        return jnp.sum(jnp.where(owned, dot(flat, chosen), 0.0), 0, keepdims=True)

    short = spread(piece, 0)
    for k in range(8):
        vec[k : k + 1, :] = pick(k, *short)

    @pl.loop(0, inner // width)
    def _(n):
        start = pl.multiple_of(n * width, width)
        bh[:, pl.ds(start, width)] = pick(8, *spread(long, start))


def parts_of(value):
    high = value.astype(BF16).astype(F32)
    rest = value - high
    middle = rest.astype(BF16).astype(F32)
    return high, middle, rest - middle


def fill(base, head, dim, values):
    lane = lax.broadcasted_iota(jnp.int32, base.shape, 1) - (dim if head == 0 else 0)
    for n, value in enumerate(values):
        base = jnp.where(lane == n, value, base)
    return base


def own_lanes(value, head, dim):
    return jnp.where(lanes_of(value.shape, head, dim), value, jnp.zeros_like(value))


def norm(h):
    centred = h - jnp.mean(h, -1, keepdims=True)
    inv = lax.rsqrt(jnp.mean(centred * centred, -1, keepdims=True) + EPSILON)
    return centred * inv, inv


def norm_back(e, n, inv):
    return inv * (e - jnp.mean(e, -1, keepdims=True) - n * jnp.mean(e * n, -1, keepdims=True))


FRONT_SAVED = ("qkv", "att", "att_t", "z1_t", "x_t", "n1", "inv1", "g_t", "slope", "dh2", "df", "outputs", "wqkv", "wo", "wh", "wp")


TURNS = {
    "init": "60 61 62 63 64 65 66 67 68 69 610 611 20 21 22 30 31 23 32 40 33 41 50",
    "proj0": "24", "p0.0": "51", "p0.3": "42 34 25", "p1.1": "52 43", "p1.3": "35 26", "proj2": "53", "p2.0": "44",
    "p2.2": "36 27", "p2.3": "54", "p3.0": "45", "p3.2": "37 28", "p3.3": "55", "p4.0": "46 29", "p4.1": "38",
    "p4.3": "56", "p5.0": "210", "p5.1": "47 39", "p5.3": "211", "tr": "57", "out": "310", "ff0": "311", "ff1": "48",
    "ff4": "58", "ff6": "49", "ff9": "59", "ff11": "410", "fp0": "411 510", "fp1": "511",
}


def front_kernel(size, lengths, skip, x_in, cot_in, *refs):
    refs = list(refs)

    def take(n):
        out = refs[:n]
        del refs[:n]
        return out

    vectors = take(9)
    wq_own, wk_own, wv_own, wo_own, wh_own, wp_own = take(6)
    saved = dict(zip(FRONT_SAVED, take(len(FRONT_SAVED))))
    vec, gvec = take(2)
    (x, cot, qkv, att, z1, n1, inv1, g, slope, f, outputs, df, x_t, att_t, z1_t, g_t) = take(16)
    wqkv, wo, wh, wp, packed = take(5)
    bh, keys, values, mine, qkv_own, send_sem, recv_sem, local_sem, load_sem, save_sem = refs
    rows, width = x.shape
    inner = wh.shape[1]
    dim = width // HEADS
    pair = 2 * dim
    group = 2 * pair
    count = width // pair
    step = 256
    parts = rows // step
    loads = [(x_in, x), (cot_in, cot)]
    for number in range(count):
        for w, own in enumerate((wq_own, wk_own, wv_own)):
            loads.append((own.at[:, pl.ds(number * pair, pair)], qkv_own.at[:, pl.ds((3 * number + w) * pair, pair)]))
    loads = [pltpu.make_async_copy(a, b, load_sem.at[i]) for i, (a, b) in enumerate(loads)]
    for load in [*loads[2:], *loads[:2]]:
        load.start()
    mine[...] = jnp.zeros_like(mine)
    for row, piece in enumerate(vectors):
        mine[row, : piece.shape[0]] = piece[...].astype(F32)
    for load in loads[2:]:
        load.wait()
    spans = [(0, 1), (1, 1), *((p, 2) for p in range(2, count, 2))]
    items = [(qkv_own, wqkv, pl.ds(p * 3 * pair, n * 3 * pair)) for p, n in spans]
    items.append((wo_own, wo, pl.ds(0, width)))
    items += [(wh_own, wh, pl.ds(c, width)) for c in range(0, inner, width)]
    items += [(wp_own, wp, pl.ds(c, group)) for c in range(0, width, group)]
    vector_item = len(items)
    items.append((mine, packed, None))
    move = Gather(items, size // 8, send_sem, recv_sem, local_sem)

    def moves(text):
        for word in text.split():
            move.stage(int(word[0]), int(word[1:]))
            if word[1:] == "0":
                move.stage(int(word[0]), vector_item)

    saves = []

    def save(src, name):
        n = FRONT_SAVED.index(name)
        pltpu.make_async_copy(src, saved[name], save_sem.at[n]).start()
        saves.append((src, n))

    for number in range(vector_item):
        moves("1%d" % number)
    moves(TURNS["init"])
    unpack(packed, vec, bh, size)
    bq, bv, bo, gain1, shift1, bp, gain2, shift2 = (vec[i : i + 1, :] for i in range(8))
    loads[0].wait()
    bias = jnp.where(lax.broadcasted_iota(jnp.int32, (LIVE, 1), 0) < lengths[0], 0.0, NEG_FILL).astype(F32)
    for head in range(2):
        values[head, :, pair:] = jnp.ones((LIVE, pair), BF16)

    for first, many in spans:
        base = 3 * first * pair

        @pl.loop(0, parts)
        def _(part):
            at = pl.ds(pl.multiple_of(part * step, step), step)
            out = dot(x[at, :], wqkv[:, base : base + 3 * many * pair])
            for n in range(many):
                lane = 3 * n * pair
                real = (first + n) * pair
                to = 4 * real
                query = (out[:, lane : lane + pair] + bq[:, real : real + pair]).astype(BF16)
                query = query.astype(F32) * (1.0 / math.sqrt(dim))
                for head in range(2):
                    held = fill(own_lanes(query, head, dim), head, dim, (0.0, 0.0, 0.0, 1.0))
                    qkv[at, to + head * pair : to + (head + 1) * pair] = held.astype(BF16)
                qkv[at, to + 2 * pair : to + 3 * pair] = out[:, lane + pair : lane + 2 * pair].astype(BF16)
                qkv[at, to + 3 * pair : to + 4 * pair] = (
                    out[:, lane + 2 * pair : lane + 3 * pair] + bv[:, real : real + pair]
                ).astype(BF16)

        moves(TURNS.get("proj%d" % first, ""))
        for number in range(first, first + many):
            start = 4 * number * pair
            whole = qkv[:LIVE, start + 2 * pair : start + 3 * pair].astype(F32)
            for head in range(2):
                keys[head] = fill(own_lanes(whole, head, dim), head, dim, (1.0, 1.0, 1.0, bias)).astype(BF16)
                values[head, :, :pair] = qkv[:LIVE, start + 3 * pair : start + 4 * pair]
            to = pl.ds(number * pair, pair)

            @pl.loop(0, parts)
            def _(part):
                at = pl.ds(pl.multiple_of(part * step, step), step)
                outs = []
                for head in range(2):
                    wide = pl.ds(start + head * pair, pair)
                    here = qkv[at, wide]
                    s = dot(here, keys[head], NT)
                    peak = jnp.max(s, -1, keepdims=True)
                    o = dot(jnp.exp(s - peak).astype(BF16), values[head])
                    total = o[:, pair:]
                    outs.append(o[:, :pair] / total)
                    log_sum = parts_of(-(peak + jnp.log(total)))
                    qkv[at, wide] = fill(here.astype(F32), head, dim, log_sum).astype(BF16)
                att[at, to] = jnp.where(lanes_of(outs[0].shape, 0, dim), outs[0], outs[1]).astype(BF16)
                for spot in range(parts):
                    if text := TURNS.get("p%d.%d" % (number, spot)):

                        @pl.when(part == spot)
                        def _():
                            moves(text)

    x_t[...] = x[:LIVE, :].T
    att_t[...] = att[:LIVE, :].T
    save(qkv, "qkv")
    save(x_t, "x_t")
    save(att, "att")
    save(att_t, "att_t")
    save(wqkv, "wqkv")
    save(wo, "wo")
    moves(TURNS.get("tr", ""))

    @pl.loop(0, parts)
    def _(part):
        at = pl.ds(pl.multiple_of(part * step, step), step)
        h = x[at, :].astype(F32) + (dot(att[at, :], wo[...]) + bo)
        n, inv = norm(h)
        n1[at, :] = n
        inv1[at, :] = jnp.broadcast_to(inv, (step, 128))
        z1[at, :] = (n * gain1 + shift1).astype(BF16)

    z1_t[...] = z1[:LIVE, :].T
    save(z1_t, "z1_t")
    save(n1.at[pl.ds(0, LIVE)], "n1")
    save(inv1.at[pl.ds(0, LIVE)], "inv1")
    moves(TURNS.get("out", ""))

    @pl.loop(0, inner // step)
    def _(block):
        cols = pl.ds(pl.multiple_of(block * step, step), step)
        b = bh[:, cols]
        for start in range(0, rows, step):
            at = pl.ds(start, step)
            u = dot(z1[at, :], wh[:, cols]) + b
            phi = 0.5 * (1.0 + lax.erf(u * 0.7071067811865476))
            g[at, cols] = (u * phi).astype(BF16)
            if start < LIVE:
                slope[at, cols] = (phi + u * (jnp.exp(-0.5 * u * u) * 0.3989422804014327)).astype(BF16)
        g_t[cols, :] = g[:LIVE, cols].T

        for spot in range(inner // step):
            if text := TURNS.get("ff%d" % spot):

                @pl.when(block == spot)
                def _():
                    moves(text)

    save(g_t, "g_t")
    save(slope.at[pl.ds(0, LIVE)], "slope")
    save(wh, "wh")
    for first in range(0, width, group):
        moves(TURNS.get("fp%d" % (first // group - 1), ""))
        cols = pl.ds(first, group)

        @pl.loop(0, parts)
        def _(part):
            at = pl.ds(pl.multiple_of(part * step, step), step)
            f[at, cols] = dot(g[at, :], wp[:, cols])

    save(wp, "wp")
    loads[1].wait()
    gvec[...] = jnp.zeros_like(gvec)
    keep = 1.0 - skip[0].astype(F32)

    @pl.loop(0, parts)
    def _(part):
        at = pl.ds(pl.multiple_of(part * step, step), step)
        n, inv = norm(z1[at, :].astype(F32) + (f[at, :] + bp))
        outputs[at, :] = jnp.where(skip[0] == 1, x[at, :], (n * gain2 + shift2).astype(BF16))
        row = lax.broadcasted_iota(jnp.int32, (step, 1), 0) + part * step
        dy = jnp.where(row < lengths[0], cot[at, :].astype(F32), 0.0) * keep
        d = norm_back(dy * gain2, n, inv)
        low = d.astype(BF16)
        f[at, :] = d
        df[at, :] = low
        gvec[5:6, :] += jnp.sum(low.astype(F32), 0, keepdims=True)
        gvec[6:7, :] += jnp.sum(dy * n, 0, keepdims=True)
        gvec[7:8, :] += jnp.sum(dy, 0, keepdims=True)

    save(f.at[pl.ds(0, LIVE)], "dh2")
    save(df.at[pl.ds(0, LIVE)], "df")
    save(outputs, "outputs")
    for src, n in saves:
        pltpu.make_async_copy(src, src, save_sem.at[n]).wait()
    move.finish()


def front(size, lengths, skip, x, cot, weights, vectors):
    rows, width = x.shape
    inner = weights[4].shape[1]
    like = jax.ShapeDtypeStruct
    smem, vmem, any_ = (pl.BlockSpec(memory_space=m) for m in (pltpu.SMEM, VMEM, pl.ANY))
    saved = {
        "qkv": ((rows, 4 * width), BF16), "att": ((rows, width), BF16), "att_t": ((width, LIVE), BF16), "z1_t": ((width, LIVE), BF16),
        "x_t": ((width, LIVE), BF16), "n1": ((LIVE, width), F32), "inv1": ((LIVE, 128), F32),
        "g_t": ((inner, LIVE), BF16), "slope": ((LIVE, inner), BF16), "dh2": ((LIVE, width), F32),
        "df": ((LIVE, width), BF16), "outputs": ((rows, width), BF16), "wqkv": ((width, 3 * width), BF16),
        "wo": ((width, width), BF16), "wh": ((width, inner), BF16), "wp": ((inner, width), BF16),
    }
    pair = 2 * width // HEADS
    full = VMEM((rows, width), BF16)
    single = VMEM((rows, width), F32)
    turned = VMEM((width, LIVE), BF16)
    planes = size // 8
    items = 1 + width // (2 * pair) + 2 + inner // width + width // (2 * pair)
    out = pl.pallas_call(
        functools.partial(front_kernel, size),
        out_shape=[*[like(*saved[n]) for n in FRONT_SAVED], like((8, width), F32), like((8, width), F32)],
        in_specs=[smem, smem] + [any_] * 2 + [vmem] * 9 + [any_] * 6,
        out_specs=[any_] * len(FRONT_SAVED) + [vmem] * 2,
        scratch_shapes=[
            full, full, VMEM((rows, 4 * width), BF16), full, full, single, VMEM((rows, 128), F32),
            VMEM((rows, inner), BF16), VMEM((rows, inner), BF16), single, full, full,
            turned, turned, turned, VMEM((inner, LIVE), BF16),
            *[VMEM(saved[n][0], BF16) for n in ("wqkv", "wo", "wh", "wp")], VMEM((planes, size // planes, 16, 128), F32),
            VMEM((1, inner), F32), VMEM((2, LIVE, pair), BF16), VMEM((2, LIVE, 2 * pair), BF16),
            VMEM((16, 128), F32), VMEM((width // size, 3 * width), BF16),
            pltpu.SemaphoreType.DMA((items, 4 * planes + 3)),
            pltpu.SemaphoreType.DMA((items, 4 * planes + 3)),
            pltpu.SemaphoreType.DMA((items,)),
            pltpu.SemaphoreType.DMA((2 + 3 * (width // pair),)),
            pltpu.SemaphoreType.DMA((len(FRONT_SAVED),)),
        ],
        compiler_params=pltpu.CompilerParams(collective_id=0, has_side_effects=True, vmem_limit_bytes=67043328),
        name="front",
    )(lengths, skip, x, cot, *vectors, *weights)
    return dict(zip(FRONT_SAVED, out)), out[-2], out[-1]


class Scatter:
    def __init__(self, tensors, planes, send_sem, recv_sem, out_sem, vector):
        self.tensors = tensors
        self.planes = planes
        self.sems = send_sem, recv_sem, out_sem
        self.vector = vector
        me = lax.axis_index("fsdp")
        self.core, self.near, self.far, self.plane, self.index = place(me, planes)
        self.other = self.index(self.plane, self.far, self.near, 1 - self.core)
        self.near_peer = self.index(self.plane, 1 - self.near, self.far, self.core)
        self.far_peer = self.index(self.plane, self.near, 1 - self.far, self.core)
        self.others = [lax.rem(self.plane + step, planes) for step in range(1, planes)]
        self.plane_peers = [self.index(p, self.near, self.far, self.core) for p in self.others]
        away = ((1, 1), (0, 1), (1, 0), (0, 0))
        flip = lambda step, value: 1 - value if step else value
        self.ours = [self.index(0, flip(n, self.near), flip(f, self.far), self.core) for n, f in away]
        self.theirs = [self.index(0, flip(n, self.far), flip(f, self.near), 1 - self.core) for n, f in away]
        greet([self.other, self.near_peer, self.far_peer, *self.plane_peers])

    def push(self, src, dst, number, spot, peer):
        pltpu.make_async_remote_copy(
            src_ref=src, dst_ref=dst, send_sem=self.sems[0].at[number, spot],
            recv_sem=self.sems[1].at[number, spot], device_id=(peer,), device_id_type=MESH,
        ).start()

    def landed(self, ref, number, spot):
        pltpu.make_async_copy(ref, ref, self.sems[1].at[number, spot]).wait()

    def stage(self, which, tensor, number, start, many):
        part, got0, got1, got2, got3, final, result, rows = self.tensors[tensor]
        cols = pl.ds(start, many)
        planes = self.planes
        view = part.reshape(planes, part.shape[0] // planes, part.shape[1])

        def mine(place_, plane=slice(None)):
            return view.at[plane, pl.ds(pl.multiple_of(place_ * rows, 8), rows), cols]

        def land(ref, column):
            return ref.at[pl.ds(column * planes, planes), :, cols]

        def value(ref):
            return ref[...].astype(F32)

        if which == 0:
            for column in range(4):
                self.push(mine(self.theirs[column]), land(got0, column), number, column, self.other)
        elif which == 1:
            for column in range(2):
                self.landed(land(got0, column), number, column)
                here = mine(self.ours[column])
                here[...] = (value(here) + value(land(got0, column))).astype(BF16)
                self.push(here, land(got1, column), number, 4 + column, self.far_peer)
        elif which == 2:
            self.landed(land(got0, 2), number, 2)
            self.landed(land(got1, 0), number, 4)
            here = mine(self.ours[2])
            here[...] = (value(here) + value(land(got0, 2)) + value(land(got1, 0))).astype(BF16)
            self.push(here, land(got2, 0), number, 6, self.near_peer)
        elif which == 3:
            self.landed(land(got0, 3), number, 3)
            self.landed(land(got1, 1), number, 5)
            self.landed(land(got2, 0), number, 6)
            for step in range(planes):
                p = lax.rem(self.plane + 1 + step, planes)
                here = mine(self.ours[3], p)
                total = value(here) + value(got0.at[3 * planes + p, :, cols])
                total = total + value(got1.at[planes + p, :, cols]) + value(got2.at[p, :, cols])
                if step == planes - 1:
                    final[:, cols] = total
                else:
                    here[...] = total.astype(BF16)
                    self.push(here, got3.at[step, :, cols], number, 7 + step, self.plane_peers[step])
        else:
            for step in range(planes - 1):
                self.landed(got3.at[step, :, cols], number, 7 + step)
            total = final[:, cols]
            for step in range(planes - 1):
                total = total + value(got3.at[step, :, cols])
            final[:, cols] = total
            pltpu.make_async_copy(final.at[:, cols], result.at[:, cols], self.sems[2].at[number]).start()

    def vector_stage(self, which):
        sums, got, number, result = self.vector
        steps = [self.other, self.near_peer, self.far_peer]
        if which > 0:
            if which < 4:
                self.landed(got.at[which - 1], number, which - 1)
                sums[which] = sums[which - 1] + got[which - 1]
            else:
                total = sums[3]
                for step in range(self.planes - 1):
                    self.landed(got.at[3 + step], number, 3 + step)
                    total = total + got[3 + step]
                sums[4] = total
                pltpu.make_async_copy(sums.at[4], result, self.sems[2].at[number]).start()
        if which < 3:
            self.push(sums.at[which], got.at[which], number, which, steps[which])
        elif which == 3:
            for step, peer in enumerate(self.plane_peers):
                self.push(sums.at[3], got.at[3 + step], number, 3 + step, peer)

    def finish(self, items):
        for tensor, number, start, many in items:
            got = self.tensors[tensor][1]
            one = got.at[0, :, pl.ds(start, many)]
            column = got.at[pl.ds(0, self.planes), :, pl.ds(start, many)]
            for spot in range(6 + self.planes):
                ref = column if spot < 7 else one
                pltpu.make_async_copy(ref, ref, self.sems[0].at[number, spot]).wait()
            final = self.tensors[tensor][5].at[:, pl.ds(start, many)]
            pltpu.make_async_copy(final, final, self.sems[2].at[number]).wait()
        sums, got, number, result = self.vector
        for spot in range(3 + self.planes - 1):
            pltpu.make_async_copy(got.at[0], got.at[0], self.sems[0].at[number, spot]).wait()
        pltpu.make_async_copy(got.at[0], got.at[0], self.sems[2].at[number]).wait()


BACK_INPUTS = ("df", "g_t", "wp", "slope", "dh2", "wh", "z1_t", "wo", "n1", "inv1", "att_t", "qkv", "att", "x_t", "wqkv", "cot")


LATE_INPUTS = ("wqkv", "cot", "x_t")

BACK_TURNS = {
    "wp2": "10", "a5": "11", "a8": "20", "dz1": "12", "dz3": "30 21", "wh2": "13", "wh3": "31", "c1": "40 22 14", "c3": "15",
    "dwo": "16", "0.1": "41 32 23 17", "1.0": "24", "1.1": "33", "1.3": "42", "f1": "34 25", "2.0": "43", "2.1": "18",
    "2.3": "35 44 26", "3.2": "27", "3.3": "36", "f3": "45", "4.0": "37", "4.1": "28 19", "4.2": "46", "5.0": "47 38 29 110",
    "5.3": "210", "v": "v0", "f5": "39", "e0": "v1 48", "e1": "310 111 v2", "e3": "211 49 v3 311", "end": "410 v4 411",
}


def back_kernel(size, lengths, skip, vec, gtop, *refs):
    refs = list(refs)

    def take(n):
        out = refs[:n]
        del refs[:n]
        return out

    count = len(BACK_INPUTS)
    source = dict(zip(BACK_INPUTS, take(count)))
    gin = take(1)[0]
    results = take(4)
    vector_result = take(1)[0]
    held = [n for n in BACK_INPUTS if n not in LATE_INPUTS]
    here = dict(zip(held, take(len(held))))
    dwqkv, dwp, keys, values, dk_acc, dv_acc = take(6)
    got = [take(4) for _ in range(4)]
    final = take(4)
    sums, sums_got = take(2)
    send_sem, recv_sem, out_sem, load_sem, gin_sem = refs
    df, g_t, wp, slope, f, wh, z1_t, wo, n1, inv1, att_t, qkv, att = (here[n] for n in held)
    width, inner = wh.shape
    dim = width // HEADS
    pair = 2 * dim
    group = 2 * pair
    wide = 256
    planes = size // 8
    pieces = inner // width

    loads = {}
    for name in held:
        dst, src = here[name], source[name]
        rows = min(src.shape[0], dst.shape[0])
        if name in ("wp", "g_t"):
            cuts = [(pl.ds(n * width, width), pl.ds(0, dst.shape[1])) for n in range(pieces)]
        elif name == "slope":
            cuts = [(pl.ds(0, rows), pl.ds(n * width, width)) for n in range(pieces)]
        else:
            cuts = [(pl.ds(0, rows), pl.ds(0, dst.shape[1]))]
        loads[name] = [
            pltpu.make_async_copy(src.at[cut], dst.at[cut], load_sem.at[BACK_INPUTS.index(name), n])
            for n, cut in enumerate(cuts)
        ]
    for name in held:
        for load in loads[name]:
            load.start()
    late = [
        pltpu.make_async_copy(
            source["wqkv"].at[:, pl.ds(n * width, width)], g_t.at[pl.ds(n * width, width), pl.ds(0, width)],
            load_sem.at[BACK_INPUTS.index("wqkv"), n],
        )
        for n in range(3)
    ]
    cot, x_t = df, z1_t
    x_load = pltpu.make_async_copy(source["x_t"], x_t, load_sem.at[BACK_INPUTS.index("x_t"), 0])
    cot_load = pltpu.make_async_copy(
        source["cot"].at[pl.ds(0, LIVE)], cot, load_sem.at[BACK_INPUTS.index("cot"), 0]
    )
    grads = [dwqkv, wo, wh, dwp]
    tensors = [
        (grads[t], got[0][t], got[1][t], got[2][t], got[3][t], final[t], results[t], grads[t].shape[0] // size)
        for t in range(4)
    ]
    groups = width // group
    items = [(3, c, group) for c in range(0, width, group)] + [(2, c, width) for c in range(0, inner, width)]
    items.append((1, 0, width))
    fixed = len(items)
    singles = 2
    items += [(0, n * 3 * group, 3 * group) for n in range(groups - 1)]
    items += [(0, (2 * groups - singles + n) * 3 * pair, 3 * pair) for n in range(singles)]
    move = Scatter(tensors, planes, send_sem, recv_sem, out_sem, (sums, sums_got, len(items), vector_result))

    def begin(number):
        tensor, start, many = items[number]
        move.stage(0, tensor, number, start, many)

    def moves(text):
        for word in text.split():
            if word[0] == "v":
                move.vector_stage(int(word[1:]))
            else:
                number = int(word[1:])
                tensor, start, many = items[number]
                move.stage(int(word[0]), tensor, number, start, many)

    gain1, few = vec[3:4, :], 200
    gvec = sums.at[0]
    gvec[...] = jnp.zeros(gvec.shape, F32)
    gvec[0:8, :] = gtop[...]
    loads["df"][0].wait()
    for number, first in enumerate(range(0, width, group)):
        cols = pl.ds(first, group)

        @pl.loop(0, pieces)
        def _(part):
            if number == 0:
                for n in range(pieces):

                    @pl.when(part == n)
                    def _():
                        loads["g_t"][n].wait()

            at = pl.ds(pl.multiple_of(part * width, width), width)
            dwp[at, cols] = dot(g_t[at, :], df[:, cols]).astype(BF16)

        begin(number)
        moves(BACK_TURNS.get("wp%d" % number, ""))
    for load in late:
        load.start()

    @pl.loop(0, inner // wide)
    def _(block):
        for n in range(pieces):

            @pl.when(block == n * (width // wide))
            def _():
                loads["wp"][n].wait()
                loads["slope"][n].wait()

        cols = pl.ds(pl.multiple_of(block * wide, wide), wide)
        total = jnp.zeros((1, wide), F32)
        half = LIVE // 2
        for start in range(0, LIVE, half):
            at = pl.ds(start, half)
            du = (dot(df[at, :], wp[cols, :], NT) * slope[at, cols].astype(F32)).astype(BF16)
            total = total + jnp.sum(du.astype(F32), 0, keepdims=True)
            slope[at, cols] = du
        for spot in range(inner // wide):
            if text := BACK_TURNS.get("a%d" % spot):

                @pl.when(block == spot)
                def _():
                    moves(text)

        row = (block * wide) // width
        for r in range(pieces):

            @pl.when(row == r)
            def _():
                gvec[8 + r : 9 + r, pl.ds(pl.multiple_of(lax.rem(block * wide, width), wide), wide)] = total

    loads["dh2"][0].wait()
    loads["wh"][0].wait()
    @pl.loop(0, LIVE // few)
    def _(part):
        at = pl.ds(pl.multiple_of(part * few, few), few)
        f[at, :] += dot(slope[at, :], wh[...], NT)

        for spot in range(LIVE // few):
            if text := BACK_TURNS.get("dz%d" % spot):

                @pl.when(part == spot)
                def _():
                    moves(text)

    loads["z1_t"][0].wait()
    for number in range(pieces):
        for first in range(number * width, (number + 1) * width, wide):
            cols = pl.ds(first, wide)
            wh[:, cols] = dot(z1_t[...], slope[:LIVE, cols]).astype(BF16)
        begin(groups + number)
        if number == pieces - 1:
            x_load.start()
        moves(BACK_TURNS.get("wh%d" % number, ""))
    for name in ("wo", "n1", "inv1", "att_t"):
        loads[name][0].wait()
    da = slope.at[:, pl.ds(3 * width, width)]

    few = 200

    @pl.loop(0, LIVE // few)
    def _(part):
        at = pl.ds(pl.multiple_of(part * few, few), few)
        dz = f[at, :]
        n = n1[at, :]
        gvec[3:4, :] += jnp.sum(dz * n, 0, keepdims=True)
        gvec[4:5, :] += jnp.sum(dz, 0, keepdims=True)
        d = norm_back(dz * gain1, n, inv1[at, :1])
        f[at, :] = d
        low = d.astype(BF16)
        df[at, :] = low
        gvec[2:3, :] += jnp.sum(low.astype(F32), 0, keepdims=True)
        da[at, :] = dot(low, wo[...], NT).astype(BF16)
        for spot in range(LIVE // few):
            if text := BACK_TURNS.get("c%d" % spot):

                @pl.when(part == spot)
                def _():
                    moves(text)

    padded = slope.shape[0]
    da[LIVE:, :] = jnp.zeros((padded - LIVE, width), BF16)
    for start in range(0, width, wide):
        cols = pl.ds(start, wide)
        wo[:, cols] = dot(att_t[...], df[:, cols]).astype(BF16)
    begin(fixed - 1)
    cot_load.start()
    moves(BACK_TURNS.get("dwo", ""))

    loads["qkv"][0].wait()
    loads["att"][0].wait()
    chunk = 256
    bias = jnp.where(lax.broadcasted_iota(jnp.int32, (LIVE, 1), 0) < lengths[0], 0.0, NEG_FILL).astype(F32)

    def block(which, start, size):
        at = pl.ds(start, size)
        base = pl.multiple_of(which * 3 * pair, pair)
        to = pl.ds(pl.multiple_of(which * pair, pair), pair)
        da_c = da[at, to].astype(F32)
        product = da_c * att[at, to].astype(F32)
        outs = []
        for head in range(2):
            q_c = qkv[at, pl.ds(pl.multiple_of((which * 4 + head) * pair, pair), pair)]
            mean = jnp.sum(own_lanes(product, head, dim), -1, keepdims=True)
            da_h = own_lanes(da_c, head, dim)
            p = jnp.exp(dot(keys[head], q_c, NT))
            dp = dot(values[head], fill(da_h, head, dim, parts_of(-mean)).astype(BF16), NT)
            ds = (p * dp).astype(BF16)
            dv_acc[...] += dot(p.astype(BF16), da_h.astype(BF16))
            dk_acc[...] += dot(ds, own_lanes(q_c, head, dim))
            outs.append(dot(ds, keys[head], TN))
        dq_c = jnp.where(lanes_of(outs[0].shape, 0, dim), outs[0], outs[1])
        slope[at, pl.ds(base, pair)] = (dq_c * (1.0 / math.sqrt(dim))).astype(BF16)

    turns = {
        (a, spot): text for a in range(width // pair) for spot in range(LIVE // chunk + 1)
        if (text := BACK_TURNS.get("%d.%d" % (a, spot)))
    }

    def tick(which, part):
        for (a, spot), text in turns.items():
            if isinstance(part, int) and part != spot:
                continue
            now = which == a if isinstance(part, int) else jnp.logical_and(which == a, part == spot)

            @pl.when(now)
            def _():
                moves(text)

    @pl.loop(0, width // pair)
    def _(which):
        base = pl.multiple_of(which * 3 * pair, pair)
        to = pl.multiple_of(which * pair, pair)
        four = pl.multiple_of(which * 4 * pair, pair)
        whole = qkv[:LIVE, pl.ds(four + 2 * pair, pair)].astype(F32)
        whole_v = qkv[:LIVE, pl.ds(four + 3 * pair, pair)].astype(F32)
        for head in range(2):
            keys[head] = fill(own_lanes(whole, head, dim), head, dim, (1.0, 1.0, 1.0, bias)).astype(BF16)
            values[head] = fill(own_lanes(whole_v, head, dim), head, dim, (1.0, 1.0, 1.0)).astype(BF16)
        dk_acc[...] = jnp.zeros_like(dk_acc)
        dv_acc[...] = jnp.zeros_like(dv_acc)

        @pl.loop(0, LIVE // chunk)
        def _(part):
            block(which, pl.multiple_of(part * chunk, chunk), chunk)
            tick(which, part)

        block(which, LIVE // chunk * chunk, padded - LIVE // chunk * chunk)
        slope[:LIVE, pl.ds(base + pair, pair)] = dk_acc[...].astype(BF16)
        low = dv_acc[...].astype(BF16)
        slope[:LIVE, pl.ds(base + 2 * pair, pair)] = low
        gvec[0:1, pl.ds(to, pair)] = jnp.sum(slope[:LIVE, pl.ds(base, pair)].astype(F32), 0, keepdims=True)
        gvec[1:2, pl.ds(to, pair)] = jnp.sum(low.astype(F32), 0, keepdims=True)
        tick(which, LIVE // chunk)

        @pl.when(which == 1)
        def _():
            x_load.wait()

        for number in range(fixed, len(items)):
            start, many = items[number][1:]

            @pl.when(which == (start + many) // (3 * pair) - 1)
            def _():
                @pl.loop(0, many // (3 * pair))
                def _(part):
                    cols = pl.ds(pl.multiple_of(start + part * 3 * pair, pair), 3 * pair)
                    dwqkv[:, cols] = dot(x_t[...], slope[:LIVE, cols]).astype(BF16)

                begin(number)
                moves(BACK_TURNS.get("f%d" % ((start + many) // (3 * pair) - 1), ""))

    moves(BACK_TURNS.get("v", ""))
    for load in late:
        load.wait()
    cot_load.wait()

    @pl.loop(0, LIVE // few)
    def _(part):
        at = pl.ds(pl.multiple_of(part * few, few), few)
        row = lax.broadcasted_iota(jnp.int32, (few, 1), 0) + part * few
        dropped = jnp.where(row < lengths[0], cot[at, :].astype(F32), 0.0)
        total = f[at, :]
        for n in range(3):
            total = total + dot(slope[at, n * width : (n + 1) * width], g_t[n * width : (n + 1) * width, :width], NT)
        f[at, :] = jnp.where(skip[0] == 1, dropped, total)

        for spot in range(LIVE // few):
            text = BACK_TURNS.get("e%d" % spot, "")

            @pl.when(part == spot)
            def _():
                moves(text)

    out = [pltpu.make_async_copy(f, gin.at[pl.ds(0, LIVE)], gin_sem.at[0])]
    n1[: gin.shape[0] - LIVE, :] = jnp.zeros((gin.shape[0] - LIVE, width), F32)
    out.append(pltpu.make_async_copy(n1.at[pl.ds(0, gin.shape[0] - LIVE)], gin.at[pl.ds(LIVE, gin.shape[0] - LIVE)], gin_sem.at[1]))
    for copy in out:
        copy.start()
    moves(BACK_TURNS.get("end", ""))
    for copy in out:
        copy.wait()
    move.finish([(tensor, number, start, many) for number, (tensor, start, many) in enumerate(items)])


def back(size, lengths, skip, vec, gtop, arrays):
    rows, width = arrays["cot"].shape
    inner = arrays["wh"].shape[1]
    planes = size // 8
    half = size // 2
    like = jax.ShapeDtypeStruct
    smem, vmem, any_ = (pl.BlockSpec(memory_space=m) for m in (pltpu.SMEM, VMEM, pl.ANY))
    padded = -(-LIVE // 128) * 128
    keep = {"slope": padded, "qkv": padded, "att": padded}
    held = [
        VMEM((keep.get(name, arrays[name].shape[0]), arrays[name].shape[1]), arrays[name].dtype)
        for name in BACK_INPUTS
        if name not in LATE_INPUTS
    ]
    shapes = [(width // size, 3 * width), (width // size, width), (width // size, inner), (inner // size, width)]
    lands = lambda many: [VMEM((many, r, w), BF16) for r, w in shapes]
    pair = 2 * width // HEADS
    numbers = 2 * (width // (2 * pair)) + inner // width + 1 + 1 + 1
    spots = 6 + planes
    return pl.pallas_call(
        functools.partial(back_kernel, size),
        out_shape=[like((rows, width), F32), *[like(s, F32) for s in shapes], like((16, width), F32)],
        in_specs=[smem, smem, vmem, vmem] + [any_] * len(BACK_INPUTS),
        out_specs=[any_] * 6,
        scratch_shapes=[
            *held,
            VMEM((width, 3 * width), BF16), VMEM((inner, width), BF16), VMEM((2, LIVE, pair), BF16), VMEM((2, LIVE, pair), BF16),
            VMEM((LIVE, pair), F32), VMEM((LIVE, pair), F32),
            *lands(half), *lands(half // 2), *lands(planes), *lands(planes - 1),
            *[VMEM(s, F32) for s in shapes],
            VMEM((5, 16, width), F32), VMEM((3 + planes - 1, 16, width), F32),
            pltpu.SemaphoreType.DMA((numbers, spots)), pltpu.SemaphoreType.DMA((numbers, spots)),
            pltpu.SemaphoreType.DMA((numbers,)), pltpu.SemaphoreType.DMA((len(BACK_INPUTS), inner // width)),
            pltpu.SemaphoreType.DMA((2,)),
        ],
        compiler_params=pltpu.CompilerParams(collective_id=1, has_side_effects=True, vmem_limit_bytes=67043328),
        name="back",
    )(lengths, skip, vec, gtop, *[arrays[n] for n in BACK_INPUTS])


def finish_kernel(size, sums_in, qkv_in, wo_in, wh_in, wp_in, gin_in, outputs_in, *refs):
    pieces, (gq, gk, gv, go, gh, gp, gin, outputs), (sums, sem) = refs[:9], refs[9:17], refs[17:]
    width = sums.shape[1]
    pair = 2 * width // HEADS
    moves = [(sums_in, sums), (wo_in, go), (wh_in, gh), (wp_in, gp), (gin_in, gin), (outputs_in, outputs)]
    for number in range(width // pair):
        to = pl.ds(number * pair, pair)
        for w, out in enumerate((gq, gk, gv)):
            moves.append((qkv_in.at[:, pl.ds((3 * number + w) * pair, pair)], out.at[:, to]))
    moves = [pltpu.make_async_copy(a, b, sem.at[n]) for n, (a, b) in enumerate(moves)]
    for copy in moves:
        copy.start()
    me = lax.axis_index("fsdp")
    piece = width // size

    def pick(value, first):
        lane = lax.broadcasted_iota(jnp.int32, (width, 128), 1)
        entry = lax.broadcasted_iota(jnp.int32, (width, 128), 0)
        one = jnp.where(entry == lane + first, 1.0, 0.0)
        return lax.dot_general(
            value, one, (((1,), (0,)), ((), ())), precision=lax.Precision.HIGHEST, preferred_element_type=F32
        )

    moves[0].wait()
    short = pick(sums[0:8, :], me * piece)
    for k in range(8):
        pieces[k][...] = short[k, :piece]
    long = pieces[8].shape[0]
    each = width // long
    row = lax.broadcasted_iota(jnp.int32, (8, width), 0)
    chosen = jnp.sum(jnp.where(row == me // each, sums[8:16, :], 0.0), 0, keepdims=True)
    spread = pick(jnp.broadcast_to(chosen, (8, width)), lax.rem(me, each) * long)
    pieces[8][...] = spread[0, :long]
    for copy in moves[1:]:
        copy.wait()


def finish(size, sums, matrices, gin, outputs):
    width = sums.shape[1]
    like = jax.ShapeDtypeStruct
    vmem, any_ = pl.BlockSpec(memory_space=VMEM), pl.BlockSpec(memory_space=pl.ANY)
    piece = width // size
    inner = matrices[2].shape[1]
    row = like((piece, width), F32)
    return pl.pallas_call(
        functools.partial(finish_kernel, size),
        out_shape=[
            *[like((piece,), F32)] * 8, like((inner // size,), F32),
            row, row, row, *[like(m.shape, F32) for m in matrices[1:]], like(gin.shape, F32), like(outputs.shape, BF16),
        ],
        in_specs=[any_] * 7,
        out_specs=[vmem] * 17,
        scratch_shapes=[VMEM(sums.shape, F32), pltpu.SemaphoreType.DMA((6 + 3 * HEADS // 2,))],
        compiler_params=pltpu.CompilerParams(vmem_limit_bytes=67043328),
        name="finish",
    )(sums, *matrices, gin, outputs)


def local(
    size,
    inputs,
    cotangent,
    lengths,
    skip_bit,
    w_query,
    w_key,
    w_value,
    w_out,
    b_query,
    b_value,
    b_out,
    ln1_gain,
    ln1_bias,
    w_hidden,
    b_hidden,
    w_proj,
    b_proj,
    ln2_gain,
    ln2_bias,
):
    vectors = [b_query, b_value, b_out, ln1_gain, ln1_bias, b_proj, ln2_gain, ln2_bias, b_hidden]
    weights = [w_query, w_key, w_value, w_out, w_hidden, w_proj]
    saved, vec, gtop = front(size, lengths, skip_bit, inputs, cotangent, weights, vectors)
    grad_inputs, *matrices, sums = back(size, lengths, skip_bit, vec, gtop, {**saved, "cot": cotangent})
    (
        g_b_query, g_b_value, g_b_out, g_ln1_gain, g_ln1_bias, g_b_proj, g_ln2_gain, g_ln2_bias, g_b_hidden,
        g_w_query, g_w_key, g_w_value, g_w_out, g_w_hidden, g_w_proj, grad_inputs, outputs,
    ) = finish(size, sums, matrices, grad_inputs, saved["outputs"])
    return (
        outputs,
        grad_inputs,
        g_w_query,
        g_w_key,
        g_w_value,
        g_w_out,
        g_b_query,
        g_b_value,
        g_b_out,
        g_ln1_gain,
        g_ln1_bias,
        g_w_hidden,
        g_b_hidden,
        g_w_proj,
        g_b_proj,
        g_ln2_gain,
        g_ln2_bias,
    )


def local_plain(
    inputs,
    cotangent,
    lengths,
    skip_bit,
    w_query,
    w_key,
    w_value,
    w_out,
    b_query,
    b_value,
    b_out,
    ln1_gain,
    ln1_bias,
    w_hidden,
    b_hidden,
    w_proj,
    b_proj,
    ln2_gain,
    ln2_bias,
):
    (
        query_full, key_full, value_full, out_full, hidden_full, proj_full,
        bq_full, bv_full, bo_full, gain_one, shift_one, bh_full, bp_full, gain_two, shift_two,
    ) = [
        lax.all_gather(p, "fsdp", axis=0, tiled=True)
        for p in (
            w_query, w_key, w_value, w_out, w_hidden, w_proj,
            b_query, b_value, b_out, ln1_gain, ln1_bias, b_hidden, b_proj, ln2_gain, ln2_bias,
        )
    ]
    row = lambda v: as_float(v)[None, :]
    q, k, v, att = attend(
        lengths, inputs, query_full, key_full, value_full, row(bq_full), row(bv_full)
    )
    vec = jnp.stack([as_float(v_) for v_ in (bo_full, gain_one, shift_one, bp_full, gain_two, shift_two)])
    vec = jnp.pad(vec, ((0, 2), (0, 0)))
    outputs, dh1, da, d_weight_out, d_weight_hidden, d_weight_proj, gvec, gbh = middle(
        lengths, skip_bit, inputs, att, cotangent, out_full, hidden_full, proj_full, vec, row(bh_full)
    )
    grad_inputs, d_weight_query, d_weight_key, d_weight_value, gbq, gbv = attend_back(
        lengths, inputs, dh1, q, k, v, da, query_full, key_full, value_full, cotangent, skip_bit
    )
    (
        g_w_query, g_w_key, g_w_value, g_w_out, g_w_hidden, g_w_proj,
        g_b_query, g_b_value, g_b_out, g_ln1_gain, g_ln1_bias,
        g_b_hidden, g_b_proj, g_ln2_gain, g_ln2_bias,
    ) = [
        lax.psum_scatter(lax.optimization_barrier(as_float(grad)), "fsdp", scatter_dimension=0, tiled=True)
        for grad in (
            d_weight_query, d_weight_key, d_weight_value, d_weight_out, d_weight_hidden, d_weight_proj,
            gbq[0], gbv[0], gvec[0], gvec[1], gvec[2], gbh[0], gvec[3], gvec[4], gvec[5],
        )
    ]
    return (
        outputs,
        grad_inputs,
        g_w_query,
        g_w_key,
        g_w_value,
        g_w_out,
        g_b_query,
        g_b_value,
        g_b_out,
        g_ln1_gain,
        g_ln1_bias,
        g_w_hidden,
        g_b_hidden,
        g_w_proj,
        g_b_proj,
        g_ln2_gain,
        g_ln2_bias,
    )


def solution(mesh):
    size = mesh.shape["fsdp"]
    placed = (
        P("fsdp", None),
        P("fsdp", None),
        P("fsdp"),
        P("fsdp"),
        P("fsdp", None),
        P("fsdp", None),
        P("fsdp", None),
        P("fsdp", None),
        P("fsdp"),
        P("fsdp"),
        P("fsdp"),
        P("fsdp"),
        P("fsdp"),
        P("fsdp", None),
        P("fsdp"),
        P("fsdp", None),
        P("fsdp"),
        P("fsdp"),
        P("fsdp"),
    )
    return jax.shard_map(
        functools.partial(local, size) if size == 32 else local_plain,
        mesh=mesh,
        in_specs=placed,
        out_specs=(
            P("fsdp", None),
            P("fsdp", None),
            P("fsdp", None),
            P("fsdp", None),
            P("fsdp", None),
            P("fsdp", None),
            P("fsdp"),
            P("fsdp"),
            P("fsdp"),
            P("fsdp"),
            P("fsdp"),
            P("fsdp", None),
            P("fsdp"),
            P("fsdp", None),
            P("fsdp"),
            P("fsdp"),
            P("fsdp"),
        ),
        check_vma=False,
    )
```
